32 devices in a mesh: space: 4 (over y, core), chan: 8 (over z, x).
Axes of the slice: x: 2, y: 2, z: 4, core: 2. Of those that a mesh axis runs over, the one named last changes fastest.
Arguments:
- volume: bfloat16 [4, 32, 32, 64, 128], P(None, 'space', 'chan'), may hold values from -6 to 6
- w_first: bfloat16 [3, 3, 3, 128, 256], P(None, None, None, None, 'chan'), may hold values from -0.109375 to 0.109375
- w_second: bfloat16 [3, 3, 3, 256, 256], P(None, None, None, None, 'chan'), may hold values from -0.078125 to 0.078125
- cotangent: bfloat16 [4, 8, 8, 16, 256], P(None, 'space', None, None, 'chan'), may hold values from -6 to 6
Outputs:
- second_out: bfloat16 [4, 8, 8, 16, 256], P(None, 'space', None, None, 'chan')
- volume_grad: bfloat16 [4, 32, 32, 64, 128], P(None, 'space', 'chan')
- first_grad: float32 [3, 3, 3, 128, 256], P(None, None, None, None, 'chan')
- second_grad: float32 [3, 3, 3, 256, 256], P(None, None, None, None, 'chan')
The draws below stay inside these ranges and needn't reach their ends.
All inputs are finite; a program needn't handle non-finite values.
Results may differ from the reference program's by a relative error of at most 0.018.
Values may be sent and summed in bfloat16 or wider, within the bound.
No kernel may reach another device: no remote copies, remote signals or barrier semaphores. Data moves between devices by JAX's collectives and lax.ppermute only.
A program may use at most 64 MiB of HBM per device.

```python
import jax
import jax.numpy as jnp

VOLS = 4
DEPTH = 64
C_IN = 128
C_MID = 256
C_OUT = 256
SIDE_X = 32
SIDE_Y = 32


def levels(own_key, shape, pieces, least, largest):
    def one(dim, blocks):
        heights = jax.random.uniform(jax.random.fold_in(jax.random.fold_in(own_key, 6), dim), (blocks,), jnp.float32, least / len(pieces), largest / len(pieces))
        return jnp.repeat(jnp.exp(heights), shape[dim] // blocks).reshape((-1,) + (1,) * (len(shape) - dim - 1))

    loudness = one(*pieces[0])
    for cut in pieces[1:]:
        loudness = loudness * one(*cut)
    return loudness


def gaussian(key, shape, deviation, reach, shards=(), kind=jnp.bfloat16):
    level = levels(key, shape, shards, -0.22, 0.18) if shards else 1.0
    values = jax.random.normal(key, shape, jnp.float32) * deviation * level
    return jnp.minimum(jnp.maximum(values, -reach), reach).astype(kind)


def setup_inputs(seed: int = 0) -> dict:
    streams_of = jax.random.split(jax.random.key(seed), 5)
    volume = gaussian(streams_of[0], (VOLS, SIDE_X, SIDE_Y, DEPTH, C_IN), 1.0, 6.0, ((1, 4), (2, 8)))
    w_first = gaussian(streams_of[1], (3, 3, 3, C_IN, C_MID), (27 * C_IN) ** -0.5, 0.109375, ((4, 8),))
    w_second = gaussian(streams_of[2], (3, 3, 3, C_MID, C_OUT), (27 * C_MID) ** -0.5, 0.078125, ((4, 8),))
    cotangent = gaussian(streams_of[3], (VOLS, SIDE_X // 4, SIDE_Y // 4, DEPTH // 4, C_OUT), 1.0, 6.0, ((1, 4), (4, 8)))
    return dict(volume=volume, w_first=w_first, w_second=w_second, cotangent=cotangent)


def pad_low(field):
    return jnp.pad(field, ((0, 0), (1, 0), (1, 0), (1, 0), (0, 0)))

def tap_slice(padded, i, j, k, out_a, out_b, out_c):
    return padded[:, i:i + 2 * out_a:2, j:j + 2 * out_b:2, k:k + 2 * out_c:2, :]

def conv_forward(padded, filters):
    out_a = (padded.shape[1] - 1) // 2
    out_b = (padded.shape[2] - 1) // 2
    out_c = (padded.shape[3] - 1) // 2
    total = jnp.zeros((padded.shape[0], out_a, out_b, out_c, filters.shape[4]), jnp.float32)
    for i in range(3):
        for j in range(3):
            for k in range(3):
                piece = tap_slice(padded, i, j, k, out_a, out_b, out_c)
                total = total + jnp.dot(piece, filters[i, j, k], preferred_element_type=jnp.float32)
    return total

def filter_grad(padded, grad_cells):
    out_a, out_b, out_c = (grad_cells.shape[1], grad_cells.shape[2], grad_cells.shape[3])
    flat_grad = grad_cells.reshape(-1, grad_cells.shape[4])
    rows_all = []
    for i in range(3):
        rows_j = []
        for j in range(3):
            rows_k = []
            for k in range(3):
                piece = tap_slice(padded, i, j, k, out_a, out_b, out_c).reshape(-1, padded.shape[4])
                rows_k.append(jnp.dot(piece.T, flat_grad, preferred_element_type=jnp.float32))
            rows_j.append(jnp.stack(rows_k))
        rows_all.append(jnp.stack(rows_j))
    return jnp.stack(rows_all)

def input_grad_trim(grad_cells, filters):
    count, out_a, out_b, out_c = (grad_cells.shape[0], grad_cells.shape[1], grad_cells.shape[2], grad_cells.shape[3])
    grad_high = jnp.pad(grad_cells, ((0, 0), (0, 1), (0, 1), (0, 1), (0, 0)))
    parity_taps = [[(1, 0)], [(0, 1), (2, 0)]]
    result = jnp.zeros((count, 2 * out_a, 2 * out_b, 2 * out_c, filters.shape[3]), jnp.float32)
    for s_one in range(2):
        for s_two in range(2):
            for s_three in range(2):
                total = jnp.zeros((count, out_a, out_b, out_c, filters.shape[3]), jnp.float32)
                for i, d_one in parity_taps[s_one]:
                    for j, d_two in parity_taps[s_two]:
                        for k, d_three in parity_taps[s_three]:
                            piece = grad_high[:, d_one:d_one + out_a, d_two:d_two + out_b, d_three:d_three + out_c, :]
                            total = total + jnp.dot(piece, filters[i, j, k].T, preferred_element_type=jnp.float32)
                result = result.at[:, s_one::2, s_two::2, s_three::2, :].set(total)
    return result

def reference(volume, w_first, w_second, cotangent):
    vol_pad = pad_low(volume)
    pre_first = conv_forward(vol_pad, w_first)
    hidden_act = jnp.where(pre_first > 0, pre_first, 0.3 * pre_first).astype(jnp.bfloat16)
    act_pad = pad_low(hidden_act)
    second_out = conv_forward(act_pad, w_second).astype(jnp.bfloat16)
    second_grad = filter_grad(act_pad, cotangent)
    act_back = input_grad_trim(cotangent, w_second)
    pre_back = (act_back * jnp.where(pre_first > 0, 1.0, 0.3)).astype(jnp.bfloat16)
    first_grad = filter_grad(vol_pad, pre_back)
    volume_grad = input_grad_trim(pre_back, w_first).astype(jnp.bfloat16)
    return (second_out, volume_grad, first_grad, second_grad)
```

```python
import jax
import jax.numpy as jnp
from jax import lax
from jax.sharding import PartitionSpec as P

BF16 = jnp.bfloat16
F32 = jnp.float32


def shifted(value, axis, steps):
    count = lax.axis_size(axis)
    first, last = (max(0, -steps), min(count, count - steps))
    return lax.ppermute(value, axis, [(source, source + steps) for source in range(first, last)])


def swapped(value, axis, bit):
    count = lax.axis_size(axis)
    return lax.ppermute(value, axis, [(i, i ^ (1 << bit)) for i in range(count)])


def bit_of(axis, bit):
    return (lax.axis_index(axis) >> bit) & 1


def doubled(value, axis, bit, dim):
    other = swapped(value, axis, bit)
    high = bit_of(axis, bit) == 1
    return jnp.stack([jnp.where(high, other, value), jnp.where(high, value, other)], axis=dim)


def halved(value, axis, bit, dim):
    mine = bit_of(axis, bit)
    keep = lax.dynamic_index_in_dim(value, mine, dim, keepdims=False)
    send = lax.dynamic_index_in_dim(value, 1 - mine, dim, keepdims=False)
    return keep.astype(F32) + swapped(send.astype(BF16), axis, bit).astype(F32)


def bits(axis):
    return lax.axis_size(axis).bit_length() - 1


def gather_filters(shard):
    space, chan = lax.axis_size("space"), lax.axis_size("chan")
    edge, inputs, mine = shard.shape[0], shard.shape[3], shard.shape[4]
    taps = edge**3
    each = -(-taps // space)
    flat = jnp.transpose(shard.reshape(taps, inputs, mine), (0, 2, 1))
    flat = jnp.pad(flat, ((0, each * space - taps), (0, 0), (0, 0)))
    part = lax.dynamic_slice_in_dim(flat, lax.axis_index("space") * each, each, 0)
    count = bits("chan")
    for step, bit in enumerate(reversed(range(count))):
        part = doubled(part, "chan", bit, step)
    part = part.reshape(chan, each, mine, inputs)
    count = bits("space")
    for step, bit in enumerate(reversed(range(count))):
        part = doubled(part, "space", bit, step)
    part = part.reshape(space, chan, each, mine, inputs)
    full = jnp.transpose(part, (0, 2, 1, 3, 4)).reshape(each * space, chan * mine, inputs)
    full = full[:taps].reshape(edge, edge, edge, chan * mine, inputs)
    return jnp.transpose(full, (0, 1, 2, 4, 3))


def sum_filters(terms):
    space, chan = lax.axis_size("space"), lax.axis_size("chan")
    edge, inputs, filters = terms.shape[0], terms.shape[3], terms.shape[4]
    taps = edge**3
    each = -(-taps // space)
    mine = filters // chan
    flat = jnp.transpose(terms.reshape(taps, inputs, filters), (0, 2, 1))
    flat = jnp.pad(flat, ((0, each * space - taps), (0, 0), (0, 0)))
    count = bits("space")
    part = flat.reshape((2,) * count + (each, filters, inputs))
    for bit in range(count):
        part = halved(part, "space", bit, count - 1 - bit)
    count = bits("chan")
    part = part.reshape((each,) + (2,) * count + (mine, inputs))
    for bit in range(count):
        part = halved(part, "chan", bit, 1 + count - 1 - bit)
    part = part.astype(BF16)
    count = bits("space")
    for step, bit in enumerate(reversed(range(count))):
        part = doubled(part, "space", bit, step)
    full = part.reshape(each * space, mine, inputs)[:taps].astype(F32)
    return jnp.transpose(full, (0, 2, 1)).reshape(edge, edge, edge, inputs, mine)


def conv_forward(padded, filters):
    return lax.conv_general_dilated(
        padded,
        filters,
        (2, 2, 2),
        "VALID",
        dimension_numbers=("NDHWC", "DHWIO", "NDHWC"),
        preferred_element_type=F32,
    )


def filter_grad(padded, grad_cells):
    result = lax.conv_general_dilated(
        padded,
        grad_cells,
        (1, 1, 1),
        "VALID",
        rhs_dilation=(2, 2, 2),
        dimension_numbers=("CDHWN", "IDHWO", "NDHWC"),
        preferred_element_type=F32,
    )
    return jnp.transpose(result, (1, 2, 3, 0, 4)).astype(BF16)


def input_grad(grad_ext, filters):
    flipped = filters[::-1, ::-1, ::-1]
    return lax.conv_general_dilated(
        grad_ext,
        flipped,
        (1, 1, 1),
        ((1, 0), (1, 0), (1, 2)),
        lhs_dilation=(2, 2, 2),
        dimension_numbers=("NDHWC", "DHWOI", "NDHWC"),
        preferred_element_type=F32,
    )


def low_padded(block):
    plane = shifted(block[:, -1:], "space", 1)
    stacked = jnp.concatenate([plane, block], axis=1)
    row = shifted(stacked[:, :, -1:], "chan", 1)
    both = jnp.concatenate([row, stacked], axis=2)
    return jnp.pad(both, ((0, 0), (0, 0), (0, 0), (1, 0), (0, 0)))


def high_extended(cells):
    plane = shifted(cells[:, :1], "space", -1)
    stacked = jnp.concatenate([cells, plane], axis=1)
    row = shifted(stacked[:, :, :1], "chan", -1)
    return jnp.concatenate([stacked, row], axis=2)


def spread_cells(cotangent):
    chan = lax.axis_size("chan")
    vols, side_a, side_b, side_c, mine = cotangent.shape
    rows = side_b // chan
    flat = cotangent.reshape(vols, side_a, side_b, side_c * mine)
    count = bits("chan")
    for step, bit in enumerate(reversed(range(count))):
        flat = doubled(flat, "chan", bit, step)
    flat = flat.reshape(chan, vols, side_a, side_b, side_c * mine)
    flat = jnp.pad(flat, ((0, 0), (0, 0), (0, 0), (0, 1), (0, 0)))
    near = lax.dynamic_slice_in_dim(flat, lax.axis_index("chan") * rows, rows + 1, 3)
    near = near.reshape(chan, vols, side_a, rows + 1, side_c, mine)
    near = jnp.transpose(near, (1, 2, 3, 4, 0, 5))
    near = near.reshape(vols, side_a, rows + 1, side_c, chan * mine)
    plane = shifted(near[:, :1], "space", -1)
    return jnp.concatenate([near, plane], axis=1)


def local(volume, w_first, w_second, cotangent):
    first_full = gather_filters(w_first)
    vol_pad = low_padded(volume)
    grad_ext = spread_cells(cotangent)
    grad_cells = grad_ext[:, :-1, :-1]
    pre_first = conv_forward(vol_pad, first_full)
    hidden_act = jnp.where(pre_first > 0, pre_first, 0.3 * pre_first).astype(BF16)
    act_pad = low_padded(hidden_act)
    second_full = gather_filters(w_second)
    second_grad = sum_filters(filter_grad(act_pad, grad_cells))
    local_out = conv_forward(act_pad, second_full).astype(BF16)
    second_out = lax.all_to_all(local_out, "chan", split_axis=4, concat_axis=2, tiled=True)
    act_back = input_grad(grad_ext, second_full)
    pre_back = (act_back * jnp.where(pre_first > 0, 1.0, 0.3)).astype(BF16)
    first_grad = sum_filters(filter_grad(vol_pad, pre_back))
    volume_grad = input_grad(high_extended(pre_back), first_full).astype(BF16)
    return (second_out, volume_grad, first_grad, second_grad)


def solution(mesh):
    return jax.shard_map(
        local,
        mesh=mesh,
        in_specs=(
            P(None, "space", "chan", None, None),
            P(None, None, None, None, "chan"),
            P(None, None, None, None, "chan"),
            P(None, "space", None, None, "chan"),
        ),
        out_specs=(
            P(None, "space", None, None, "chan"),
            P(None, "space", "chan", None, None),
            P(None, None, None, None, "chan"),
            P(None, None, None, None, "chan"),
        ),
        check_vma=False,
    )
```

```python
import functools

import jax
import jax.numpy as jnp
from jax import lax
from jax.experimental import pallas as pl
from jax.experimental.pallas import tpu as pltpu
from jax.sharding import PartitionSpec as P

BF16 = jnp.bfloat16
F32 = jnp.float32
LANES = 128
PAD = 8
NT = (((1,), (1,)), ((), ()))
NN = (((1,), (0,)), ((), ()))
REACH = (((1, 0),), ((0, 1), (2, 0)))


def dot(left, right, dims):
    return lax.dot_general(left, right, dims, preferred_element_type=F32)


def bits(axis):
    return lax.axis_size(axis).bit_length() - 1


def gather_order(axis):
    return list(reversed(range(bits(axis))))


def chan_gather_order():
    return [bit for bit in reversed(range(bits("chan"))) if bit] + [0]


def chan_sum_order():
    return [0] + [bit for bit in reversed(range(bits("chan"))) if bit]


def shifted(value, steps):
    pairs = []
    sizes = (lax.axis_size("space"), lax.axis_size("chan"))
    for a in range(sizes[0]):
        for b in range(sizes[1]):
            to = (a + steps[0], b + steps[1])
            if 0 <= to[0] < sizes[0] and 0 <= to[1] < sizes[1]:
                pairs.append((a * sizes[1] + b, to[0] * sizes[1] + to[1]))
    return lax.ppermute(value, ("space", "chan"), pairs)


def swapped(value, axis, bit):
    count = lax.axis_size(axis)
    return lax.ppermute(value, axis, [(i, i ^ (1 << bit)) for i in range(count)])


def doubled(value, axis, bit):
    return jnp.stack([value, swapped(value, axis, bit)])


def position():
    return jnp.stack([lax.axis_index("space"), lax.axis_index("chan")]).astype(jnp.int32)


def gather_filters(shard):
    space = lax.axis_size("space")
    edge, inputs, mine = shard.shape[0], shard.shape[3], shard.shape[4]
    taps = edge**3
    each = -(-taps // space)
    flat = jnp.transpose(shard.reshape(taps, inputs, mine), (0, 2, 1))
    flat = jnp.pad(flat, ((0, each * space - taps), (0, 0), (0, 0)))
    part = lax.dynamic_slice_in_dim(flat, lax.axis_index("space") * each, each, 0)
    for bit in chan_gather_order():
        part = doubled(part, "chan", bit)
    for bit in gather_order("space"):
        part = doubled(part, "space", bit)
    return part.reshape(space, lax.axis_size("chan"), each, mine, inputs)


def relative(index, mine, order):
    apart = index ^ mine
    place = 0
    for bit in order:
        place = place * 2 + ((apart >> bit) & 1)
    return place


def filter_tap(ref, here, tap, orders):
    each = ref.shape[2]
    owner = relative(tap // each, here[0], orders[0])
    rows = [
        ref[owner, relative(chan, here[1], orders[1]), tap % each]
        for chan in range(ref.shape[1])
    ]
    return jnp.concatenate(rows, axis=0)


def call(kernel, outs, args, scratch=(), grid=None, in_specs=None, out_specs=None, flops=0):
    moved = sum(a.size * a.dtype.itemsize for a in args)
    moved += sum(o.size * o.dtype.itemsize for o in outs)
    whole = pl.BlockSpec(memory_space=pltpu.VMEM)
    smem = pl.BlockSpec(memory_space=pltpu.SMEM)
    specs = in_specs or [smem if a.dtype == jnp.int32 else whole for a in args]
    return pl.pallas_call(
        kernel,
        out_shape=outs,
        grid=grid or (),
        in_specs=specs,
        out_specs=out_specs or [whole] * len(outs),
        scratch_shapes=scratch,
        cost_estimate=pl.CostEstimate(flops=flops, bytes_accessed=moved, transcendentals=0),
        compiler_params=pltpu.CompilerParams(vmem_limit_bytes=56 * 2**20),
    )(*args)


def parted_tile(tile, wide, base, store):
    depth, lanes = tile.shape
    for part in range(lanes // LANES):
        rows = wide.at[part]
        rows[pl.ds(base, PAD), :] = jnp.zeros((PAD, LANES), F32)
        rows[pl.ds(base + PAD, depth), :] = tile[:, part * LANES : (part + 1) * LANES].astype(F32)
        for k in range(3):
            piece = rows[pl.ds(base + PAD - 1 + k, depth // 2, stride=2), :]
            store(k, part, piece.astype(BF16))


def part_kernel(own, plane, row, out, wide):
    _, wide_a, wide_b, depth, _ = (1, out.shape[2], out.shape[3], own.shape[3], own.shape[4])
    for a in range(wide_a):
        for b in range(wide_b):
            if b == 0:
                tile = row[0, a, 0]
            elif a == 0:
                tile = plane[0, 0, b - 1]
            else:
                tile = own[0, a - 1, b - 1]
            slot = ((a * wide_b + b) % 8) * (PAD + depth)

            def store(k, part, piece):
                out[k, 0, a, b, :, part * LANES : (part + 1) * LANES] = piece

            parted_tile(tile, wide, slot, store)


def parted(own, plane, row):
    vols, side_a, side_b, depth, lanes = own.shape
    out = jax.ShapeDtypeStruct((3, vols, side_a + 1, side_b + 1, depth // 2, lanes), BF16)

    def block(shape):
        return pl.BlockSpec((1,) + shape[1:], lambda n: (n, 0, 0, 0, 0))

    return call(
        part_kernel,
        [out],
        (own, plane, row),
        [pltpu.VMEM((lanes // LANES, 8 * (PAD + depth), LANES), F32)],
        (vols,),
        [block(own.shape), block(plane.shape), block(row.shape)],
        [pl.BlockSpec((3, 1) + out.shape[2:], lambda n: (0, n, 0, 0, 0, 0))],
    )[0]


def window(ref, i, j, sides):
    vols, side_a, side_b = sides
    rows = []
    for n in range(vols):
        for a in range(side_a):
            for b in range(side_b):
                rows.append(
                    jnp.concatenate([ref[k, n, 2 * a + i, 2 * b + j] for k in range(3)], axis=1)
                )
    return jnp.concatenate(rows, axis=0)


def forward_kernel(orders, sides, here, ref, filters, *rest):
    outs, acc = rest[:-1], rest[-1]

    def step(ij, carry):
        i, j = ij // 3, ij % 3
        left = window(ref, i, j, sides)
        right = jnp.concatenate(
            [filter_tap(filters, here, ij * 3 + k, orders) for k in range(3)], axis=1
        )
        part = dot(left, right, NT)
        acc[...] = jnp.where(ij == 0, part, acc[...] + part)
        return carry

    lax.fori_loop(0, 9, step, 0)
    total = acc[...]
    depth = ref.shape[4]
    vols, side_a, side_b = sides
    if len(outs) == 1:
        outs[0][...] = total.astype(BF16).reshape(outs[0].shape)
        return
    hidden, plane, row = outs
    act = jnp.where(total > 0, total, 0.3 * total).astype(BF16)
    act = act.reshape(vols, side_a, side_b, depth, total.shape[1])
    hidden[...] = act
    plane[...] = act[:, side_a - 1 :]
    row[...] = act[:, :, side_b - 1 :]


def forward(here, ref, filters, orders, split):
    _, vols, wide_a, wide_b, depth, inputs = ref.shape
    sides = (vols, (wide_a - 1) // 2, (wide_b - 1) // 2)
    count = filters.shape[1] * filters.shape[3]
    cells = vols * sides[1] * sides[2] * depth
    shape = sides + (depth, count)
    outs = [jax.ShapeDtypeStruct(shape, BF16)]
    if split:
        outs.append(jax.ShapeDtypeStruct((vols, 1) + shape[2:], BF16))
        outs.append(jax.ShapeDtypeStruct(shape[:2] + (1,) + shape[3:], BF16))
    return call(
        functools.partial(forward_kernel, orders, sides),
        outs,
        (here, ref, filters),
        [pltpu.VMEM((cells, count), F32)],
        flops=2 * cells * 27 * inputs * count,
    )


def grads_kernel(orders, sides, here, ref, grads, keep, send, turned):
    cells, count = turned.shape[1], turned.shape[0]
    inputs = ref.shape[5]
    chans = 2 ** len(orders[1])
    mine = count // chans
    each = keep.shape[2]
    turned[...] = jnp.transpose(grads[...].reshape(cells, count).astype(F32), (1, 0)).astype(BF16)

    def step(ij, carry):
        part = dot(turned[...], window(ref, ij // 3, ij % 3, sides), NN).astype(BF16)
        for k in range(3):
            tap = ij * 3 + k
            place = relative(tap // each, here[0], orders[0])
            half = keep.shape[0]
            for chan in range(chans):
                block = part[chan * mine : (chan + 1) * mine, k * inputs : (k + 1) * inputs]
                to = relative(chan, here[1], orders[1])

                @pl.when(place < half)
                def _():
                    keep[place, to, tap % each] = block

                @pl.when(place >= half)
                def _():
                    send[place - half, to, tap % each] = block

        return carry

    lax.fori_loop(0, 9, step, 0)
    for tap in range(27, each * 2 * keep.shape[0]):
        place = relative(tap // each, here[0], orders[0])
        blank = jnp.zeros((chans, mine, inputs), BF16)

        @pl.when(place < keep.shape[0])
        def _():
            keep[place, :, tap % each] = blank

        @pl.when(place >= keep.shape[0])
        def _():
            send[place - keep.shape[0], :, tap % each] = blank


def filter_grads(here, ref, grads, orders):
    _, vols, wide_a, wide_b, depth, inputs = ref.shape
    sides = (vols, (wide_a - 1) // 2, (wide_b - 1) // 2)
    cells = vols * sides[1] * sides[2] * depth
    count = grads.shape[-1]
    space, chans = 2 ** len(orders[0]), 2 ** len(orders[1])
    each = -(-27 // space)
    out = jax.ShapeDtypeStruct((space // 2, chans, each, count // chans, inputs), BF16)
    return call(
        functools.partial(grads_kernel, orders, sides),
        [out, out],
        (here, ref, grads),
        [pltpu.VMEM((count, cells), BF16)],
        flops=2 * cells * 27 * inputs * count,
    )


def sum_filters(keep, send):
    each, mine, inputs = keep.shape[2:]
    total = None
    order = [("space", bit) for bit in range(bits("space"))]
    order += [("chan", bit) for bit in chan_sum_order()]
    for axis, bit in order:
        if total is not None:
            half = total.shape[0] // 2
            keep, send = total[:half], total[half:]
        else:
            keep = keep.reshape(-1, each, mine, inputs)
            send = send.reshape(-1, each, mine, inputs)
        total = keep.astype(F32) + swapped(send.astype(BF16), axis, bit).astype(F32)
    part = total[0].astype(BF16)
    for bit in gather_order("space"):
        part = doubled(part, "space", bit)
    space = lax.axis_size("space")
    part = part.reshape(space, each, mine, inputs)
    places = jnp.arange(space) ^ lax.axis_index("space")
    taps = [lax.dynamic_index_in_dim(part, space_order(places[s]), 0, keepdims=False) for s in range(space)]
    full = jnp.concatenate(taps, axis=0)[:27].astype(F32)
    return jnp.transpose(full, (0, 2, 1)).reshape(3, 3, 3, inputs, mine)


def space_order(apart):
    place = 0
    for bit in range(bits("space")):
        place = place * 2 + ((apart >> bit) & 1)
    return place


def stepped_tile(tile, wide, base, store):
    depth, lanes = tile.shape
    for part in range(lanes // LANES):
        rows = wide.at[part]
        rows[pl.ds(base + depth, PAD), :] = jnp.zeros((PAD, LANES), F32)
        rows[pl.ds(base, depth), :] = tile[:, part * LANES : (part + 1) * LANES].astype(F32)
        store(part, rows[pl.ds(base + 1, depth), :].astype(BF16))


def back_kernel(orders, here, cells, filters, hidden, out, plane, row, wide, moved, spread):
    vols, wide_a, wide_b, depth, count = cells.shape
    side_a, side_b = wide_a - 1, wide_b - 1
    inputs = filters.shape[4]
    for n in range(vols):
        for a in range(wide_a):
            for b in range(wide_b):
                slot = ((n * wide_a + a) * wide_b + b) % 8 * (PAD + depth)

                def store(part, piece):
                    moved[n, a, b, :, part * LANES : (part + 1) * LANES] = piece

                stepped_tile(cells[n, a, b], wide, slot, store)

    def lefts(ref, da, db):
        return ref[:, da : da + side_a, db : db + side_b].reshape(-1, count)

    for sa in range(2):
        for sb in range(2):
            even = odd = None
            for i, da in REACH[sa]:
                for j, db in REACH[sb]:
                    tap = (i * 3 + j) * 3
                    here_cells = lefts(cells, da, db)
                    first = dot(here_cells, filter_tap(filters, here, tap + 1, orders), NN)
                    second = dot(here_cells, filter_tap(filters, here, tap + 2, orders), NN)
                    second += dot(lefts(moved, da, db), filter_tap(filters, here, tap, orders), NN)
                    even = first if even is None else even + first
                    odd = second if odd is None else odd + second
            for parity, value in enumerate((even, odd)):
                value = value.reshape(vols, side_a, side_b, depth, inputs)
                for n in range(vols):
                    for a in range(side_a):
                        for b in range(side_b):
                            for part in range(inputs // LANES):
                                spread[
                                    part, n, 2 * a + sa, 2 * b + sb, pl.ds(parity, depth, stride=2), :
                                ] = value[n, a, b, :, part * LANES : (part + 1) * LANES]
    for part in range(inputs // LANES):
        lanes = slice(part * LANES, (part + 1) * LANES)
        act = hidden[:, :, :, :, lanes].astype(F32)
        value = (spread[part] * jnp.where(act > 0, 1.0, 0.3)).astype(BF16)
        out[:, :, :, :, lanes] = value
        plane[:, :, :, :, lanes] = value[:, :1]
        row[:, :, :, :, lanes] = value[:, :, :1]


def hidden_back(here, cells, filters, hidden, orders):
    vols, wide_a, wide_b, depth, count = cells.shape
    inputs = hidden.shape[-1]
    shape = hidden.shape
    outs = [
        jax.ShapeDtypeStruct(shape, BF16),
        jax.ShapeDtypeStruct((vols, 1) + shape[2:], BF16),
        jax.ShapeDtypeStruct(shape[:2] + (1,) + shape[3:], BF16),
    ]
    return call(
        functools.partial(back_kernel, orders),
        outs,
        (here, cells, filters, hidden),
        [
            pltpu.VMEM((count // LANES, 8 * (PAD + depth), LANES), F32),
            pltpu.VMEM(cells.shape, BF16),
            pltpu.VMEM((inputs // LANES,) + shape[:4] + (LANES,), F32),
        ],
        flops=2 * vols * (wide_a - 1) * (wide_b - 1) * depth * 27 * inputs * count,
    )


def volume_kernel(orders, here, cells, plane, row, filters, out, wide, ext, moved, spread):
    _, side_a, side_b, depth, count = cells.shape
    inputs = filters.shape[4]
    for a in range(side_a + 1):
        for b in range(side_b + 1):
            if b == side_b:
                tile = row[0, a, 0]
            elif a == side_a:
                tile = plane[0, 0, b]
            else:
                tile = cells[0, a, b]
            ext[a, b] = tile
            slot = ((a * (side_b + 1) + b) % 8) * (PAD + depth)

            def store(part, piece):
                moved[a, b, :, part * LANES : (part + 1) * LANES] = piece

            stepped_tile(tile, wide, slot, store)

    def lefts(ref, da, db):
        return ref[da : da + side_a, db : db + side_b].reshape(-1, count)

    for sa in range(2):
        for sb in range(2):
            both = late = None
            for i, da in REACH[sa]:
                for j, db in REACH[sb]:
                    tap = (i * 3 + j) * 3
                    pair = jnp.concatenate(
                        [filter_tap(filters, here, tap + k, orders) for k in (1, 2)], axis=1
                    )
                    first = dot(lefts(ext, da, db), pair, NN)
                    second = dot(lefts(moved, da, db), filter_tap(filters, here, tap, orders), NN)
                    both = first if both is None else both + first
                    late = second if late is None else late + second
            halves = (both[:, :inputs], both[:, inputs:] + late)
            for parity, value in enumerate(halves):
                value = value.reshape(side_a, side_b, depth, inputs)
                for a in range(side_a):
                    for b in range(side_b):
                        spread[2 * a + sa, 2 * b + sb, pl.ds(parity, depth, stride=2), :] = value[a, b]
    out[0] = spread[...].astype(BF16)


def volume_grads(here, cells, plane, row, filters, orders):
    vols, side_a, side_b, depth, count = cells.shape
    inputs = filters.shape[4]
    out = jax.ShapeDtypeStruct((vols, 2 * side_a, 2 * side_b, 2 * depth, inputs), BF16)

    def block(shape):
        return pl.BlockSpec((1,) + shape[1:], lambda n: (n, 0, 0, 0, 0))

    return call(
        functools.partial(volume_kernel, orders),
        [out],
        (here, cells, plane, row, filters),
        [
            pltpu.VMEM((count // LANES, 8 * (PAD + depth), LANES), F32),
            pltpu.VMEM((side_a + 1, side_b + 1, depth, count), BF16),
            pltpu.VMEM((side_a + 1, side_b + 1, depth, count), BF16),
            pltpu.VMEM((2 * side_a, 2 * side_b, 2 * depth, inputs), F32),
        ],
        (vols,),
        [
            pl.BlockSpec(memory_space=pltpu.SMEM),
            block(cells.shape),
            block(plane.shape),
            block(row.shape),
            pl.BlockSpec(memory_space=pltpu.VMEM),
        ],
        [block(out.shape)],
        flops=2 * vols * side_a * side_b * depth * 27 * inputs * count,
    )[0]


def spread_cells(cotangent):
    chan = lax.axis_size("chan")
    vols, side_a, side_b, side_c, mine = cotangent.shape
    rows = side_b // chan
    flat = cotangent.reshape(vols, side_a, side_b, side_c * mine)
    for step, bit in enumerate(gather_order("chan")):
        other = swapped(flat, "chan", bit)
        high = (lax.axis_index("chan") >> bit) & 1 == 1
        flat = jnp.stack([jnp.where(high, other, flat), jnp.where(high, flat, other)], axis=step)
    flat = flat.reshape(chan, vols, side_a, side_b, side_c * mine)
    flat = jnp.pad(flat, ((0, 0), (0, 0), (0, 0), (0, 1), (0, 0)))
    near = lax.dynamic_slice_in_dim(flat, lax.axis_index("chan") * rows, rows + 1, 3)
    near = near.reshape(chan, vols, side_a, rows + 1, side_c, mine)
    near = jnp.transpose(near, (1, 2, 3, 4, 0, 5))
    near = near.reshape(vols, side_a, rows + 1, side_c, chan * mine)
    plane = shifted(near[:, :1], (-1, 0))
    return jnp.concatenate([near, plane], axis=1)


def local(volume, w_first, w_second, cotangent):
    here = position()
    gathered = (list(range(bits("space"))), [0] + [b for b in range(1, bits("chan"))])
    summed = (list(range(bits("space"))), chan_sum_order())
    plane = shifted(volume[:, -1:], (1, 0))
    row = shifted(jnp.concatenate([plane, volume], axis=1)[:, :, -1:], (0, 1))
    first_full = gather_filters(w_first)
    second_full = gather_filters(w_second)
    grad_ext = spread_cells(cotangent)
    grad_cells = grad_ext[:, :-1, :-1]
    vol_parts = parted(volume, plane, row)
    hidden, hid_plane, hid_row = forward(here, vol_parts, first_full, gathered, True)
    plane = shifted(hid_plane, (1, 0))
    row = shifted(hid_row, (0, 1))
    corner = shifted(hid_row[:, -1:], (1, 1))
    act_parts = parted(hidden, plane, jnp.concatenate([corner, row], axis=1))
    second_grad = sum_filters(*filter_grads(here, act_parts, grad_cells, summed))
    pre_back, pre_plane, pre_row = hidden_back(here, grad_ext, second_full, hidden, gathered)
    first_grad = sum_filters(*filter_grads(here, vol_parts, pre_back, summed))
    local_out = forward(here, act_parts, second_full, gathered, False)[0]
    second_out = lax.all_to_all(local_out, "chan", split_axis=4, concat_axis=2, tiled=True)
    plane = shifted(pre_plane, (-1, 0))
    row = shifted(jnp.concatenate([pre_row, plane[:, :, :1]], axis=1), (0, -1))
    volume_grad = volume_grads(here, pre_back, plane, row, first_full, gathered)
    return (second_out, volume_grad, first_grad, second_grad)


def solution(mesh):
    return jax.shard_map(
        local,
        mesh=mesh,
        in_specs=(
            P(None, "space", "chan", None, None),
            P(None, None, None, None, "chan"),
            P(None, None, None, None, "chan"),
            P(None, "space", None, None, "chan"),
        ),
        out_specs=(
            P(None, "space", None, None, "chan"),
            P(None, "space", "chan", None, None),
            P(None, None, None, None, "chan"),
            P(None, None, None, None, "chan"),
        ),
        check_vma=False,
    )
```

```python
import functools

import jax
import jax.numpy as jnp
from jax import lax
from jax.experimental import pallas as pl
from jax.experimental.pallas import tpu as pltpu
from jax.sharding import PartitionSpec as P

BF16 = jnp.bfloat16
F32 = jnp.float32
LANES = 128
PAD = 8
NT = (((1,), (1,)), ((), ()))
NN = (((1,), (0,)), ((), ()))
REACH = (((1, 0),), ((0, 1), (2, 0)))


def dot(left, right, dims):
    return lax.dot_general(left, right, dims, preferred_element_type=F32)


def bits(axis):
    return lax.axis_size(axis).bit_length() - 1


def chan_sum_order():
    return [0] + [bit for bit in reversed(range(bits("chan"))) if bit]


def shifted(value, steps):
    pairs = []
    sizes = (lax.axis_size("space"), lax.axis_size("chan"))
    for a in range(sizes[0]):
        for b in range(sizes[1]):
            to = (a + steps[0], b + steps[1])
            if 0 <= to[0] < sizes[0] and 0 <= to[1] < sizes[1]:
                pairs.append((a * sizes[1] + b, to[0] * sizes[1] + to[1]))
    return lax.ppermute(value, ("space", "chan"), pairs)


def swapped(value, axis, bit):
    count = lax.axis_size(axis)
    return lax.ppermute(value, axis, [(i, i ^ (1 << bit)) for i in range(count)])


def doubled(value, axis, bit, name):
    with jax.named_scope(name):
        other = swapped(value, axis, bit)
    return jnp.stack([value, other])


def position():
    return jnp.stack([lax.axis_index("space"), lax.axis_index("chan")]).astype(jnp.int32)


def own_part(shard):
    space = lax.axis_size("space")
    edge, inputs, mine = shard.shape[0], shard.shape[3], shard.shape[4]
    taps = edge**3
    each = -(-taps // space)
    flat = jnp.transpose(shard.reshape(taps, inputs, mine), (0, 2, 1))
    flat = jnp.pad(flat, ((0, each * space - taps), (0, 0), (0, 0)))
    return lax.dynamic_slice_in_dim(flat, lax.axis_index("space") * each, each, 0)


def far_bits():
    return list(reversed(range(1, bits("chan"))))


def high_bits():
    return list(reversed(range(1, bits("space"))))


def after(value, other):
    return lax.optimization_barrier((value, other))[0]


def finish_gather(part, name, gate=None):
    each, mine, inputs = part.shape[-3:]
    for bit in high_bits():
        part = doubled(part, "space", bit, f"{name}_y")
    part = doubled(part, "space", 0, f"{name}_core")
    return part.reshape(lax.axis_size("space"), lax.axis_size("chan"), each, mine, inputs)


def mixed_gather(part, name):
    each, mine, inputs = part.shape
    for bit in far_bits():
        part = doubled(part, "chan", bit, f"{name}_z")
    far = part.shape[:-3]
    highs = len(high_bits())
    cut = (each + 1) // 2
    one, two = part[..., :cut, :, :], part[..., cut:, :, :]
    one = doubled(one, "chan", 0, f"{name}_x1")
    for bit in high_bits():
        two = doubled(two, "space", bit, f"{name}_y1")
    for bit in high_bits():
        one = doubled(one, "space", bit, f"{name}_y2")
    two = doubled(two, "chan", 0, f"{name}_x2")
    one = doubled(one, "space", 0, f"{name}_core")
    two = doubled(two, "space", 0, f"{name}_core")
    two = jnp.moveaxis(two, 1, 1 + highs)
    whole = jnp.concatenate([one, two], axis=-3)
    return whole.reshape(lax.axis_size("space"), lax.axis_size("chan"), each, mine, inputs)


def relative(index, mine, order):
    apart = index ^ mine
    place = 0
    for bit in order:
        place = place * 2 + ((apart >> bit) & 1)
    return place


def filter_tap(ref, here, tap, orders):
    each = ref.shape[2]
    owner = relative(tap // each, here[0], orders[0])
    rows = [
        ref[owner, relative(chan, here[1], orders[1]), tap % each]
        for chan in range(ref.shape[1])
    ]
    return jnp.concatenate(rows, axis=0)


def call(kernel, outs, args, scratch=(), grid=None, in_specs=None, out_specs=None, flops=0):
    moved = sum(a.size * a.dtype.itemsize for a in args)
    moved += sum(o.size * o.dtype.itemsize for o in outs)
    whole = pl.BlockSpec(memory_space=pltpu.VMEM)
    smem = pl.BlockSpec(memory_space=pltpu.SMEM)
    specs = in_specs or [smem if a.dtype == jnp.int32 else whole for a in args]
    return pl.pallas_call(
        kernel,
        out_shape=outs,
        grid=grid or (),
        in_specs=specs,
        out_specs=out_specs or [whole] * len(outs),
        scratch_shapes=scratch,
        cost_estimate=pl.CostEstimate(flops=flops, bytes_accessed=moved, transcendentals=0),
        compiler_params=pltpu.CompilerParams(vmem_limit_bytes=56 * 2**20),
    )(*args)


def parted_tile(tile, wide, base, store):
    depth, lanes = tile.shape
    for part in range(lanes // LANES):
        rows = wide.at[part]
        rows[pl.ds(base, PAD), :] = jnp.zeros((PAD, LANES), F32)
        rows[pl.ds(base + PAD, depth), :] = tile[:, part * LANES : (part + 1) * LANES].astype(F32)
        for k in range(3):
            piece = rows[pl.ds(base + PAD - 1 + k, depth // 2, stride=2), :]
            store(k, part, piece.astype(BF16))


def part_kernel(own, plane, row, out, wide):
    _, wide_a, wide_b, depth, _ = (1, out.shape[2], out.shape[3], own.shape[3], own.shape[4])
    for a in range(wide_a):
        for b in range(wide_b):
            if b == 0:
                tile = row[0, a, 0]
            elif a == 0:
                tile = plane[0, 0, b - 1]
            else:
                tile = own[0, a - 1, b - 1]
            slot = ((a * wide_b + b) % 8) * (PAD + depth)

            def store(k, part, piece):
                out[k, 0, a, b, :, part * LANES : (part + 1) * LANES] = piece

            parted_tile(tile, wide, slot, store)


def parted(own, plane, row):
    vols, side_a, side_b, depth, lanes = own.shape
    out = jax.ShapeDtypeStruct((3, vols, side_a + 1, side_b + 1, depth // 2, lanes), BF16)

    def block(shape):
        return pl.BlockSpec((1,) + shape[1:], lambda n: (n, 0, 0, 0, 0))

    return call(
        part_kernel,
        [out],
        (own, plane, row),
        [pltpu.VMEM((lanes // LANES, 8 * (PAD + depth), LANES), F32)],
        (vols,),
        [block(own.shape), block(plane.shape), block(row.shape)],
        [pl.BlockSpec((3, 1) + out.shape[2:], lambda n: (0, n, 0, 0, 0, 0))],
    )[0]


def window(ref, i, j, sides):
    vols, side_a, side_b = sides
    rows = []
    for n in range(vols):
        for a in range(side_a):
            for b in range(side_b):
                rows.append(
                    jnp.concatenate([ref[k, n, 2 * a + i, 2 * b + j] for k in range(3)], axis=1)
                )
    return jnp.concatenate(rows, axis=0)


def forward_kernel(orders, sides, here, ref, filters, *rest):
    outs, acc = rest[:-1], rest[-1]

    def step(ij, carry):
        i, j = ij // 3, ij % 3
        left = window(ref, i, j, sides)
        right = jnp.concatenate(
            [filter_tap(filters, here, ij * 3 + k, orders) for k in range(3)], axis=1
        )
        part = dot(left, right, NT)
        acc[...] = jnp.where(ij == 0, part, acc[...] + part)
        return carry

    lax.fori_loop(0, 9, step, 0)
    total = acc[...]
    depth = ref.shape[4]
    vols, side_a, side_b = sides
    if len(outs) == 1:
        outs[0][...] = total.astype(BF16).reshape(outs[0].shape)
        return
    hidden, plane, row = outs
    act = jnp.where(total > 0, total, 0.3 * total).astype(BF16)
    act = act.reshape(vols, side_a, side_b, depth, total.shape[1])
    hidden[...] = act
    plane[...] = act[:, side_a - 1 :]
    row[...] = act[:, :, side_b - 1 :]


def forward(here, ref, filters, orders, split):
    _, vols, wide_a, wide_b, depth, inputs = ref.shape
    sides = (vols, (wide_a - 1) // 2, (wide_b - 1) // 2)
    count = filters.shape[1] * filters.shape[3]
    cells = vols * sides[1] * sides[2] * depth
    shape = sides + (depth, count)
    outs = [jax.ShapeDtypeStruct(shape, BF16)]
    if split:
        outs.append(jax.ShapeDtypeStruct((vols, 1) + shape[2:], BF16))
        outs.append(jax.ShapeDtypeStruct(shape[:2] + (1,) + shape[3:], BF16))
    return call(
        functools.partial(forward_kernel, orders, sides),
        outs,
        (here, ref, filters),
        [pltpu.VMEM((cells, count), F32)],
        flops=2 * cells * 27 * inputs * count,
    )


def grads_kernel(orders, sides, here, ref, grads, keep, send, turned):
    cells, count = turned.shape[1], turned.shape[0]
    inputs = ref.shape[5]
    chans = 2 ** len(orders[1])
    mine = count // chans
    each = keep.shape[2]
    turned[...] = jnp.transpose(grads[...].reshape(cells, count).astype(F32), (1, 0)).astype(BF16)

    def step(ij, carry):
        part = dot(turned[...], window(ref, ij // 3, ij % 3, sides), NN).astype(BF16)
        for k in range(3):
            tap = ij * 3 + k
            place = relative(tap // each, here[0], orders[0])
            half = keep.shape[0]
            for chan in range(chans):
                block = part[chan * mine : (chan + 1) * mine, k * inputs : (k + 1) * inputs]
                to = relative(chan, here[1], orders[1])

                @pl.when(place < half)
                def _():
                    keep[place, to, tap % each] = block

                @pl.when(place >= half)
                def _():
                    send[place - half, to, tap % each] = block

        return carry

    lax.fori_loop(0, 9, step, 0)
    for tap in range(27, each * 2 * keep.shape[0]):
        place = relative(tap // each, here[0], orders[0])
        blank = jnp.zeros((chans, mine, inputs), BF16)

        @pl.when(place < keep.shape[0])
        def _():
            keep[place, :, tap % each] = blank

        @pl.when(place >= keep.shape[0])
        def _():
            send[place - keep.shape[0], :, tap % each] = blank


def filter_grads(here, ref, grads, orders):
    _, vols, wide_a, wide_b, depth, inputs = ref.shape
    sides = (vols, (wide_a - 1) // 2, (wide_b - 1) // 2)
    cells = vols * sides[1] * sides[2] * depth
    count = grads.shape[-1]
    space, chans = 2 ** len(orders[0]), 2 ** len(orders[1])
    each = -(-27 // space)
    out = jax.ShapeDtypeStruct((space // 2, chans, each, count // chans, inputs), BF16)
    return call(
        functools.partial(grads_kernel, orders, sides),
        [out, out],
        (here, ref, grads),
        [pltpu.VMEM((count, cells), BF16)],
        flops=2 * cells * 27 * inputs * count,
    )


def core_sum(keep, send, name):
    tail = keep.shape[2:]
    with jax.named_scope(f"{name}_core"):
        other = swapped(send, "space", 0)
    total = keep.astype(F32) + other.astype(F32)
    highs = bits("space") - 1
    return total.reshape((2,) * highs + (2, -1) + tail)


def half_sum(value, axis, bit, dim, name):
    keep = lax.index_in_dim(value, 0, dim, keepdims=False)
    send = lax.index_in_dim(value, 1, dim, keepdims=False)
    with jax.named_scope(name):
        other = swapped(send.astype(BF16), axis, bit)
    return keep.astype(F32) + other.astype(F32)


def sum_filters(total, name):
    each, mine, inputs = total.shape[-3:]
    highs = list(range(1, bits("space")))
    cut = (each + 1) // 2
    one, two = total[..., :cut, :, :], total[..., cut:, :, :]
    two = half_sum(two, "chan", 0, len(highs), f"{name}_x1")
    for bit in highs:
        one = half_sum(one, "space", bit, 0, f"{name}_y1")
    one = half_sum(one, "chan", 0, 0, f"{name}_x2")
    for bit in highs:
        two = half_sum(two, "space", bit, 0, f"{name}_y2")
    part = jnp.concatenate([one, two], axis=-3)
    for bit in far_bits():
        part = part.reshape((2, -1, each, mine, inputs))
        part = half_sum(part, "chan", bit, 0, f"{name}_z")
    part = part.reshape(each, mine, inputs).astype(BF16)
    for bit in high_bits():
        part = doubled(part, "space", bit, f"{name}_end")
    part = doubled(part, "space", 0, f"{name}_end")
    space = lax.axis_size("space")
    part = part.reshape(space, each, mine, inputs)
    places = jnp.arange(space) ^ lax.axis_index("space")
    taps = [lax.dynamic_index_in_dim(part, space_order(places[s]), 0, keepdims=False) for s in range(space)]
    full = jnp.concatenate(taps, axis=0)[:27].astype(F32)
    return jnp.transpose(full, (0, 2, 1)).reshape(3, 3, 3, inputs, mine)


def space_order(apart):
    place = 0
    for bit in range(bits("space")):
        place = place * 2 + ((apart >> bit) & 1)
    return place


def stepped_tile(tile, wide, base, store):
    depth, lanes = tile.shape
    for part in range(lanes // LANES):
        rows = wide.at[part]
        rows[pl.ds(base + depth, PAD), :] = jnp.zeros((PAD, LANES), F32)
        rows[pl.ds(base, depth), :] = tile[:, part * LANES : (part + 1) * LANES].astype(F32)
        store(part, rows[pl.ds(base + 1, depth), :].astype(BF16))


def back_kernel(orders, here, cells, filters, hidden, out, plane, row, wide, moved, spread):
    vols, wide_a, wide_b, depth, count = cells.shape
    side_a, side_b = wide_a - 1, wide_b - 1
    inputs = filters.shape[4]
    for n in range(vols):
        for a in range(wide_a):
            for b in range(wide_b):
                slot = ((n * wide_a + a) * wide_b + b) % 8 * (PAD + depth)

                def store(part, piece):
                    moved[n, a, b, :, part * LANES : (part + 1) * LANES] = piece

                stepped_tile(cells[n, a, b], wide, slot, store)

    def lefts(ref, da, db):
        return ref[:, da : da + side_a, db : db + side_b].reshape(-1, count)

    for sa in range(2):
        for sb in range(2):
            even = odd = None
            for i, da in REACH[sa]:
                for j, db in REACH[sb]:
                    tap = (i * 3 + j) * 3
                    here_cells = lefts(cells, da, db)
                    first = dot(here_cells, filter_tap(filters, here, tap + 1, orders), NN)
                    second = dot(here_cells, filter_tap(filters, here, tap + 2, orders), NN)
                    second += dot(lefts(moved, da, db), filter_tap(filters, here, tap, orders), NN)
                    even = first if even is None else even + first
                    odd = second if odd is None else odd + second
            for parity, value in enumerate((even, odd)):
                value = value.reshape(vols, side_a, side_b, depth, inputs)
                for n in range(vols):
                    for a in range(side_a):
                        for b in range(side_b):
                            for part in range(inputs // LANES):
                                spread[
                                    part, n, 2 * a + sa, 2 * b + sb, pl.ds(parity, depth, stride=2), :
                                ] = value[n, a, b, :, part * LANES : (part + 1) * LANES]
    for part in range(inputs // LANES):
        lanes = slice(part * LANES, (part + 1) * LANES)
        act = hidden[:, :, :, :, lanes].astype(F32)
        value = (spread[part] * jnp.where(act > 0, 1.0, 0.3)).astype(BF16)
        out[:, :, :, :, lanes] = value
        plane[:, :, :, :, lanes] = value[:, :1]
        row[:, :, :, :, lanes] = value[:, :, :1]


def hidden_back(here, cells, filters, hidden, orders):
    vols, wide_a, wide_b, depth, count = cells.shape
    inputs = hidden.shape[-1]
    shape = hidden.shape
    outs = [
        jax.ShapeDtypeStruct(shape, BF16),
        jax.ShapeDtypeStruct((vols, 1) + shape[2:], BF16),
        jax.ShapeDtypeStruct(shape[:2] + (1,) + shape[3:], BF16),
    ]
    return call(
        functools.partial(back_kernel, orders),
        outs,
        (here, cells, filters, hidden),
        [
            pltpu.VMEM((count // LANES, 8 * (PAD + depth), LANES), F32),
            pltpu.VMEM(cells.shape, BF16),
            pltpu.VMEM((inputs // LANES,) + shape[:4] + (LANES,), F32),
        ],
        flops=2 * vols * (wide_a - 1) * (wide_b - 1) * depth * 27 * inputs * count,
    )


def volume_kernel(orders, here, cells, plane, row, filters, out, wide, ext, moved, spread):
    _, side_a, side_b, depth, count = cells.shape
    inputs = filters.shape[4]
    for a in range(side_a + 1):
        for b in range(side_b + 1):
            if b == side_b:
                tile = row[0, a, 0]
            elif a == side_a:
                tile = plane[0, 0, b]
            else:
                tile = cells[0, a, b]
            ext[a, b] = tile
            slot = ((a * (side_b + 1) + b) % 8) * (PAD + depth)

            def store(part, piece):
                moved[a, b, :, part * LANES : (part + 1) * LANES] = piece

            stepped_tile(tile, wide, slot, store)

    def lefts(ref, da, db):
        return ref[da : da + side_a, db : db + side_b].reshape(-1, count)

    for sa in range(2):
        for sb in range(2):
            both = late = None
            for i, da in REACH[sa]:
                for j, db in REACH[sb]:
                    tap = (i * 3 + j) * 3
                    pair = jnp.concatenate(
                        [filter_tap(filters, here, tap + k, orders) for k in (1, 2)], axis=1
                    )
                    first = dot(lefts(ext, da, db), pair, NN)
                    second = dot(lefts(moved, da, db), filter_tap(filters, here, tap, orders), NN)
                    both = first if both is None else both + first
                    late = second if late is None else late + second
            halves = (both[:, :inputs], both[:, inputs:] + late)
            for parity, value in enumerate(halves):
                value = value.reshape(side_a, side_b, depth, inputs)
                for a in range(side_a):
                    for b in range(side_b):
                        spread[2 * a + sa, 2 * b + sb, pl.ds(parity, depth, stride=2), :] = value[a, b]
    out[0] = spread[...].astype(BF16)


def volume_grads(here, cells, plane, row, filters, orders):
    vols, side_a, side_b, depth, count = cells.shape
    inputs = filters.shape[4]
    out = jax.ShapeDtypeStruct((vols, 2 * side_a, 2 * side_b, 2 * depth, inputs), BF16)

    def block(shape):
        return pl.BlockSpec((1,) + shape[1:], lambda n: (n, 0, 0, 0, 0))

    return call(
        functools.partial(volume_kernel, orders),
        [out],
        (here, cells, plane, row, filters),
        [
            pltpu.VMEM((count // LANES, 8 * (PAD + depth), LANES), F32),
            pltpu.VMEM((side_a + 1, side_b + 1, depth, count), BF16),
            pltpu.VMEM((side_a + 1, side_b + 1, depth, count), BF16),
            pltpu.VMEM((2 * side_a, 2 * side_b, 2 * depth, inputs), F32),
        ],
        (vols,),
        [
            pl.BlockSpec(memory_space=pltpu.SMEM),
            block(cells.shape),
            block(plane.shape),
            block(row.shape),
            pl.BlockSpec(memory_space=pltpu.VMEM),
        ],
        [block(out.shape)],
        flops=2 * vols * side_a * side_b * depth * 27 * inputs * count,
    )[0]


class CellExchange:
    def __init__(self, cotangent):
        vols, side_a, side_b, side_c, mine = cotangent.shape
        self.count = bits("chan")
        self.tail = (side_b // 2**self.count, vols, side_a, side_c, mine)
        flat = cotangent.reshape(vols, side_a, side_b, side_c * mine)
        flat = jnp.transpose(flat, (2, 0, 1, 3))
        self.value = flat.reshape((2,) * self.count + (-1,) + flat.shape[1:])

    def stage(self, step):
        bit = self.count - 1 - step
        mine = (lax.axis_index("chan") >> bit) & 1
        keep = lax.dynamic_index_in_dim(self.value, mine, 0, keepdims=False)
        send = lax.dynamic_index_in_dim(self.value, 1 - mine, 0, keepdims=False)
        with jax.named_scope("cells"):
            other = swapped(send, "chan", bit)
        low, high = jnp.where(mine == 1, other, keep), jnp.where(mine == 1, keep, other)
        self.value = jnp.stack([low, high], axis=self.count - 1)

    def finish(self):
        rows, vols, side_a, side_c, mine = self.tail
        chan = 2**self.count
        value = self.value.reshape((chan, rows, vols, side_a, side_c, mine))
        value = jnp.transpose(value, (2, 3, 1, 4, 0, 5))
        own = value.reshape(vols, side_a, rows, side_c, chan * mine)
        with jax.named_scope("cells_row"):
            row = shifted(own[:, :, :1], (0, -1))
        near = jnp.concatenate([own, row], axis=2)
        with jax.named_scope("cells_plane"):
            plane = shifted(near[:, :1], (-1, 0))
        return own, jnp.concatenate([near, plane], axis=1)


def local(volume, w_first, w_second, cotangent):
    here = position()
    far = list(range(1, bits("chan")))
    gathered = (list(range(bits("space"))), [0] + far)
    summed = (list(range(bits("space"))), [0] + far[::-1])
    cells = CellExchange(cotangent)
    with jax.named_scope("plane"):
        plane = shifted(volume[:, -1:], (1, 0))
    part = own_part(w_first)
    for step, bit in enumerate(far_bits() + [0]):
        part = doubled(part, "chan", bit, "first_zx")
        cells.stage(step)
    row = jnp.concatenate([plane, volume], axis=1)[:, :, -1:]
    with jax.named_scope("row"):
        row = shifted(after(row, part), (0, 1))
    first_full = finish_gather(part, "first")
    second_full = mixed_gather(after(own_part(w_second), part), "second")
    grad_cells, grad_ext = cells.finish()
    vol_parts = parted(volume, plane, row)
    hidden, hid_plane, hid_row = forward(here, vol_parts, first_full, gathered, True)
    with jax.named_scope("hidden_halo"):
        row = shifted(hid_row, (0, 1))
        plane = shifted(hid_plane, (1, 0))
        corner = shifted(hid_row[:, -1:], (1, 1))
    act_parts = parted(hidden, plane, jnp.concatenate([corner, row], axis=1))
    second_terms = core_sum(*filter_grads(here, act_parts, grad_cells, summed), "sum_second")
    second_grad = sum_filters(second_terms, "sum_second")
    grad_ext = after(grad_ext, second_terms)
    pre_back, pre_plane, pre_row = hidden_back(here, grad_ext, second_full, hidden, gathered)
    first_terms = core_sum(*filter_grads(here, vol_parts, pre_back, summed), "sum_first")
    first_grad = sum_filters(first_terms, "sum_first")
    with jax.named_scope("back_plane"):
        plane = shifted(pre_plane, (-1, 0))
    with jax.named_scope("back_row"):
        row = shifted(jnp.concatenate([pre_row, plane[:, :, :1]], axis=1), (0, -1))
    local_out = forward(here, after(act_parts, first_terms), second_full, gathered, False)[0]
    with jax.named_scope("out"):
        second_out = lax.all_to_all(local_out, "chan", split_axis=4, concat_axis=2, tiled=True)
    volume_grad = volume_grads(here, pre_back, plane, row, first_full, gathered)
    return (second_out, volume_grad, first_grad, second_grad)


def solution(mesh):
    return jax.shard_map(
        local,
        mesh=mesh,
        in_specs=(
            P(None, "space", "chan", None, None),
            P(None, None, None, None, "chan"),
            P(None, None, None, None, "chan"),
            P(None, "space", None, None, "chan"),
        ),
        out_specs=(
            P(None, "space", None, None, "chan"),
            P(None, "space", "chan", None, None),
            P(None, None, None, None, "chan"),
            P(None, None, None, None, "chan"),
        ),
        check_vma=False,
    )
```

```python
import functools

import jax
import jax.numpy as jnp
from jax import lax
from jax.experimental import pallas as pl
from jax.experimental.pallas import tpu as pltpu
from jax.sharding import PartitionSpec as P


BF16 = jnp.bfloat16
F32 = jnp.float32
LANES = 128
PAD = 8
NT = (((1,), (1,)), ((), ()))
NN = (((1,), (0,)), ((), ()))
REACH = (((1, 0),), ((0, 1), (2, 0)))


def dot(left, right, dims):
    return lax.dot_general(left, right, dims, preferred_element_type=F32)


def bits(axis):
    return lax.axis_size(axis).bit_length() - 1


def shifted(value, steps):
    pairs = []
    sizes = (lax.axis_size("space"), lax.axis_size("chan"))
    for a in range(sizes[0]):
        for b in range(sizes[1]):
            to = (a + steps[0], b + steps[1])
            if 0 <= to[0] < sizes[0] and 0 <= to[1] < sizes[1]:
                pairs.append((a * sizes[1] + b, to[0] * sizes[1] + to[1]))
    return lax.ppermute(value, ("space", "chan"), pairs)


def swapped(value, axis, bit):
    count = lax.axis_size(axis)
    return lax.ppermute(value, axis, [(i, i ^ (1 << bit)) for i in range(count)])


def doubled(value, axis, bit):
    other = swapped(value, axis, bit)
    return jnp.stack([value, other])


def position():
    return jnp.stack([lax.axis_index("space"), lax.axis_index("chan")]).astype(jnp.int32)


def own_part(shard):
    space = lax.axis_size("space")
    edge, inputs, mine = shard.shape[0], shard.shape[3], shard.shape[4]
    taps = edge**3
    each = -(-taps // space)
    flat = jnp.transpose(shard.reshape(taps, inputs, mine), (0, 2, 1))
    flat = jnp.pad(flat, ((0, each * space - taps), (0, 0), (0, 0)))
    return lax.dynamic_slice_in_dim(flat, lax.axis_index("space") * each, each, 0)


def far_bits():
    return list(reversed(range(1, bits("chan"))))


def high_bits():
    return list(reversed(range(1, bits("space"))))


def mixed_gather(part):
    each, mine, inputs = part.shape
    for bit in far_bits():
        part = doubled(part, "chan", bit)
    highs = len(high_bits())
    cut = (each + 1) // 2
    one, two = part[..., :cut, :, :], part[..., cut:, :, :]
    one = doubled(one, "chan", 0)
    for bit in high_bits():
        two = doubled(two, "space", bit)
    for bit in high_bits():
        one = doubled(one, "space", bit)
    two = doubled(two, "chan", 0)
    one = doubled(one, "space", 0)
    two = doubled(two, "space", 0)
    two = jnp.moveaxis(two, 1, 1 + highs)
    whole = jnp.concatenate([one, two], axis=-3)
    return whole.reshape(lax.axis_size("space"), lax.axis_size("chan"), each, mine, inputs)


def relative(index, mine, order):
    apart = index ^ mine
    place = 0
    for bit in order:
        place = place * 2 + ((apart >> bit) & 1)
    return place


def filter_tap(ref, here, tap, orders):
    each = ref.shape[2]
    owner = relative(tap // each, here[0], orders[0])
    rows = [
        ref[owner, relative(chan, here[1], orders[1]), tap % each]
        for chan in range(ref.shape[1])
    ]
    return jnp.concatenate(rows, axis=0)


def call(kernel, outs, args, scratch=(), grid=None, in_specs=None, out_specs=None, flops=0):
    moved = sum(a.size * a.dtype.itemsize for a in args)
    moved += sum(o.size * o.dtype.itemsize for o in outs)
    whole = pl.BlockSpec(memory_space=pltpu.VMEM)
    smem = pl.BlockSpec(memory_space=pltpu.SMEM)
    specs = in_specs or [smem if a.dtype == jnp.int32 else whole for a in args]
    return pl.pallas_call(
        kernel,
        out_shape=outs,
        grid=grid or (),
        in_specs=specs,
        out_specs=out_specs or [whole] * len(outs),
        scratch_shapes=scratch,
        cost_estimate=pl.CostEstimate(flops=flops, bytes_accessed=moved, transcendentals=0),
        compiler_params=pltpu.CompilerParams(vmem_limit_bytes=56 * 2**20),
    )(*args)


def parted_tile(tile, wide, base, store):
    depth, lanes = tile.shape
    for part in range(lanes // LANES):
        rows = wide.at[part]
        rows[pl.ds(base, PAD), :] = jnp.zeros((PAD, LANES), F32)
        rows[pl.ds(base + PAD, depth), :] = tile[:, part * LANES : (part + 1) * LANES].astype(F32)
        for k in range(3):
            piece = rows[pl.ds(base + PAD - 1 + k, depth // 2, stride=2), :]
            store(k, part, piece.astype(BF16))


def part_kernel(pick, shape, wide, out_of):
    wide_a, wide_b, depth = shape
    for a in range(wide_a):
        for b in range(wide_b):
            slot = ((a * wide_b + b) % 8) * (PAD + depth)

            def store(k, part, piece):
                out_of[k, 0, a, b, :, part * LANES : (part + 1) * LANES] = piece

            parted_tile(pick(a, b), wide, slot, store)


def parted(blocks, shape, picker):
    vols, wide_a, wide_b, depth, lanes = shape
    out = jax.ShapeDtypeStruct((3, vols, wide_a, wide_b, depth // 2, lanes), BF16)

    def kernel(*refs):
        *ins, out_ref, wide = refs
        part_kernel(picker(ins), (wide_a, wide_b, depth), wide, out_ref)

    def block(shape):
        return pl.BlockSpec((1,) + shape[1:], lambda n: (n, 0, 0, 0, 0))

    return call(
        kernel,
        [out],
        blocks,
        [pltpu.VMEM((lanes // LANES, 8 * (PAD + depth), LANES), F32)],
        (vols,),
        [block(b.shape) for b in blocks],
        [pl.BlockSpec((3, 1) + out.shape[2:], lambda n: (0, n, 0, 0, 0, 0))],
    )[0]


def window(refs, i, j, sides):
    vols, side_a, cells_b = sides
    rows = []
    for n in range(vols):
        for a in range(side_a):
            for b in cells_b:
                y = 2 * b + j
                ref = refs[0]
                if len(refs) == 2:
                    ref, y = (refs[1], 0) if y == 0 else (refs[0], y - 1)
                assert 0 <= y < ref.shape[3]
                rows.append(jnp.concatenate([ref[k, n, 2 * a + i, y] for k in range(3)], axis=1))
    return jnp.concatenate(rows, axis=0)


def forward_kernel(orders, sides, act, split, here, filters, *rest):
    *refs, out, acc = rest
    if split and len(refs) == 1:
        refs.append(None)
    acc[...] = jnp.zeros_like(acc)

    def step(i, carry):
        for j in range(3):
            right = jnp.concatenate(
                [filter_tap(filters, here, i * 9 + j * 3 + k, orders) for k in range(3)], axis=1
            )
            acc[...] += dot(window(refs, i, j, sides), right, NT)
        return carry

    lax.fori_loop(0, 3, step, 0)
    total = acc[...]
    if act:
        total = jnp.where(total > 0, total, 0.3 * total)
    out[...] = total.astype(BF16).reshape(out.shape)


def forward(here, refs, filters, orders, cells_b, act):
    _, vols, wide_a, _, depth, inputs = refs[0].shape
    sides = (vols, (wide_a - 1) // 2, cells_b)
    count = filters.shape[1] * filters.shape[3]
    cells = vols * sides[1] * len(cells_b) * depth
    out = jax.ShapeDtypeStruct((vols, sides[1], len(cells_b), depth, count), BF16)
    return call(
        functools.partial(forward_kernel, orders, sides, act, len(refs) == 2),
        [out],
        (here, filters, *(r for r in refs if r is not None)),
        [pltpu.VMEM((cells, count), F32)],
        flops=2 * cells * 27 * inputs * count,
    )[0]


def grads_kernel(orders, sides, here, grads, *rest):
    *refs, keep, send, turned = rest
    cells, count = turned.shape[1], turned.shape[0]
    inputs = refs[0].shape[5]
    chans = 2 ** len(orders[1])
    mine = count // chans
    each = keep.shape[2]
    half = keep.shape[0]
    turned[...] = jnp.transpose(grads[...].reshape(cells, count).astype(F32), (1, 0)).astype(BF16)

    def put(ref, place, tap, part):
        for chan in range(chans):
            to = relative(chan, here[1], orders[1])
            ref[place, to, tap % each] = part[chan * mine : (chan + 1) * mine]

    def step(i, carry):
        for j in range(3):
            part = dot(turned[...], window(refs, i, j, sides), NN).astype(BF16)
            for k in range(3):
                tap = i * 9 + j * 3 + k
                place = relative(tap // each, here[0], orders[0])
                piece = part[:, k * inputs : (k + 1) * inputs]

                @pl.when(place < half)
                def _():
                    put(keep, place, tap, piece)

                @pl.when(place >= half)
                def _():
                    put(send, place - half, tap, piece)

        return carry

    lax.fori_loop(0, 3, step, 0)
    for tap in range(27, each * 2 * half):
        place = relative(tap // each, here[0], orders[0])
        blank = jnp.zeros((chans, mine, inputs), BF16)

        @pl.when(place < half)
        def _():
            keep[place, :, tap % each] = blank

        @pl.when(place >= half)
        def _():
            send[place - half, :, tap % each] = blank


def filter_grads(here, refs, grads, orders):
    inputs = refs[0].shape[5]
    vols, side_a, side_b, depth, count = grads.shape
    sides = (vols, side_a, range(side_b))
    cells = vols * side_a * side_b * depth
    space, chans = 2 ** len(orders[0]), 2 ** len(orders[1])
    each = -(-27 // space)
    out = jax.ShapeDtypeStruct((space // 2, chans, each, count // chans, inputs), BF16)
    return call(
        functools.partial(grads_kernel, orders, sides),
        [out, out],
        (here, grads, *refs),
        [pltpu.VMEM((count, cells), BF16)],
        flops=2 * cells * 27 * inputs * count,
    )


def core_sum(keep, send):
    tail = keep.shape[2:]
    other = swapped(send, "space", 0)
    total = keep.astype(F32) + other.astype(F32)
    highs = bits("space") - 1
    return total.reshape((2,) * highs + (2, -1) + tail)


def half_sum(value, axis, bit, dim):
    keep = lax.index_in_dim(value, 0, dim, keepdims=False)
    send = lax.index_in_dim(value, 1, dim, keepdims=False)
    other = swapped(send.astype(BF16), axis, bit)
    return keep.astype(F32) + other.astype(F32)


def sum_filters(total):
    each, mine, inputs = total.shape[-3:]
    highs = list(range(1, bits("space")))
    cut = (each + 1) // 2
    one, two = total[..., :cut, :, :], total[..., cut:, :, :]
    two = half_sum(two, "chan", 0, len(highs))
    for bit in highs:
        one = half_sum(one, "space", bit, 0)
    one = half_sum(one, "chan", 0, 0)
    for bit in highs:
        two = half_sum(two, "space", bit, 0)
    part = jnp.concatenate([one, two], axis=-3)
    for bit in far_bits():
        part = part.reshape((2, -1, each, mine, inputs))
        part = half_sum(part, "chan", bit, 0)
    part = part.reshape(each, mine, inputs).astype(BF16)
    for bit in high_bits():
        part = doubled(part, "space", bit)
    part = doubled(part, "space", 0)
    space = lax.axis_size("space")
    part = part.reshape(space, each, mine, inputs)
    places = jnp.arange(space) ^ lax.axis_index("space")
    taps = [lax.dynamic_index_in_dim(part, space_order(places[s]), 0, keepdims=False) for s in range(space)]
    full = jnp.concatenate(taps, axis=0)[:27].astype(F32)
    return jnp.transpose(full, (0, 2, 1)).reshape(3, 3, 3, inputs, mine)


def space_order(apart):
    place = 0
    for bit in range(bits("space")):
        place = place * 2 + ((apart >> bit) & 1)
    return place


def stepped_tile(tile, wide, base, store):
    depth, lanes = tile.shape
    for part in range(lanes // LANES):
        rows = wide.at[part]
        rows[pl.ds(base + depth, PAD), :] = jnp.zeros((PAD, LANES), F32)
        rows[pl.ds(base, depth), :] = tile[:, part * LANES : (part + 1) * LANES].astype(F32)
        store(part, rows[pl.ds(base + 1, depth), :].astype(BF16))


def back_kernel(orders, here, cells, filters, low, high, out, plane, row, wide, moved, spread):
    vols, wide_a, wide_b, depth, count = cells.shape
    side_a, side_b = wide_a - 1, wide_b - 1
    inputs = filters.shape[4]
    for n in range(vols):
        for a in range(wide_a):
            for b in range(wide_b):
                slot = ((n * wide_a + a) * wide_b + b) % 8 * (PAD + depth)

                def store(part, piece):
                    moved[n, a, b, :, part * LANES : (part + 1) * LANES] = piece

                stepped_tile(cells[n, a, b], wide, slot, store)

    def lefts(ref, da, db):
        return ref[:, da : da + side_a, db : db + side_b].reshape(-1, count)

    for sa in range(2):
        for sb in range(2):
            even = odd = None
            for i, da in REACH[sa]:
                for j, db in REACH[sb]:
                    tap = (i * 3 + j) * 3
                    here_cells = lefts(cells, da, db)
                    first = dot(here_cells, filter_tap(filters, here, tap + 1, orders), NN)
                    second = dot(here_cells, filter_tap(filters, here, tap + 2, orders), NN)
                    second += dot(lefts(moved, da, db), filter_tap(filters, here, tap, orders), NN)
                    even = first if even is None else even + first
                    odd = second if odd is None else odd + second
            for parity, value in enumerate((even, odd)):
                value = value.reshape(vols, side_a, side_b, depth, inputs)
                for n in range(vols):
                    for a in range(side_a):
                        for b in range(side_b):
                            for part in range(inputs // LANES):
                                spread[
                                    part, n, 2 * a + sa, 2 * b + sb, pl.ds(parity, depth, stride=2), :
                                ] = value[n, a, b, :, part * LANES : (part + 1) * LANES]
    for part in range(inputs // LANES):
        lanes = slice(part * LANES, (part + 1) * LANES)
        act = jnp.concatenate([low[:, :, :, :, lanes], high[:, :, :, :, lanes]], axis=2)
        act = act.astype(F32)
        value = (spread[part] * jnp.where(act > 0, 1.0, 0.3)).astype(BF16)
        out[:, :, :, :, lanes] = value
        plane[:, :, :, :, lanes] = value[:, :1]
        row[:, :, :, :, lanes] = value[:, :, :1]


def hidden_back(here, cells, filters, low, high, orders):
    vols, wide_a, wide_b, depth, count = cells.shape
    inputs = low.shape[-1]
    shape = low.shape[:2] + (low.shape[2] + high.shape[2],) + low.shape[3:]
    outs = [
        jax.ShapeDtypeStruct(shape, BF16),
        jax.ShapeDtypeStruct((vols, 1) + shape[2:], BF16),
        jax.ShapeDtypeStruct(shape[:2] + (1,) + shape[3:], BF16),
    ]
    return call(
        functools.partial(back_kernel, orders),
        outs,
        (here, cells, filters, low, high),
        [
            pltpu.VMEM((count // LANES, 8 * (PAD + depth), LANES), F32),
            pltpu.VMEM(cells.shape, BF16),
            pltpu.VMEM((inputs // LANES,) + shape[:4] + (LANES,), F32),
        ],
        flops=2 * vols * (wide_a - 1) * (wide_b - 1) * depth * 27 * inputs * count,
    )


def volume_kernel(orders, here, cells, plane, row, filters, out, wide, ext, moved, spread):
    _, side_a, side_b, depth, count = cells.shape
    inputs = filters.shape[4]
    for a in range(side_a + 1):
        for b in range(side_b + 1):
            if b == side_b:
                tile = row[0, a, 0]
            elif a == side_a:
                tile = plane[0, 0, b]
            else:
                tile = cells[0, a, b]
            ext[a, b] = tile
            slot = ((a * (side_b + 1) + b) % 8) * (PAD + depth)

            def store(part, piece):
                moved[a, b, :, part * LANES : (part + 1) * LANES] = piece

            stepped_tile(tile, wide, slot, store)

    def lefts(ref, da, db):
        return ref[da : da + side_a, db : db + side_b].reshape(-1, count)

    for sa in range(2):
        for sb in range(2):
            both = late = None
            for i, da in REACH[sa]:
                for j, db in REACH[sb]:
                    tap = (i * 3 + j) * 3
                    pair = jnp.concatenate(
                        [filter_tap(filters, here, tap + k, orders) for k in (1, 2)], axis=1
                    )
                    first = dot(lefts(ext, da, db), pair, NN)
                    second = dot(lefts(moved, da, db), filter_tap(filters, here, tap, orders), NN)
                    both = first if both is None else both + first
                    late = second if late is None else late + second
            halves = (both[:, :inputs], both[:, inputs:] + late)
            for parity, value in enumerate(halves):
                value = value.reshape(side_a, side_b, depth, inputs)
                for a in range(side_a):
                    for b in range(side_b):
                        spread[2 * a + sa, 2 * b + sb, pl.ds(parity, depth, stride=2), :] = value[a, b]
    out[0] = spread[...].astype(BF16)


def volume_grads(here, cells, plane, row, filters, orders):
    vols, side_a, side_b, depth, count = cells.shape
    inputs = filters.shape[4]
    out = jax.ShapeDtypeStruct((vols, 2 * side_a, 2 * side_b, 2 * depth, inputs), BF16)

    def block(shape):
        return pl.BlockSpec((1,) + shape[1:], lambda n: (n, 0, 0, 0, 0))

    return call(
        functools.partial(volume_kernel, orders),
        [out],
        (here, cells, plane, row, filters),
        [
            pltpu.VMEM((count // LANES, 8 * (PAD + depth), LANES), F32),
            pltpu.VMEM((side_a + 1, side_b + 1, depth, count), BF16),
            pltpu.VMEM((side_a + 1, side_b + 1, depth, count), BF16),
            pltpu.VMEM((2 * side_a, 2 * side_b, 2 * depth, inputs), F32),
        ],
        (vols,),
        [
            pl.BlockSpec(memory_space=pltpu.SMEM),
            block(cells.shape),
            block(plane.shape),
            block(row.shape),
            pl.BlockSpec(memory_space=pltpu.VMEM),
        ],
        [block(out.shape)],
        flops=2 * vols * side_a * side_b * depth * 27 * inputs * count,
    )[0]


class CellExchange:
    def __init__(self, cotangent):
        vols, side_a, side_b, side_c, mine = cotangent.shape
        self.count = bits("chan")
        self.tail = (side_b // 2**self.count, vols, side_a, side_c, mine)
        flat = cotangent.reshape(vols, side_a, side_b, side_c * mine)
        flat = jnp.transpose(flat, (2, 0, 1, 3))
        self.value = flat.reshape((2,) * self.count + (-1,) + flat.shape[1:])
        self.open = list(reversed(range(self.count)))
        self.done = []

    def stage(self, bit):
        dim = self.open.index(bit)
        mine = (lax.axis_index("chan") >> bit) & 1
        keep = lax.dynamic_index_in_dim(self.value, mine, dim, keepdims=False)
        send = lax.dynamic_index_in_dim(self.value, 1 - mine, dim, keepdims=False)
        other = swapped(send, "chan", bit)
        low, high = jnp.where(mine == 1, other, keep), jnp.where(mine == 1, keep, other)
        self.value = jnp.stack([low, high], axis=self.count - 1)
        self.open.remove(bit)
        self.done.append(bit)

    def finish(self):
        rows, vols, side_a, side_c, mine = self.tail
        count = self.count
        value = self.value.reshape((2,) * count + (rows, vols, side_a, side_c, mine))
        sources = [self.done.index(bit) for bit in reversed(range(count))]
        value = jnp.transpose(
            value, (count + 1, count + 2, count, count + 3, *sources, count + 4)
        )
        own = value.reshape(vols, side_a, rows, side_c, 2**count * mine)
        row = shifted(own[:, :, :1], (0, -1))
        near = jnp.concatenate([own, row], axis=2)
        plane = shifted(near[:, :1], (-1, 0))
        return own, jnp.concatenate([near, plane], axis=1)


def volume_picker(refs):
    own, plane = refs
    return lambda a, b: plane[0, 0, b] if a == 0 else own[0, a - 1, b]


def row_picker(refs):
    return lambda a, b: refs[0][0, a, 0]


def hidden_picker(refs):
    low, high, plane, row, corner = refs

    def pick(a, b):
        if b == 0:
            return corner[0, 0, 0] if a == 0 else row[0, a - 1, 0]
        if a == 0:
            return plane[0, 0, b - 1]
        return low[0, a - 1, 0] if b == 1 else high[0, a - 1, b - 2]

    return pick


def local(volume, w_first, w_second, cotangent):
    here = position()
    far = list(range(1, bits("chan")))
    gathered = (list(range(bits("space"))), [0] + far)
    summed = (list(range(bits("space"))), [0] + far[::-1])
    vols, side_x, side_y, depth, inputs = volume.shape
    side_b = side_y // 2

    cells = CellExchange(cotangent)
    plane = shifted(volume[:, -1:], (1, 0))
    part = own_part(w_first)
    for bit in far_bits():
        part = doubled(part, "chan", bit)
    part = doubled(part, "chan", 0)
    for bit in high_bits():
        part = doubled(part, "space", bit)
    part = doubled(part, "space", 0)
    first_full = part.reshape(lax.axis_size("space"), lax.axis_size("chan"), *part.shape[-3:])
    for bit in [0] + far_bits():
        cells.stage(bit)
    grad_cells, grad_ext = cells.finish()
    row = jnp.concatenate([plane, volume], axis=1)[:, :, -1:]
    row = shifted(row, (0, 1))
    second_full = mixed_gather(own_part(w_second))

    wide = (vols, side_x + 1, side_y, depth, inputs)
    vol_main = parted((volume, plane), wide, volume_picker)
    high = forward(here, (vol_main, None), first_full, gathered, range(1, side_b), True)
    hid_row = shifted(high[:, :, -1:], (0, 1))
    hid_corner = shifted(high[:, -1:, -1:], (1, 1))
    vol_row = parted((row,), wide[:2] + (1, depth, inputs), row_picker)
    vol_parts = (vol_main, vol_row)
    low = forward(here, vol_parts, first_full, gathered, range(1), True)
    hid_plane = jnp.concatenate([low[:, -1:], high[:, -1:]], axis=2)
    hid_plane = shifted(hid_plane, (1, 0))
    shape = (vols, side_x // 2 + 1, side_b + 1) + low.shape[3:]
    act_blocks = (low, high, hid_plane, hid_row, hid_corner)
    act_parts = (parted(act_blocks, shape, hidden_picker),)
    second_terms = core_sum(*filter_grads(here, act_parts, grad_cells, summed))
    second_grad = sum_filters(second_terms)

    pre_back, pre_plane, pre_row = hidden_back(here, grad_ext, second_full, low, high, gathered)
    first_terms = core_sum(*filter_grads(here, vol_parts, pre_back, summed))
    first_grad = sum_filters(first_terms)
    plane = shifted(pre_plane, (-1, 0))
    row = jnp.concatenate([pre_row, plane[:, :, :1]], axis=1)
    row = shifted(row, (0, -1))
    out_b = (shape[2] - 1) // 2
    local_out = forward(here, act_parts, second_full, gathered, range(out_b), False)
    second_out = lax.all_to_all(local_out, "chan", split_axis=4, concat_axis=2, tiled=True)
    volume_grad = volume_grads(here, pre_back, plane, row, first_full, gathered)
    return (second_out, volume_grad, first_grad, second_grad)


def solution(mesh):
    return jax.shard_map(
        local,
        mesh=mesh,
        in_specs=(
            P(None, "space", "chan", None, None),
            P(None, None, None, None, "chan"),
            P(None, None, None, None, "chan"),
            P(None, "space", None, None, "chan"),
        ),
        out_specs=(
            P(None, "space", None, None, "chan"),
            P(None, "space", "chan", None, None),
            P(None, None, None, None, "chan"),
            P(None, None, None, None, "chan"),
        ),
        check_vma=False,
    )
```

```python
import functools

import jax
import jax.numpy as jnp
from jax import lax
from jax.experimental import pallas as pl
from jax.experimental.pallas import tpu as pltpu
from jax.sharding import PartitionSpec as P


BF16 = jnp.bfloat16
F32 = jnp.float32
LANES = 128
PAD = 8
NT = (((1,), (1,)), ((), ()))
NN = (((1,), (0,)), ((), ()))
REACH = (((1, 0),), ((0, 1), (2, 0)))


def dot(left, right, dims):
    return lax.dot_general(left, right, dims, preferred_element_type=F32)


def bits(axis):
    return lax.axis_size(axis).bit_length() - 1


def shifted(value, steps):
    pairs = []
    sizes = (lax.axis_size("space"), lax.axis_size("chan"))
    for a in range(sizes[0]):
        for b in range(sizes[1]):
            to = (a + steps[0], b + steps[1])
            if 0 <= to[0] < sizes[0] and 0 <= to[1] < sizes[1]:
                pairs.append((a * sizes[1] + b, to[0] * sizes[1] + to[1]))
    return lax.ppermute(value, ("space", "chan"), pairs)


def swapped(value, axis, bit):
    count = lax.axis_size(axis)
    return lax.ppermute(value, axis, [(i, i ^ (1 << bit)) for i in range(count)])


def doubled(value, axis, bit):
    other = swapped(value, axis, bit)
    return jnp.stack([value, other])


def position():
    return jnp.stack([lax.axis_index("space"), lax.axis_index("chan")]).astype(jnp.int32)


def own_part(shard):
    space = lax.axis_size("space")
    edge, inputs, mine = shard.shape[0], shard.shape[3], shard.shape[4]
    taps = edge**3
    each = -(-taps // space)
    flat = jnp.transpose(shard.reshape(taps, inputs, mine), (0, 2, 1))
    flat = jnp.pad(flat, ((0, each * space - taps), (0, 0), (0, 0)))
    return lax.dynamic_slice_in_dim(flat, lax.axis_index("space") * each, each, 0)


def far_bits():
    return list(reversed(range(1, bits("chan"))))


def high_bits():
    return list(reversed(range(1, bits("space"))))


def far_swapped(value, mask):
    count = lax.axis_size("chan")
    return lax.ppermute(value, "chan", [(i, i ^ (mask << 1)) for i in range(count)])


def far_gather(part):
    others = [far_swapped(part, m) for m in range(1, lax.axis_size("chan") // 2)]
    return jnp.stack([part, *others])


def near_gather(part):
    each, mine, inputs = part.shape[-3:]
    for bit in high_bits():
        part = doubled(part, "space", bit)
    part = doubled(part, "space", 0)
    return part.reshape(lax.axis_size("space"), lax.axis_size("chan"), each, mine, inputs)


def relative(index, mine, order):
    apart = index ^ mine
    place = 0
    for bit in order:
        place = place * 2 + ((apart >> bit) & 1)
    return place


def filter_tap(ref, here, tap, orders):
    each = ref.shape[2]
    owner = relative(tap // each, here[0], orders[0])
    rows = [
        ref[owner, relative(chan, here[1], orders[1]), tap % each]
        for chan in range(ref.shape[1])
    ]
    return jnp.concatenate(rows, axis=0)


def scratch_avals(scratch):
    return [jax.ShapeDtypeStruct(ref.inner_aval.shape, ref.inner_aval.dtype) for ref in scratch]


def call(kernel, outs, args, scratch=(), grid=None, in_specs=None, out_specs=None, flops=0):
    moved = sum(a.size * a.dtype.itemsize for a in args)
    moved += sum(o.size * o.dtype.itemsize for o in outs)
    used = sum(v.size * v.dtype.itemsize for v in scratch_avals(scratch))
    grant = min(56 * 2**20, moved + used + 6 * 2**20)
    whole = pl.BlockSpec(memory_space=pltpu.VMEM)
    smem = pl.BlockSpec(memory_space=pltpu.SMEM)
    specs = in_specs or [smem if a.dtype == jnp.int32 else whole for a in args]
    return pl.pallas_call(
        kernel,
        out_shape=outs,
        grid=grid or (),
        in_specs=specs,
        out_specs=out_specs or [whole] * len(outs),
        scratch_shapes=scratch,
        cost_estimate=pl.CostEstimate(flops=flops, bytes_accessed=moved, transcendentals=0),
        compiler_params=pltpu.CompilerParams(vmem_limit_bytes=grant),
    )(*args)


def parted_tile(tile, wide, base, store):
    depth, lanes = tile.shape
    for part in range(lanes // LANES):
        rows = wide.at[part]
        rows[pl.ds(base, PAD), :] = jnp.zeros((PAD, LANES), F32)
        rows[pl.ds(base + PAD, depth), :] = tile[:, part * LANES : (part + 1) * LANES].astype(F32)
        for k in range(3):
            piece = rows[pl.ds(base + PAD - 1 + k, depth // 2, stride=2), :]
            store(k, part, piece.astype(BF16))


def part_block(pick, out, n, shape, wide):
    wide_a, wide_b, depth = shape
    for a in range(wide_a):
        for b in range(wide_b):
            slot = ((a * wide_b + b) % 8) * (PAD + depth)

            def store(k, part, piece):
                out[k, n, a, b, :, part * LANES : (part + 1) * LANES] = piece

            parted_tile(pick(a, b), wide, slot, store)


def part_scratch(depth, lanes):
    return pltpu.VMEM((lanes // LANES, 8 * (PAD + depth), LANES), F32)


def parted_volume(own, plane):
    vols, side_a, side_b, depth, lanes = own.shape
    out = jax.ShapeDtypeStruct((3, vols, side_a + 1, side_b, depth // 2, lanes), BF16)

    def kernel(own, plane, out, wide):
        def pick(a, b):
            return plane[0, 0, b] if a == 0 else own[0, a - 1, b]

        part_block(pick, out, 0, (side_a + 1, side_b, depth), wide)

    def block(shape):
        return pl.BlockSpec((1,) + shape[1:], lambda n: (n, 0, 0, 0, 0))

    return call(
        kernel,
        [out],
        (own, plane),
        [part_scratch(depth, lanes)],
        (vols,),
        [block(own.shape), block(plane.shape)],
        [pl.BlockSpec((3, 1) + out.shape[2:], lambda n: (0, n, 0, 0, 0, 0))],
    )[0]


def window(refs, i, j, sides):
    vols, side_a, cells_b = sides
    rows = []
    for n in range(vols):
        for a in range(side_a):
            for b in cells_b:
                y = 2 * b + j
                ref = refs[0]
                if len(refs) == 2:
                    ref, y = (refs[1], 0) if y == 0 else (refs[0], y - 1)
                assert 0 <= y < ref.shape[3]
                rows.append(jnp.concatenate([ref[k, n, 2 * a + i, y] for k in range(3)], axis=1))
    return jnp.concatenate(rows, axis=0)


def forward_total(orders, sides, refs, here, filters, acc):
    acc[...] = jnp.zeros_like(acc)

    def step(i, carry):
        for j in range(3):
            right = jnp.concatenate(
                [filter_tap(filters, here, i * 9 + j * 3 + k, orders) for k in range(3)], axis=1
            )
            acc[...] += dot(window(refs, i, j, sides), right, NT)
        return carry

    lax.fori_loop(0, 3, step, 0)
    return acc[...]


def leaky(total):
    return jnp.where(total > 0, total, 0.3 * total)


def forward(here, parts, filters, orders, cells_b, kind):
    main = parts[0]
    _, vols, wide_a, _, depth, inputs = main.shape
    sides = (vols, (wide_a - 1) // 2, cells_b)
    count = filters.shape[1] * filters.shape[3]
    cells = vols * sides[1] * len(cells_b) * depth
    outs = [jax.ShapeDtypeStruct((vols, sides[1], len(cells_b), depth, count), BF16)]
    scratch = [pltpu.VMEM((cells, count), F32)]
    if kind == "low":
        outs.append(jax.ShapeDtypeStruct(main.shape[:3] + (1,) + main.shape[4:], BF16))
        scratch.append(part_scratch(2 * depth, inputs))

    def kernel(here, filters, main, *rest):
        if kind == "low":
            row, out, row_parts, acc, wide = rest

            def split(n, carry):
                part_block(lambda a, b: row[n, a, 0], row_parts, n, (wide_a, 1, 2 * depth), wide)
                return carry

            lax.fori_loop(0, vols, split, 0)
            refs = (main, row_parts)
        else:
            out, acc = rest
            refs = (main, None) if kind == "high" else (main,)
        total = forward_total(orders, sides, refs, here, filters, acc)
        if kind != "out":
            total = leaky(total)
        out[...] = total.astype(BF16).reshape(out.shape)

    return call(
        kernel,
        outs,
        (here, filters, *parts),
        scratch,
        flops=2 * cells * 27 * inputs * count,
    )


def grads_body(orders, sides, here, grads, refs, keep, send, turned):
    cells, count = turned.shape[1], turned.shape[0]
    inputs = refs[0].shape[5]
    pieces = inputs // LANES
    chans = 2 ** len(orders[1])
    mine = count // chans
    each = keep.shape[2] // pieces
    half = keep.shape[0]
    turned[...] = jnp.transpose(grads[...].reshape(cells, count).astype(F32), (1, 0)).astype(BF16)

    def put(ref, place, tap, part):
        for chan in range(chans):
            to = relative(chan, here[1], orders[1])
            for piece in range(pieces):
                lanes = slice(piece * LANES, (piece + 1) * LANES)
                ref[place, to, (tap % each) * pieces + piece] = part[chan * mine : (chan + 1) * mine, lanes]

    def step(i, carry):
        for j in range(3):
            part = dot(turned[...], window(refs, i, j, sides), NN).astype(BF16)
            for k in range(3):
                tap = i * 9 + j * 3 + k
                place = relative(tap // each, here[0], orders[0])
                piece = part[:, k * inputs : (k + 1) * inputs]

                @pl.when(place < half)
                def _():
                    put(keep, place, tap, piece)

                @pl.when(place >= half)
                def _():
                    put(send, place - half, tap, piece)

        return carry

    lax.fori_loop(0, 3, step, 0)
    blank = jnp.zeros((count, inputs), BF16)
    for tap in range(27, each * 2 * half):
        place = relative(tap // each, here[0], orders[0])

        @pl.when(place < half)
        def _():
            put(keep, place, tap, blank)

        @pl.when(place >= half)
        def _():
            put(send, place - half, tap, blank)


def grads_out(count, inputs, orders):
    space, chans = 2 ** len(orders[0]), 2 ** len(orders[1])
    each = -(-27 // space) * (inputs // LANES)
    return jax.ShapeDtypeStruct((space // 2, chans, each, count // chans, LANES), BF16)


def first_grads(here, refs, grads, orders):
    inputs = refs[0].shape[5]
    vols, side_a, side_b, depth, count = grads.shape
    sides = (vols, side_a, range(side_b))
    cells = vols * side_a * side_b * depth
    out = grads_out(count, inputs, orders)

    def kernel(here, grads, main, row, keep, send, turned):
        grads_body(orders, sides, here, grads, (main, row), keep, send, turned)

    return call(
        kernel,
        [out, out],
        (here, grads, *refs),
        [pltpu.VMEM((count, cells), BF16)],
        flops=2 * cells * 27 * inputs * count,
    )


def second_grads(here, blocks, grads, orders):
    low, high = blocks[:2]
    side_x, deep, inputs = low.shape[1], low.shape[3], low.shape[4]
    wide_b = low.shape[2] + high.shape[2] + 1
    vols, side_a, side_b, depth, count = grads.shape
    sides = (vols, side_a, range(side_b))
    cells = vols * side_a * side_b * depth
    out = grads_out(count, inputs, orders)
    parts = jax.ShapeDtypeStruct((3, vols, side_x + 1, wide_b, depth, inputs), BF16)

    def kernel(here, grads, low, high, plane, row, corner, keep, send, parts, turned, wide):
        def split(n, carry):
            def pick(a, b):
                if b == 0:
                    return corner[n, 0, 0] if a == 0 else row[n, a - 1, 0]
                if a == 0:
                    return plane[n, 0, b - 1]
                return low[n, a - 1, 0] if b == 1 else high[n, a - 1, b - 2]

            part_block(pick, parts, n, (side_x + 1, wide_b, deep), wide)
            return carry

        lax.fori_loop(0, vols, split, 0)
        grads_body(orders, sides, here, grads, (parts,), keep, send, turned)

    return call(
        kernel,
        [out, out, parts],
        (here, grads, *blocks),
        [pltpu.VMEM((count, cells), BF16), part_scratch(deep, inputs)],
        flops=2 * cells * 27 * inputs * count,
    )


def core_sum(keep, send):
    tail = keep.shape[2:]
    other = swapped(send, "space", 0)
    total = keep.astype(F32) + other.astype(F32)
    highs = bits("space") - 1
    return total.reshape((2,) * highs + (2, -1) + tail)


def half_sum(value, axis, bit, dim):
    keep = lax.index_in_dim(value, 0, dim, keepdims=False)
    send = lax.index_in_dim(value, 1, dim, keepdims=False)
    other = swapped(send.astype(BF16), axis, bit)
    return keep.astype(F32) + other.astype(F32)


def plain_sum(total):
    for bit in range(1, bits("space")):
        total = half_sum(total, "space", bit, 0)
    return half_sum(total, "chan", 0, 0)


def mixed_sum(total):
    highs = list(range(1, bits("space")))
    cut = (total.shape[-3] + 1) // 2
    one, two = total[..., :cut, :, :], total[..., cut:, :, :]
    two = half_sum(two, "chan", 0, len(highs))
    for bit in highs:
        one = half_sum(one, "space", bit, 0)
    one = half_sum(one, "chan", 0, 0)
    for bit in highs:
        two = half_sum(two, "space", bit, 0)
    return jnp.concatenate([one, two], axis=-3)


def finish_sum(totals):
    count = lax.axis_size("chan") // 2
    space = lax.axis_size("space")
    merged = jnp.concatenate(totals, axis=1)
    part = merged[0].astype(F32)
    for m in range(1, count):
        part = part + far_swapped(merged[m].astype(BF16), m).astype(F32)
    part = part.astype(BF16)
    for bit in high_bits():
        part = doubled(part, "space", bit)
    part = doubled(part, "space", 0)
    part = part.reshape((space,) + merged.shape[1:])
    apart = [jnp.int32(s) ^ lax.axis_index("space") for s in range(space)]
    ordered = [lax.dynamic_index_in_dim(part, space_order(a), 0, keepdims=False) for a in apart]
    outs, begin = [], 0
    taps = -(-27 // space)
    for total in totals:
        rows, mine = total.shape[1], total.shape[2]
        pieces = rows // taps
        full = jnp.concatenate([o[begin : begin + rows] for o in ordered], axis=0)
        full = full.reshape(space * taps, pieces, mine, LANES)[:27].astype(F32)
        full = jnp.transpose(full, (0, 1, 3, 2)).reshape(3, 3, 3, pieces * LANES, mine)
        outs.append(full)
        begin += rows
    return outs


def space_order(apart):
    place = 0
    for bit in range(bits("space")):
        place = place * 2 + ((apart >> bit) & 1)
    return place


def stepped_tile(tile, wide, base, store):
    depth, lanes = tile.shape
    for part in range(lanes // LANES):
        rows = wide.at[part]
        rows[pl.ds(base + depth, PAD), :] = jnp.zeros((PAD, LANES), F32)
        rows[pl.ds(base, depth), :] = tile[:, part * LANES : (part + 1) * LANES].astype(F32)
        store(part, rows[pl.ds(base + 1, depth), :].astype(BF16))


def back_kernel(orders, here, cells, filters, low, high, out, plane, row, wide, moved, spread):
    vols, wide_a, wide_b, depth, count = cells.shape
    side_a, side_b = wide_a - 1, wide_b - 1
    inputs = filters.shape[4]
    for n in range(vols):
        for a in range(wide_a):
            for b in range(wide_b):
                slot = ((n * wide_a + a) * wide_b + b) % 8 * (PAD + depth)

                def store(part, piece):
                    moved[n, a, b, :, part * LANES : (part + 1) * LANES] = piece

                stepped_tile(cells[n, a, b], wide, slot, store)

    def lefts(ref, da, db):
        return ref[:, da : da + side_a, db : db + side_b].reshape(-1, count)

    for sa in range(2):
        for sb in range(2):
            even = odd = None
            for i, da in REACH[sa]:
                for j, db in REACH[sb]:
                    tap = (i * 3 + j) * 3
                    here_cells = lefts(cells, da, db)
                    first = dot(here_cells, filter_tap(filters, here, tap + 1, orders), NN)
                    second = dot(here_cells, filter_tap(filters, here, tap + 2, orders), NN)
                    second += dot(lefts(moved, da, db), filter_tap(filters, here, tap, orders), NN)
                    even = first if even is None else even + first
                    odd = second if odd is None else odd + second
            for parity, value in enumerate((even, odd)):
                value = value.reshape(vols, side_a, side_b, depth, inputs)
                for n in range(vols):
                    for a in range(side_a):
                        for b in range(side_b):
                            for part in range(inputs // LANES):
                                spread[
                                    part, n, 2 * a + sa, 2 * b + sb, pl.ds(parity, depth, stride=2), :
                                ] = value[n, a, b, :, part * LANES : (part + 1) * LANES]
    for part in range(inputs // LANES):
        lanes = slice(part * LANES, (part + 1) * LANES)
        act = jnp.concatenate([low[:, :, :, :, lanes], high[:, :, :, :, lanes]], axis=2)
        act = act.astype(F32)
        value = (spread[part] * jnp.where(act > 0, 1.0, 0.3)).astype(BF16)
        out[:, :, :, :, lanes] = value
        plane[:, :, :, :, lanes] = value[:, :1]
        row[:, :, :, :, lanes] = value[:, :, :1]


def hidden_back(here, cells, filters, low, high, orders):
    vols, wide_a, wide_b, depth, count = cells.shape
    inputs = low.shape[-1]
    shape = low.shape[:2] + (low.shape[2] + high.shape[2],) + low.shape[3:]
    outs = [
        jax.ShapeDtypeStruct(shape, BF16),
        jax.ShapeDtypeStruct((vols, 1) + shape[2:], BF16),
        jax.ShapeDtypeStruct(shape[:2] + (1,) + shape[3:], BF16),
    ]
    return call(
        functools.partial(back_kernel, orders),
        outs,
        (here, cells, filters, low, high),
        [
            pltpu.VMEM((count // LANES, 8 * (PAD + depth), LANES), F32),
            pltpu.VMEM(cells.shape, BF16),
            pltpu.VMEM((inputs // LANES,) + shape[:4] + (LANES,), F32),
        ],
        flops=2 * vols * (wide_a - 1) * (wide_b - 1) * depth * 27 * inputs * count,
    )


def volume_kernel(orders, here, cells, plane, row, filters, out, wide, ext, moved, spread):
    _, side_a, side_b, depth, count = cells.shape
    inputs = filters.shape[4]
    for a in range(side_a + 1):
        for b in range(side_b + 1):
            if b == side_b:
                tile = row[0, a, 0]
            elif a == side_a:
                tile = plane[0, 0, b]
            else:
                tile = cells[0, a, b]
            ext[a, b] = tile
            slot = ((a * (side_b + 1) + b) % 8) * (PAD + depth)

            def store(part, piece):
                moved[a, b, :, part * LANES : (part + 1) * LANES] = piece

            stepped_tile(tile, wide, slot, store)

    def lefts(ref, da, db):
        return ref[da : da + side_a, db : db + side_b].reshape(-1, count)

    for sa in range(2):
        for sb in range(2):
            both = late = None
            for i, da in REACH[sa]:
                for j, db in REACH[sb]:
                    tap = (i * 3 + j) * 3
                    pair = jnp.concatenate(
                        [filter_tap(filters, here, tap + k, orders) for k in (1, 2)], axis=1
                    )
                    first = dot(lefts(ext, da, db), pair, NN)
                    second = dot(lefts(moved, da, db), filter_tap(filters, here, tap, orders), NN)
                    both = first if both is None else both + first
                    late = second if late is None else late + second
            halves = (both[:, :inputs], both[:, inputs:] + late)
            for parity, value in enumerate(halves):
                value = value.reshape(side_a, side_b, depth, inputs)
                for a in range(side_a):
                    for b in range(side_b):
                        spread[2 * a + sa, 2 * b + sb, pl.ds(parity, depth, stride=2), :] = value[a, b]
    out[0] = spread[...].astype(BF16)


def volume_grads(here, cells, plane, row, filters, orders):
    vols, side_a, side_b, depth, count = cells.shape
    inputs = filters.shape[4]
    out = jax.ShapeDtypeStruct((vols, 2 * side_a, 2 * side_b, 2 * depth, inputs), BF16)

    def block(shape):
        return pl.BlockSpec((1,) + shape[1:], lambda n: (n, 0, 0, 0, 0))

    return call(
        functools.partial(volume_kernel, orders),
        [out],
        (here, cells, plane, row, filters),
        [
            pltpu.VMEM((count // LANES, 8 * (PAD + depth), LANES), F32),
            pltpu.VMEM((side_a + 1, side_b + 1, depth, count), BF16),
            pltpu.VMEM((side_a + 1, side_b + 1, depth, count), BF16),
            pltpu.VMEM((2 * side_a, 2 * side_b, 2 * depth, inputs), F32),
        ],
        (vols,),
        [
            pl.BlockSpec(memory_space=pltpu.SMEM),
            block(cells.shape),
            block(plane.shape),
            block(row.shape),
            pl.BlockSpec(memory_space=pltpu.VMEM),
        ],
        [block(out.shape)],
        flops=2 * vols * side_a * side_b * depth * 27 * inputs * count,
    )[0]


def near_cells(value, shape):
    chan = lax.axis_size("chan")
    vols, side_a, side_b, side_c, mine = shape
    rows = side_b // chan
    value = value.reshape(chan, vols, side_a, side_b, side_c * mine)
    value = jnp.pad(value, ((0, 0), (0, 0), (0, 0), (0, 1), (0, 0)))
    value = lax.dynamic_slice_in_dim(value, lax.axis_index("chan") * rows, rows + 1, 3)
    count = bits("chan")
    value = value.reshape((2,) * count + value.shape[1:])
    for dim, bit in enumerate([0] + far_bits()):
        mine_bit = (lax.axis_index("chan") >> bit) & 1
        value = jnp.where(mine_bit == 1, jnp.flip(value, dim), value)
    value = jnp.transpose(value, (*range(1, count), 0, *range(count, value.ndim)))
    value = value.reshape(chan, vols, side_a, rows + 1, side_c, mine)
    value = jnp.transpose(value, (1, 2, 3, 4, 0, 5))
    near = value.reshape(vols, side_a, rows + 1, side_c, chan * mine)
    plane = shifted(near[:, :1], (-1, 0))
    return near[:, :, :rows], jnp.concatenate([near, plane], axis=1)


def local(volume, w_first, w_second, cotangent):
    here = position()
    orders = (list(range(bits("space"))), [0] + far_bits())
    side_b = volume.shape[2] // 2

    plane = shifted(volume[:, -1:], (1, 0))
    part = far_gather(own_part(w_first))
    first_full = near_gather(doubled(part, "chan", 0))
    row = jnp.concatenate([plane, volume], axis=1)[:, :, -1:]
    row = shifted(row, (0, 1))
    second = own_part(w_second)
    taps = second.shape[0]
    riders = cotangent.reshape((-1,) + second.shape[1:])
    part = far_gather(jnp.concatenate([second, riders], axis=0))
    part = doubled(part, "chan", 0)
    second_full = near_gather(part[:, :, :taps])
    grad_cells, grad_ext = near_cells(part[:, :, taps:], cotangent.shape)

    vol_main = parted_volume(volume, plane)
    (high,) = forward(here, (vol_main,), first_full, orders, range(1, side_b), "high")
    low, vol_row = forward(here, (vol_main, row), first_full, orders, range(1), "low")
    hid_row = shifted(high[:, :, -1:], (0, 1))
    hid_corner = shifted(high[:, -1:, -1:], (1, 1))
    hid_plane = jnp.concatenate([low[:, -1:], high[:, -1:]], axis=2)
    hid_plane = shifted(hid_plane, (1, 0))
    blocks = (low, high, hid_plane, hid_row, hid_corner)
    keep, send, act_parts = second_grads(here, blocks, grad_cells, orders)
    second_sum = mixed_sum(core_sum(keep, send))

    pre_back, pre_plane, pre_row = hidden_back(here, grad_ext, second_full, low, high, orders)
    keep, send = first_grads(here, (vol_main, vol_row), pre_back, orders)
    first_sum = plain_sum(core_sum(keep, send))
    first_grad, second_grad = finish_sum([first_sum, second_sum])
    plane = shifted(pre_plane, (-1, 0))
    row = jnp.concatenate([pre_row, plane[:, :, :1]], axis=1)
    row = shifted(row, (0, -1))
    out_b = range(grad_cells.shape[2])
    (local_out,) = forward(here, (act_parts,), second_full, orders, out_b, "out")
    second_out = lax.all_to_all(local_out, "chan", split_axis=4, concat_axis=2, tiled=True)
    volume_grad = volume_grads(here, pre_back, plane, row, first_full, orders)
    return (second_out, volume_grad, first_grad, second_grad)


def solution(mesh):
    return jax.shard_map(
        local,
        mesh=mesh,
        in_specs=(
            P(None, "space", "chan", None, None),
            P(None, None, None, None, "chan"),
            P(None, None, None, None, "chan"),
            P(None, "space", None, None, "chan"),
        ),
        out_specs=(
            P(None, "space", None, None, "chan"),
            P(None, "space", "chan", None, None),
            P(None, None, None, None, "chan"),
            P(None, None, None, None, "chan"),
        ),
        check_vma=False,
    )
```

```python
import functools

import jax
import jax.numpy as jnp
from jax import lax
from jax.experimental import pallas as pl
from jax.experimental.pallas import tpu as pltpu
from jax.sharding import PartitionSpec as P


BF16 = jnp.bfloat16
F32 = jnp.float32
LANES = 128
PAD = 8
NT = (((1,), (1,)), ((), ()))
NN = (((1,), (0,)), ((), ()))
REACH = (((1, 0),), ((0, 1), (2, 0)))


def dot(left, right, dims):
    return lax.dot_general(left, right, dims, preferred_element_type=F32)


def bits(axis):
    return lax.axis_size(axis).bit_length() - 1


def shifted(value, steps):
    pairs = []
    sizes = (lax.axis_size("space"), lax.axis_size("chan"))
    for a in range(sizes[0]):
        for b in range(sizes[1]):
            to = (a + steps[0], b + steps[1])
            if 0 <= to[0] < sizes[0] and 0 <= to[1] < sizes[1]:
                pairs.append((a * sizes[1] + b, to[0] * sizes[1] + to[1]))
    return lax.ppermute(value, ("space", "chan"), pairs)


def swapped(value, axis, bit):
    count = lax.axis_size(axis)
    return lax.ppermute(value, axis, [(i, i ^ (1 << bit)) for i in range(count)])


def doubled(value, axis, bit):
    other = swapped(value, axis, bit)
    return jnp.stack([value, other])


def position():
    return jnp.stack([lax.axis_index("space"), lax.axis_index("chan")]).astype(jnp.int32)


def own_part(shard):
    space = lax.axis_size("space")
    edge, inputs, mine = shard.shape[0], shard.shape[3], shard.shape[4]
    taps = edge**3
    each = -(-taps // space)
    flat = jnp.transpose(shard.reshape(taps, inputs, mine), (0, 2, 1))
    flat = jnp.pad(flat, ((0, each * space - taps), (0, 0), (0, 0)))
    return lax.dynamic_slice_in_dim(flat, lax.axis_index("space") * each, each, 0)


def far_bits():
    return list(reversed(range(1, bits("chan"))))


def high_bits():
    return list(reversed(range(1, bits("space"))))


def far_swapped(value, mask):
    count = lax.axis_size("chan")
    return lax.ppermute(value, "chan", [(i, i ^ (mask << 1)) for i in range(count)])


def far_gather(part):
    others = [far_swapped(part, m) for m in range(1, lax.axis_size("chan") // 2)]
    return jnp.stack([part, *others])


def near_gather(part):
    each, mine, inputs = part.shape[-3:]
    for bit in high_bits():
        part = doubled(part, "space", bit)
    part = doubled(part, "space", 0)
    return part.reshape(lax.axis_size("space"), lax.axis_size("chan"), each, mine, inputs)


def relative(index, mine, order):
    apart = index ^ mine
    place = 0
    for bit in order:
        place = place * 2 + ((apart >> bit) & 1)
    return place


def filter_tap(ref, here, tap, orders):
    each = ref.shape[2]
    owner = relative(tap // each, here[0], orders[0])
    rows = [
        ref[owner, relative(chan, here[1], orders[1]), tap % each]
        for chan in range(ref.shape[1])
    ]
    return jnp.concatenate(rows, axis=0)


def scratch_avals(scratch):
    return [jax.ShapeDtypeStruct(ref.inner_aval.shape, ref.inner_aval.dtype) for ref in scratch]


def call(kernel, outs, args, scratch=(), grid=None, in_specs=None, out_specs=None, flops=0):
    moved = sum(a.size * a.dtype.itemsize for a in args)
    moved += sum(o.size * o.dtype.itemsize for o in outs)
    used = sum(v.size * v.dtype.itemsize for v in scratch_avals(scratch))
    grant = min(56 * 2**20, moved + used + 6 * 2**20)
    whole = pl.BlockSpec(memory_space=pltpu.VMEM)
    smem = pl.BlockSpec(memory_space=pltpu.SMEM)
    specs = in_specs or [smem if a.dtype == jnp.int32 else whole for a in args]
    return pl.pallas_call(
        kernel,
        out_shape=outs,
        grid=grid or (),
        in_specs=specs,
        out_specs=out_specs or [whole] * len(outs),
        scratch_shapes=scratch,
        cost_estimate=pl.CostEstimate(flops=flops, bytes_accessed=moved, transcendentals=0),
        compiler_params=pltpu.CompilerParams(vmem_limit_bytes=grant),
    )(*args)


def parted_tile(tile, wide, base, store):
    depth, lanes = tile.shape
    for part in range(lanes // LANES):
        rows = wide.at[part]
        rows[pl.ds(base, PAD), :] = jnp.zeros((PAD, LANES), F32)
        rows[pl.ds(base + PAD, depth), :] = tile[:, part * LANES : (part + 1) * LANES].astype(F32)
        for k in range(3):
            piece = rows[pl.ds(base + PAD - 1 + k, depth // 2, stride=2), :]
            store(k, part, piece.astype(BF16))


def part_block(pick, out, n, shape, wide):
    wide_a, wide_b, depth = shape
    for a in range(wide_a):
        for b in range(wide_b):
            slot = ((a * wide_b + b) % 8) * (PAD + depth)

            def store(k, part, piece):
                out[k, n, a, b, :, part * LANES : (part + 1) * LANES] = piece

            parted_tile(pick(a, b), wide, slot, store)


def part_scratch(depth, lanes):
    return pltpu.VMEM((lanes // LANES, 8 * (PAD + depth), LANES), F32)


def parted_volume(own, plane):
    vols, side_a, side_b, depth, lanes = own.shape
    out = jax.ShapeDtypeStruct((3, vols, side_a + 1, side_b, depth // 2, lanes), BF16)

    def kernel(own, plane, out, wide):
        def pick(a, b):
            return plane[0, 0, b] if a == 0 else own[0, a - 1, b]

        part_block(pick, out, 0, (side_a + 1, side_b, depth), wide)

    def block(shape):
        return pl.BlockSpec((1,) + shape[1:], lambda n: (n, 0, 0, 0, 0))

    return call(
        kernel,
        [out],
        (own, plane),
        [part_scratch(depth, lanes)],
        (vols,),
        [block(own.shape), block(plane.shape)],
        [pl.BlockSpec((3, 1) + out.shape[2:], lambda n: (0, n, 0, 0, 0, 0))],
    )[0]


def window(refs, i, j, sides):
    vols, side_a, cells_b = sides
    rows = []
    for n in range(vols):
        for a in range(side_a):
            for b in cells_b:
                y = 2 * b + j
                ref = refs[0]
                if len(refs) == 2:
                    ref, y = (refs[1], 0) if y == 0 else (refs[0], y - 1)
                assert 0 <= y < ref.shape[3]
                rows.append(jnp.concatenate([ref[k, n, 2 * a + i, y] for k in range(3)], axis=1))
    return jnp.concatenate(rows, axis=0)


def forward_total(orders, sides, refs, here, filters, acc):
    acc[...] = jnp.zeros_like(acc)

    def step(i, carry):
        for j in range(3):
            right = jnp.concatenate(
                [filter_tap(filters, here, i * 9 + j * 3 + k, orders) for k in range(3)], axis=1
            )
            acc[...] += dot(window(refs, i, j, sides), right, NT)
        return carry

    lax.fori_loop(0, 3, step, 0)
    return acc[...]


def leaky(total):
    return jnp.where(total > 0, total, 0.3 * total)


def forward(here, parts, filters, orders, cells_b, kind):
    main = parts[0]
    _, vols, wide_a, _, depth, inputs = main.shape
    sides = (vols, (wide_a - 1) // 2, cells_b)
    count = filters.shape[1] * filters.shape[3]
    cells = vols * sides[1] * len(cells_b) * depth
    outs = [jax.ShapeDtypeStruct((vols, sides[1], len(cells_b), depth, count), BF16)]
    scratch = [pltpu.VMEM((cells, count), F32)]
    if kind == "low":
        outs.append(jax.ShapeDtypeStruct(main.shape[:3] + (1,) + main.shape[4:], BF16))
        scratch.append(part_scratch(2 * depth, inputs))

    def kernel(here, filters, main, *rest):
        if kind == "low":
            row, out, row_parts, acc, wide = rest

            def split(n, carry):
                part_block(lambda a, b: row[n, a, 0], row_parts, n, (wide_a, 1, 2 * depth), wide)
                return carry

            lax.fori_loop(0, vols, split, 0)
            refs = (main, row_parts)
        else:
            out, acc = rest
            refs = (main, None) if kind == "high" else (main,)
        total = forward_total(orders, sides, refs, here, filters, acc)
        if kind != "out":
            total = leaky(total)
        out[...] = total.astype(BF16).reshape(out.shape)

    return call(
        kernel,
        outs,
        (here, filters, *parts),
        scratch,
        flops=2 * cells * 27 * inputs * count,
    )


def grads_body(orders, sides, here, grads, refs, keep, send, turned):
    cells, count = turned.shape[1], turned.shape[0]
    inputs = refs[0].shape[5]
    pieces = inputs // LANES
    chans = 2 ** len(orders[1])
    mine = count // chans
    each = keep.shape[2] // pieces
    half = keep.shape[0]
    turned[...] = jnp.transpose(grads[...].reshape(cells, count).astype(F32), (1, 0)).astype(BF16)

    def put(ref, place, tap, part):
        for chan in range(chans):
            to = relative(chan, here[1], orders[1])
            for piece in range(pieces):
                lanes = slice(piece * LANES, (piece + 1) * LANES)
                ref[place, to, (tap % each) * pieces + piece] = part[chan * mine : (chan + 1) * mine, lanes]

    def step(i, carry):
        for j in range(3):
            part = dot(turned[...], window(refs, i, j, sides), NN).astype(BF16)
            for k in range(3):
                tap = i * 9 + j * 3 + k
                place = relative(tap // each, here[0], orders[0])
                piece = part[:, k * inputs : (k + 1) * inputs]

                @pl.when(place < half)
                def _():
                    put(keep, place, tap, piece)

                @pl.when(place >= half)
                def _():
                    put(send, place - half, tap, piece)

        return carry

    lax.fori_loop(0, 3, step, 0)
    blank = jnp.zeros((count, inputs), BF16)
    for tap in range(27, each * 2 * half):
        place = relative(tap // each, here[0], orders[0])

        @pl.when(place < half)
        def _():
            put(keep, place, tap, blank)

        @pl.when(place >= half)
        def _():
            put(send, place - half, tap, blank)


def grads_out(count, inputs, orders):
    space, chans = 2 ** len(orders[0]), 2 ** len(orders[1])
    each = -(-27 // space) * (inputs // LANES)
    return jax.ShapeDtypeStruct((space // 2, chans, each, count // chans, LANES), BF16)


def first_grads(here, refs, grads, orders):
    inputs = refs[0].shape[5]
    vols, side_a, side_b, depth, count = grads.shape
    sides = (vols, side_a, range(side_b))
    cells = vols * side_a * side_b * depth
    out = grads_out(count, inputs, orders)

    def kernel(here, grads, main, row, keep, send, turned):
        grads_body(orders, sides, here, grads, (main, row), keep, send, turned)

    return call(
        kernel,
        [out, out],
        (here, grads, *refs),
        [pltpu.VMEM((count, cells), BF16)],
        flops=2 * cells * 27 * inputs * count,
    )


def second_grads(here, blocks, grads, orders):
    low, high = blocks[:2]
    side_x, deep, inputs = low.shape[1], low.shape[3], low.shape[4]
    wide_b = low.shape[2] + high.shape[2] + 1
    vols, side_a, side_b, depth, count = grads.shape
    sides = (vols, side_a, range(side_b))
    cells = vols * side_a * side_b * depth
    out = grads_out(count, inputs, orders)
    parts = jax.ShapeDtypeStruct((3, vols, side_x + 1, wide_b, depth, inputs), BF16)

    def kernel(here, grads, low, high, plane, row, corner, keep, send, parts, turned, wide):
        def split(n, carry):
            def pick(a, b):
                if b == 0:
                    return corner[n, 0, 0] if a == 0 else row[n, a - 1, 0]
                if a == 0:
                    return plane[n, 0, b - 1]
                return low[n, a - 1, 0] if b == 1 else high[n, a - 1, b - 2]

            part_block(pick, parts, n, (side_x + 1, wide_b, deep), wide)
            return carry

        lax.fori_loop(0, vols, split, 0)
        grads_body(orders, sides, here, grads, (parts,), keep, send, turned)

    return call(
        kernel,
        [out, out, parts],
        (here, grads, *blocks),
        [pltpu.VMEM((count, cells), BF16), part_scratch(deep, inputs)],
        flops=2 * cells * 27 * inputs * count,
    )


def core_sum(keep, send):
    tail = keep.shape[2:]
    other = swapped(send, "space", 0)
    total = keep.astype(F32) + other.astype(F32)
    highs = bits("space") - 1
    return total.reshape((2,) * highs + (2, -1) + tail)


def half_sum(value, axis, bit, dim):
    keep = lax.index_in_dim(value, 0, dim, keepdims=False)
    send = lax.index_in_dim(value, 1, dim, keepdims=False)
    other = swapped(send.astype(BF16), axis, bit)
    return keep.astype(F32) + other.astype(F32)


def plain_sum(total):
    for bit in range(1, bits("space")):
        total = half_sum(total, "space", bit, 0)
    return half_sum(total, "chan", 0, 0)


def mixed_sum(total):
    highs = list(range(1, bits("space")))
    cut = (total.shape[-3] + 1) // 2
    one, two = total[..., :cut, :, :], total[..., cut:, :, :]
    two = half_sum(two, "chan", 0, len(highs))
    for bit in highs:
        one = half_sum(one, "space", bit, 0)
    one = half_sum(one, "chan", 0, 0)
    for bit in highs:
        two = half_sum(two, "space", bit, 0)
    return jnp.concatenate([one, two], axis=-3)


def finish_sum(totals):
    count = lax.axis_size("chan") // 2
    space = lax.axis_size("space")
    merged = jnp.concatenate(totals, axis=1)
    part = merged[0].astype(F32)
    for m in range(1, count):
        part = part + far_swapped(merged[m].astype(BF16), m).astype(F32)
    part = part.astype(BF16)
    for bit in high_bits():
        part = doubled(part, "space", bit)
    part = doubled(part, "space", 0)
    part = part.reshape((space,) + merged.shape[1:])
    apart = [jnp.int32(s) ^ lax.axis_index("space") for s in range(space)]
    ordered = [lax.dynamic_index_in_dim(part, space_order(a), 0, keepdims=False) for a in apart]
    outs, begin = [], 0
    taps = -(-27 // space)
    for total in totals:
        rows, mine = total.shape[1], total.shape[2]
        pieces = rows // taps
        full = jnp.concatenate([o[begin : begin + rows] for o in ordered], axis=0)
        full = full.reshape(space * taps, pieces, mine, LANES)[:27].astype(F32)
        full = jnp.transpose(full, (0, 1, 3, 2)).reshape(3, 3, 3, pieces * LANES, mine)
        outs.append(full)
        begin += rows
    return outs


def space_order(apart):
    place = 0
    for bit in range(bits("space")):
        place = place * 2 + ((apart >> bit) & 1)
    return place


def stepped_tile(tile, wide, base, store):
    depth, lanes = tile.shape
    for part in range(lanes // LANES):
        rows = wide.at[part]
        rows[pl.ds(base + depth, PAD), :] = jnp.zeros((PAD, LANES), F32)
        rows[pl.ds(base, depth), :] = tile[:, part * LANES : (part + 1) * LANES].astype(F32)
        store(part, rows[pl.ds(base + 1, depth), :].astype(BF16))


def back_kernel(orders, here, cells, filters, low, high, out, plane, row, wide, moved, spread):
    vols, wide_a, wide_b, depth, count = cells.shape
    side_a, side_b = wide_a - 1, wide_b - 1
    inputs = filters.shape[4]
    for n in range(vols):
        for a in range(wide_a):
            for b in range(wide_b):
                slot = ((n * wide_a + a) * wide_b + b) % 8 * (PAD + depth)

                def store(part, piece):
                    moved[n, a, b, :, part * LANES : (part + 1) * LANES] = piece

                stepped_tile(cells[n, a, b], wide, slot, store)

    def lefts(ref, da, db):
        return ref[:, da : da + side_a, db : db + side_b].reshape(-1, count)

    for sa in range(2):
        for sb in range(2):
            even = odd = None
            for i, da in REACH[sa]:
                for j, db in REACH[sb]:
                    tap = (i * 3 + j) * 3
                    here_cells = lefts(cells, da, db)
                    first = dot(here_cells, filter_tap(filters, here, tap + 1, orders), NN)
                    second = dot(here_cells, filter_tap(filters, here, tap + 2, orders), NN)
                    second += dot(lefts(moved, da, db), filter_tap(filters, here, tap, orders), NN)
                    even = first if even is None else even + first
                    odd = second if odd is None else odd + second
            for parity, value in enumerate((even, odd)):
                value = value.reshape(vols, side_a, side_b, depth, inputs)
                for n in range(vols):
                    for a in range(side_a):
                        for b in range(side_b):
                            for part in range(inputs // LANES):
                                spread[
                                    part, n, 2 * a + sa, 2 * b + sb, pl.ds(parity, depth, stride=2), :
                                ] = value[n, a, b, :, part * LANES : (part + 1) * LANES]
    for part in range(inputs // LANES):
        lanes = slice(part * LANES, (part + 1) * LANES)
        act = jnp.concatenate([low[:, :, :, :, lanes], high[:, :, :, :, lanes]], axis=2)
        act = act.astype(F32)
        value = (spread[part] * jnp.where(act > 0, 1.0, 0.3)).astype(BF16)
        out[:, :, :, :, lanes] = value
        plane[:, :, :, :, lanes] = value[:, :1]
        row[:, :, :, :, lanes] = value[:, :, :1]


def hidden_back(here, cells, filters, low, high, orders):
    vols, wide_a, wide_b, depth, count = cells.shape
    inputs = low.shape[-1]
    shape = low.shape[:2] + (low.shape[2] + high.shape[2],) + low.shape[3:]
    outs = [
        jax.ShapeDtypeStruct(shape, BF16),
        jax.ShapeDtypeStruct((vols, 1) + shape[2:], BF16),
        jax.ShapeDtypeStruct(shape[:2] + (1,) + shape[3:], BF16),
    ]
    return call(
        functools.partial(back_kernel, orders),
        outs,
        (here, cells, filters, low, high),
        [
            pltpu.VMEM((count // LANES, 8 * (PAD + depth), LANES), F32),
            pltpu.VMEM(cells.shape, BF16),
            pltpu.VMEM((inputs // LANES,) + shape[:4] + (LANES,), F32),
        ],
        flops=2 * vols * (wide_a - 1) * (wide_b - 1) * depth * 27 * inputs * count,
    )


def volume_kernel(orders, here, cells, plane, row, filters, out, wide, ext, moved, spread):
    _, side_a, side_b, depth, count = cells.shape
    inputs = filters.shape[4]
    for a in range(side_a + 1):
        for b in range(side_b + 1):
            if b == side_b:
                tile = row[0, a, 0]
            elif a == side_a:
                tile = plane[0, 0, b]
            else:
                tile = cells[0, a, b]
            ext[a, b] = tile
            slot = ((a * (side_b + 1) + b) % 8) * (PAD + depth)

            def store(part, piece):
                moved[a, b, :, part * LANES : (part + 1) * LANES] = piece

            stepped_tile(tile, wide, slot, store)

    def lefts(ref, da, db):
        return ref[da : da + side_a, db : db + side_b].reshape(-1, count)

    for sa in range(2):
        for sb in range(2):
            both = late = None
            for i, da in REACH[sa]:
                for j, db in REACH[sb]:
                    tap = (i * 3 + j) * 3
                    pair = jnp.concatenate(
                        [filter_tap(filters, here, tap + k, orders) for k in (1, 2)], axis=1
                    )
                    first = dot(lefts(ext, da, db), pair, NN)
                    second = dot(lefts(moved, da, db), filter_tap(filters, here, tap, orders), NN)
                    both = first if both is None else both + first
                    late = second if late is None else late + second
            halves = (both[:, :inputs], both[:, inputs:] + late)
            for parity, value in enumerate(halves):
                value = value.reshape(side_a, side_b, depth, inputs)
                for a in range(side_a):
                    for b in range(side_b):
                        spread[2 * a + sa, 2 * b + sb, pl.ds(parity, depth, stride=2), :] = value[a, b]
    out[0] = spread[...].astype(BF16)


def volume_grads(here, cells, plane, row, filters, orders):
    vols, side_a, side_b, depth, count = cells.shape
    inputs = filters.shape[4]
    out = jax.ShapeDtypeStruct((vols, 2 * side_a, 2 * side_b, 2 * depth, inputs), BF16)

    def block(shape):
        return pl.BlockSpec((1,) + shape[1:], lambda n: (n, 0, 0, 0, 0))

    return call(
        functools.partial(volume_kernel, orders),
        [out],
        (here, cells, plane, row, filters),
        [
            pltpu.VMEM((count // LANES, 8 * (PAD + depth), LANES), F32),
            pltpu.VMEM((side_a + 1, side_b + 1, depth, count), BF16),
            pltpu.VMEM((side_a + 1, side_b + 1, depth, count), BF16),
            pltpu.VMEM((2 * side_a, 2 * side_b, 2 * depth, inputs), F32),
        ],
        (vols,),
        [
            pl.BlockSpec(memory_space=pltpu.SMEM),
            block(cells.shape),
            block(plane.shape),
            block(row.shape),
            pl.BlockSpec(memory_space=pltpu.VMEM),
        ],
        [block(out.shape)],
        flops=2 * vols * side_a * side_b * depth * 27 * inputs * count,
    )[0]


class CellExchange:
    def __init__(self, cotangent):
        vols, side_a, side_b, side_c, mine = cotangent.shape
        self.count = bits("chan")
        self.tail = (side_b // 2**self.count, vols, side_a, side_c, mine)
        flat = cotangent.reshape(vols, side_a, side_b, side_c * mine)
        flat = jnp.transpose(flat, (2, 0, 1, 3))
        self.value = flat.reshape((2,) * self.count + (-1,) + flat.shape[1:])
        self.open = list(reversed(range(self.count)))
        self.done = []

    def stage(self, bit):
        dim = self.open.index(bit)
        mine = (lax.axis_index("chan") >> bit) & 1
        keep = lax.dynamic_index_in_dim(self.value, mine, dim, keepdims=False)
        send = lax.dynamic_index_in_dim(self.value, 1 - mine, dim, keepdims=False)
        other = swapped(send, "chan", bit)
        low, high = jnp.where(mine == 1, other, keep), jnp.where(mine == 1, keep, other)
        self.value = jnp.stack([low, high], axis=self.count - 1)
        self.open.remove(bit)
        self.done.append(bit)

    def finish(self):
        rows, vols, side_a, side_c, mine = self.tail
        count = self.count
        value = self.value.reshape((2,) * count + (rows, vols, side_a, side_c, mine))
        sources = [self.done.index(bit) for bit in reversed(range(count))]
        value = jnp.transpose(
            value, (count + 1, count + 2, count, count + 3, *sources, count + 4)
        )
        own = value.reshape(vols, side_a, rows, side_c, 2**count * mine)
        row = shifted(own[:, :, :1], (0, -1))
        near = jnp.concatenate([own, row], axis=2)
        plane = shifted(near[:, :1], (-1, 0))
        return own, jnp.concatenate([near, plane], axis=1)


def local(volume, w_first, w_second, cotangent):
    here = position()
    orders = (list(range(bits("space"))), [0] + far_bits())
    side_b = volume.shape[2] // 2

    plane = shifted(volume[:, -1:], (1, 0))
    part = far_gather(own_part(w_first))
    first_full = near_gather(doubled(part, "chan", 0))
    row = jnp.concatenate([plane, volume], axis=1)[:, :, -1:]
    row = shifted(row, (0, 1))
    part = far_gather(own_part(w_second))
    second_full = near_gather(doubled(part, "chan", 0))
    cells = CellExchange(cotangent)
    for bit in far_bits() + [0]:
        cells.stage(bit)
    grad_cells, grad_ext = cells.finish()

    vol_main = parted_volume(volume, plane)
    (high,) = forward(here, (vol_main,), first_full, orders, range(1, side_b), "high")
    low, vol_row = forward(here, (vol_main, row), first_full, orders, range(1), "low")
    hid_row = shifted(high[:, :, -1:], (0, 1))
    hid_corner = shifted(high[:, -1:, -1:], (1, 1))
    hid_plane = jnp.concatenate([low[:, -1:], high[:, -1:]], axis=2)
    hid_plane = shifted(hid_plane, (1, 0))
    blocks = (low, high, hid_plane, hid_row, hid_corner)
    keep, send, act_parts = second_grads(here, blocks, grad_cells, orders)
    second_sum = mixed_sum(core_sum(keep, send))

    pre_back, pre_plane, pre_row = hidden_back(here, grad_ext, second_full, low, high, orders)
    keep, send = first_grads(here, (vol_main, vol_row), pre_back, orders)
    first_sum = plain_sum(core_sum(keep, send))
    first_grad, second_grad = finish_sum([first_sum, second_sum])
    plane = shifted(pre_plane, (-1, 0))
    row = shifted(pre_row, (0, -1))
    corner = shifted(pre_row[:, :1], (-1, -1))
    row = jnp.concatenate([row, corner], axis=1)
    out_b = range(grad_cells.shape[2])
    (local_out,) = forward(here, (act_parts,), second_full, orders, out_b, "out")
    second_out = lax.all_to_all(local_out, "chan", split_axis=4, concat_axis=2, tiled=True)
    volume_grad = volume_grads(here, pre_back, plane, row, first_full, orders)
    return (second_out, volume_grad, first_grad, second_grad)


def solution(mesh):
    return jax.shard_map(
        local,
        mesh=mesh,
        in_specs=(
            P(None, "space", "chan", None, None),
            P(None, None, None, None, "chan"),
            P(None, None, None, None, "chan"),
            P(None, "space", None, None, "chan"),
        ),
        out_specs=(
            P(None, "space", None, None, "chan"),
            P(None, "space", "chan", None, None),
            P(None, None, None, None, "chan"),
            P(None, None, None, None, "chan"),
        ),
        check_vma=False,
    )
```

```python
import functools

import jax
import jax.numpy as jnp
from jax import lax
from jax.experimental import pallas as pl
from jax.experimental.pallas import tpu as pltpu
from jax.sharding import PartitionSpec as P


BF16 = jnp.bfloat16
F32 = jnp.float32
LANES = 128
PAD = 8
NT = (((1,), (1,)), ((), ()))
NN = (((1,), (0,)), ((), ()))
REACH = (((1, 0),), ((0, 1), (2, 0)))


def dot(left, right, dims):
    return lax.dot_general(left, right, dims, preferred_element_type=F32)


def bits(axis):
    return lax.axis_size(axis).bit_length() - 1


def shifted(value, steps):
    pairs = []
    sizes = (lax.axis_size("space"), lax.axis_size("chan"))
    for a in range(sizes[0]):
        for b in range(sizes[1]):
            to = (a + steps[0], b + steps[1])
            if 0 <= to[0] < sizes[0] and 0 <= to[1] < sizes[1]:
                pairs.append((a * sizes[1] + b, to[0] * sizes[1] + to[1]))
    return lax.ppermute(value, ("space", "chan"), pairs)


def swapped(value, axis, bit):
    count = lax.axis_size(axis)
    return lax.ppermute(value, axis, [(i, i ^ (1 << bit)) for i in range(count)])


def doubled(value, axis, bit):
    other = swapped(value, axis, bit)
    return jnp.stack([value, other])


def position():
    return jnp.stack([lax.axis_index("space"), lax.axis_index("chan")]).astype(jnp.int32)


def own_part(shard):
    space = lax.axis_size("space")
    edge, inputs, mine = shard.shape[0], shard.shape[3], shard.shape[4]
    taps = edge**3
    each = -(-taps // space)
    flat = jnp.transpose(shard.reshape(taps, inputs, mine), (0, 2, 1))
    flat = jnp.pad(flat, ((0, each * space - taps), (0, 0), (0, 0)))
    return lax.dynamic_slice_in_dim(flat, lax.axis_index("space") * each, each, 0)


def far_bits():
    return list(reversed(range(1, bits("chan"))))


def high_bits():
    return list(reversed(range(1, bits("space"))))


def far_swapped(value, mask):
    count = lax.axis_size("chan")
    return lax.ppermute(value, "chan", [(i, i ^ (mask << 1)) for i in range(count)])


def far_gather(part):
    others = [far_swapped(part, m) for m in range(1, lax.axis_size("chan") // 2)]
    return jnp.stack([part, *others])


def near_gather(part):
    each, mine, inputs = part.shape[-3:]
    for bit in high_bits():
        part = doubled(part, "space", bit)
    part = doubled(part, "space", 0)
    return part.reshape(lax.axis_size("space"), lax.axis_size("chan"), each, mine, inputs)


def relative(index, mine, order):
    apart = index ^ mine
    place = 0
    for bit in order:
        place = place * 2 + ((apart >> bit) & 1)
    return place


def filter_tap(ref, here, tap, orders):
    each = ref.shape[2]
    owner = relative(tap // each, here[0], orders[0])
    rows = [
        ref[owner, relative(chan, here[1], orders[1]), tap % each]
        for chan in range(ref.shape[1])
    ]
    return jnp.concatenate(rows, axis=0)


def scratch_avals(scratch):
    return [jax.ShapeDtypeStruct(ref.inner_aval.shape, ref.inner_aval.dtype) for ref in scratch]


def call(kernel, outs, args, scratch=(), grid=None, in_specs=None, out_specs=None, flops=0):
    moved = sum(a.size * a.dtype.itemsize for a in args)
    moved += sum(o.size * o.dtype.itemsize for o in outs)
    used = sum(v.size * v.dtype.itemsize for v in scratch_avals(scratch))
    grant = min(56 * 2**20, moved + used + 6 * 2**20)
    whole = pl.BlockSpec(memory_space=pltpu.VMEM)
    smem = pl.BlockSpec(memory_space=pltpu.SMEM)
    specs = in_specs or [smem if a.dtype == jnp.int32 else whole for a in args]
    return pl.pallas_call(
        kernel,
        out_shape=outs,
        grid=grid or (),
        in_specs=specs,
        out_specs=out_specs or [whole] * len(outs),
        scratch_shapes=scratch,
        cost_estimate=pl.CostEstimate(flops=flops, bytes_accessed=moved, transcendentals=0),
        compiler_params=pltpu.CompilerParams(vmem_limit_bytes=grant),
    )(*args)


def parted_tile(tile, wide, base, store):
    depth, lanes = tile.shape
    for part in range(lanes // LANES):
        rows = wide.at[part]
        rows[pl.ds(base, PAD), :] = jnp.zeros((PAD, LANES), F32)
        rows[pl.ds(base + PAD, depth), :] = tile[:, part * LANES : (part + 1) * LANES].astype(F32)
        for k in range(3):
            piece = rows[pl.ds(base + PAD - 1 + k, depth // 2, stride=2), :]
            store(k, part, piece.astype(BF16))


def part_block(pick, out, n, shape, wide):
    wide_a, wide_b, depth = shape
    for a in range(wide_a):
        for b in range(wide_b):
            slot = ((a * wide_b + b) % 8) * (PAD + depth)

            def store(k, part, piece):
                out[k, n, a, b, :, part * LANES : (part + 1) * LANES] = piece

            parted_tile(pick(a, b), wide, slot, store)


def part_scratch(depth, lanes):
    return pltpu.VMEM((lanes // LANES, 8 * (PAD + depth), LANES), F32)


def parted_volume(own, plane):
    vols, side_a, side_b, depth, lanes = own.shape
    out = jax.ShapeDtypeStruct((3, vols, side_a + 1, side_b, depth // 2, lanes), BF16)

    def kernel(own, plane, out, wide):
        def pick(a, b):
            return plane[0, 0, b] if a == 0 else own[0, a - 1, b]

        part_block(pick, out, 0, (side_a + 1, side_b, depth), wide)

    def block(shape):
        return pl.BlockSpec((1,) + shape[1:], lambda n: (n, 0, 0, 0, 0))

    return call(
        kernel,
        [out],
        (own, plane),
        [part_scratch(depth, lanes)],
        (vols,),
        [block(own.shape), block(plane.shape)],
        [pl.BlockSpec((3, 1) + out.shape[2:], lambda n: (0, n, 0, 0, 0, 0))],
    )[0]


def window(refs, i, j, sides):
    vols, side_a, cells_b = sides
    rows = []
    for n in range(vols):
        for a in range(side_a):
            for b in cells_b:
                y = 2 * b + j
                ref = refs[0]
                if len(refs) == 2:
                    ref, y = (refs[1], 0) if y == 0 else (refs[0], y - 1)
                assert 0 <= y < ref.shape[3]
                rows.append(jnp.concatenate([ref[k, n, 2 * a + i, y] for k in range(3)], axis=1))
    return jnp.concatenate(rows, axis=0)


def forward_total(orders, sides, refs, here, filters, acc):
    acc[...] = jnp.zeros_like(acc)

    def step(i, carry):
        for j in range(3):
            right = jnp.concatenate(
                [filter_tap(filters, here, i * 9 + j * 3 + k, orders) for k in range(3)], axis=1
            )
            acc[...] += dot(window(refs, i, j, sides), right, NT)
        return carry

    lax.fori_loop(0, 3, step, 0)
    return acc[...]


def leaky(total):
    return jnp.where(total > 0, total, 0.3 * total)


def forward(here, parts, filters, orders, cells_b, kind):
    main = parts[0]
    _, vols, wide_a, _, depth, inputs = main.shape
    sides = (vols, (wide_a - 1) // 2, cells_b)
    count = filters.shape[1] * filters.shape[3]
    cells = vols * sides[1] * len(cells_b) * depth
    outs = [jax.ShapeDtypeStruct((vols, sides[1], len(cells_b), depth, count), BF16)]
    scratch = [pltpu.VMEM((cells, count), F32)]
    if kind == "high":
        outs.append(jax.ShapeDtypeStruct((vols, 1, 1, depth, count), BF16))
    if kind == "low":
        high_b = parts[2].shape[2]
        outs.append(jax.ShapeDtypeStruct((vols, 1, 1 + high_b, depth, count), BF16))
        outs.append(jax.ShapeDtypeStruct(main.shape[:3] + (1,) + main.shape[4:], BF16))
        scratch.append(part_scratch(2 * depth, inputs))

    def kernel(here, filters, main, *rest):
        if kind == "low":
            row, above, out, plane, row_parts, acc, wide = rest

            def split(n, carry):
                part_block(lambda a, b: row[n, a, 0], row_parts, n, (wide_a, 1, 2 * depth), wide)
                return carry

            lax.fori_loop(0, vols, split, 0)
            refs = (main, row_parts)
        else:
            out, acc = rest[0], rest[-1]
            refs = (main, None) if kind == "high" else (main,)
        total = forward_total(orders, sides, refs, here, filters, acc)
        if kind != "out":
            total = leaky(total)
        value = total.astype(BF16).reshape(out.shape)
        out[...] = value
        if kind == "high":
            rest[1][...] = value[:, -1:, -1:]
        if kind == "low":
            plane[:, :, :1] = value[:, -1:]
            plane[:, :, 1:] = above[:, above.shape[1] - 1 :]

    return call(
        kernel,
        outs,
        (here, filters, *parts),
        scratch,
        flops=2 * cells * 27 * inputs * count,
    )


def grads_body(orders, sides, here, refs, keep, send, turned):
    count = turned.shape[0]
    inputs = refs[0].shape[5]
    pieces = inputs // LANES
    chans = 2 ** len(orders[1])
    mine = count // chans
    each = keep.shape[2] // pieces
    half = keep.shape[0]

    def put(ref, place, tap, part):
        for chan in range(chans):
            to = relative(chan, here[1], orders[1])
            for piece in range(pieces):
                lanes = slice(piece * LANES, (piece + 1) * LANES)
                ref[place, to, (tap % each) * pieces + piece] = part[chan * mine : (chan + 1) * mine, lanes]

    def step(i, carry):
        for j in range(3):
            part = dot(turned[...], window(refs, i, j, sides), NN).astype(BF16)
            for k in range(3):
                tap = i * 9 + j * 3 + k
                place = relative(tap // each, here[0], orders[0])
                piece = part[:, k * inputs : (k + 1) * inputs]

                @pl.when(place < half)
                def _():
                    put(keep, place, tap, piece)

                @pl.when(place >= half)
                def _():
                    put(send, place - half, tap, piece)

        return carry

    lax.fori_loop(0, 3, step, 0)
    blank = jnp.zeros((count, inputs), BF16)
    for tap in range(27, each * 2 * half):
        place = relative(tap // each, here[0], orders[0])

        @pl.when(place < half)
        def _():
            put(keep, place, tap, blank)

        @pl.when(place >= half)
        def _():
            put(send, place - half, tap, blank)


def grads_out(count, inputs, orders):
    space, chans = 2 ** len(orders[0]), 2 ** len(orders[1])
    each = -(-27 // space) * (inputs // LANES)
    return jax.ShapeDtypeStruct((space // 2, chans, each, count // chans, LANES), BF16)


def first_grads(here, refs, grads, orders):
    inputs = refs[0].shape[5]
    vols, side_a, side_b, depth, count = grads.shape
    sides = (vols, side_a, range(side_b))
    cells = vols * side_a * side_b * depth
    out = grads_out(count, inputs, orders)

    def kernel(here, grads, main, row, keep, send, turned):
        flat = grads[...].reshape(cells, count).astype(F32)
        turned[...] = jnp.transpose(flat, (1, 0)).astype(BF16)
        grads_body(orders, sides, here, (main, row), keep, send, turned)

    return call(
        kernel,
        [out, out],
        (here, grads, *refs),
        [pltpu.VMEM((count, cells), BF16)],
        flops=2 * cells * 27 * inputs * count,
    )


def second_grads(here, blocks, grads, orders):
    low, high = blocks[:2]
    side_x, deep, inputs = low.shape[1], low.shape[3], low.shape[4]
    wide_b = low.shape[2] + high.shape[2] + 1
    vols, side_a, side_b, depth = low.shape[0], side_x // 2, wide_b // 2, deep // 2
    chans, mine, cells = grads.shape
    count = chans * mine
    sides = (vols, side_a, range(side_b))
    out = grads_out(count, inputs, orders)
    parts = jax.ShapeDtypeStruct((3, vols, side_x + 1, wide_b, depth, inputs), BF16)

    def kernel(here, grads, low, high, plane, row, corner, keep, send, parts, turned, wide):
        def split(n, carry):
            def pick(a, b):
                if b == 0:
                    return corner[n, 0, 0] if a == 0 else row[n, a - 1, 0]
                if a == 0:
                    return plane[n, 0, b - 1]
                return low[n, a - 1, 0] if b == 1 else high[n, a - 1, b - 2]

            part_block(pick, parts, n, (side_x + 1, wide_b, deep), wide)
            return carry

        lax.fori_loop(0, vols, split, 0)
        for chan in range(chans):
            turned[chan * mine : (chan + 1) * mine] = grads[chan ^ here[1]]
        grads_body(orders, sides, here, (parts,), keep, send, turned)

    return call(
        kernel,
        [out, out, parts],
        (here, grads, *blocks),
        [pltpu.VMEM((count, cells), BF16), part_scratch(deep, inputs)],
        flops=2 * cells * 27 * inputs * count,
    )


def core_sum(keep, send):
    tail = keep.shape[2:]
    other = swapped(send, "space", 0)
    total = keep.astype(F32) + other.astype(F32)
    highs = bits("space") - 1
    return total.reshape((2,) * highs + (2, -1) + tail)


def half_sum(value, axis, bit, dim):
    keep = lax.index_in_dim(value, 0, dim, keepdims=False)
    send = lax.index_in_dim(value, 1, dim, keepdims=False)
    other = swapped(send.astype(BF16), axis, bit)
    return keep.astype(F32) + other.astype(F32)


def plain_sum(total):
    total = half_sum(total, "chan", 0, bits("space") - 1)
    for bit in range(1, bits("space")):
        total = half_sum(total, "space", bit, 0)
    return total


def far_sum(total):
    part = total[0].astype(F32)
    for m in range(1, lax.axis_size("chan") // 2):
        part = part + far_swapped(total[m].astype(BF16), m).astype(F32)
    return part.astype(BF16)


def mixed_sum(total):
    highs = list(range(1, bits("space")))
    cut = (total.shape[-3] + 1) // 2
    one, two = total[..., :cut, :, :], total[..., cut:, :, :]
    two = half_sum(two, "chan", 0, len(highs))
    for bit in highs:
        one = half_sum(one, "space", bit, 0)
    one = half_sum(one, "chan", 0, 0)
    for bit in highs:
        two = half_sum(two, "space", bit, 0)
    return jnp.concatenate([one, two], axis=-3)


def finish_sum(totals):
    space = lax.axis_size("space")
    part = merged = jnp.concatenate(totals, axis=0)
    for bit in high_bits():
        part = doubled(part, "space", bit)
    part = doubled(part, "space", 0)
    part = part.reshape((space,) + merged.shape)
    apart = [jnp.int32(s) ^ lax.axis_index("space") for s in range(space)]
    ordered = [lax.dynamic_index_in_dim(part, space_order(a), 0, keepdims=False) for a in apart]
    outs, begin = [], 0
    taps = -(-27 // space)
    for total in totals:
        rows, mine = total.shape[0], total.shape[1]
        pieces = rows // taps
        full = jnp.concatenate([o[begin : begin + rows] for o in ordered], axis=0)
        full = full.reshape(space * taps, pieces, mine, LANES)[:27].astype(F32)
        full = jnp.transpose(full, (0, 1, 3, 2)).reshape(3, 3, 3, pieces * LANES, mine)
        outs.append(full)
        begin += rows
    return outs


def space_order(apart):
    place = 0
    for bit in range(bits("space")):
        place = place * 2 + ((apart >> bit) & 1)
    return place


def stepped_tile(tile, wide, base, store):
    depth, lanes = tile.shape
    for part in range(lanes // LANES):
        rows = wide.at[part]
        rows[pl.ds(base + depth, PAD), :] = jnp.zeros((PAD, LANES), F32)
        rows[pl.ds(base, depth), :] = tile[:, part * LANES : (part + 1) * LANES].astype(F32)
        store(part, rows[pl.ds(base + 1, depth), :].astype(BF16))


def back_kernel(
    orders, here, near, beyond, filters, low, high, out, plane, row, corner, wide, cells, moved, spread
):
    vols, wide_a, wide_b, depth, count = cells.shape
    side_a, side_b = wide_a - 1, wide_b - 1
    inputs = filters.shape[4]
    chans = near.shape[1]
    for b in range(2):
        owner = (here[1] + b) & (chans - 1)
        for ref in (near, beyond):
            rows = jnp.concatenate([ref[b, chan ^ owner] for chan in range(chans)], axis=0)
            flat = jnp.transpose(rows.astype(F32), (1, 0)).astype(BF16)
            for n in range(vols):
                for a in range(side_a if ref is near else 1):
                    begin = (n * side_a + a) * depth
                    cells[n, a if ref is near else side_a, b] = flat[begin : begin + depth]
    for n in range(vols):
        for a in range(wide_a):
            for b in range(wide_b):
                slot = ((n * wide_a + a) * wide_b + b) % 8 * (PAD + depth)

                def store(part, piece):
                    moved[n, a, b, :, part * LANES : (part + 1) * LANES] = piece

                stepped_tile(cells[n, a, b], wide, slot, store)

    def lefts(ref, da, db):
        return ref[:, da : da + side_a, db : db + side_b].reshape(-1, count)

    for sa in range(2):
        for sb in range(2):
            even = odd = None
            for i, da in REACH[sa]:
                for j, db in REACH[sb]:
                    tap = (i * 3 + j) * 3
                    here_cells = lefts(cells, da, db)
                    first = dot(here_cells, filter_tap(filters, here, tap + 1, orders), NN)
                    second = dot(here_cells, filter_tap(filters, here, tap + 2, orders), NN)
                    second += dot(lefts(moved, da, db), filter_tap(filters, here, tap, orders), NN)
                    even = first if even is None else even + first
                    odd = second if odd is None else odd + second
            for parity, value in enumerate((even, odd)):
                value = value.reshape(vols, side_a, side_b, depth, inputs)
                for n in range(vols):
                    for a in range(side_a):
                        for b in range(side_b):
                            for part in range(inputs // LANES):
                                spread[
                                    part, n, 2 * a + sa, 2 * b + sb, pl.ds(parity, depth, stride=2), :
                                ] = value[n, a, b, :, part * LANES : (part + 1) * LANES]
    for part in range(inputs // LANES):
        lanes = slice(part * LANES, (part + 1) * LANES)
        act = jnp.concatenate([low[:, :, :, :, lanes], high[:, :, :, :, lanes]], axis=2)
        act = act.astype(F32)
        value = (spread[part] * jnp.where(act > 0, 1.0, 0.3)).astype(BF16)
        out[:, :, :, :, lanes] = value
        plane[:, :, :, :, lanes] = value[:, :1]
        row[:, :, :, :, lanes] = value[:, :, :1]
        corner[:, :, :, :, lanes] = value[:, :1, :1]


def hidden_back(here, near, beyond, filters, low, high, orders):
    inputs = low.shape[-1]
    shape = low.shape[:2] + (low.shape[2] + high.shape[2],) + low.shape[3:]
    vols, depth = shape[0], shape[3] // 2
    count = near.shape[1] * near.shape[2]
    ext = (vols, shape[1] // 2 + 1, shape[2] // 2 + 1, depth, count)
    outs = [
        jax.ShapeDtypeStruct(shape, BF16),
        jax.ShapeDtypeStruct((vols, 1) + shape[2:], BF16),
        jax.ShapeDtypeStruct(shape[:2] + (1,) + shape[3:], BF16),
        jax.ShapeDtypeStruct((vols, 1, 1) + shape[3:], BF16),
    ]
    return call(
        functools.partial(back_kernel, orders),
        outs,
        (here, near, beyond, filters, low, high),
        [
            pltpu.VMEM((count // LANES, 8 * (PAD + depth), LANES), F32),
            pltpu.VMEM(ext, BF16),
            pltpu.VMEM(ext, BF16),
            pltpu.VMEM((inputs // LANES,) + shape[:4] + (LANES,), F32),
        ],
        flops=2 * vols * (ext[1] - 1) * (ext[2] - 1) * depth * 27 * inputs * count,
    )


def volume_kernel(orders, here, cells, plane, row, filters, out, wide, ext, moved, spread):
    _, side_a, side_b, depth, count = cells.shape
    inputs = filters.shape[4]
    for a in range(side_a + 1):
        for b in range(side_b + 1):
            if b == side_b:
                tile = row[0, a, 0]
            elif a == side_a:
                tile = plane[0, 0, b]
            else:
                tile = cells[0, a, b]
            ext[a, b] = tile
            slot = ((a * (side_b + 1) + b) % 8) * (PAD + depth)

            def store(part, piece):
                moved[a, b, :, part * LANES : (part + 1) * LANES] = piece

            stepped_tile(tile, wide, slot, store)

    def lefts(ref, da, db):
        return ref[da : da + side_a, db : db + side_b].reshape(-1, count)

    for sa in range(2):
        for sb in range(2):
            both = late = None
            for i, da in REACH[sa]:
                for j, db in REACH[sb]:
                    tap = (i * 3 + j) * 3
                    pair = jnp.concatenate(
                        [filter_tap(filters, here, tap + k, orders) for k in (1, 2)], axis=1
                    )
                    first = dot(lefts(ext, da, db), pair, NN)
                    second = dot(lefts(moved, da, db), filter_tap(filters, here, tap, orders), NN)
                    both = first if both is None else both + first
                    late = second if late is None else late + second
            halves = (both[:, :inputs], both[:, inputs:] + late)
            for parity, value in enumerate(halves):
                value = value.reshape(side_a, side_b, depth, inputs)
                for a in range(side_a):
                    for b in range(side_b):
                        spread[2 * a + sa, 2 * b + sb, pl.ds(parity, depth, stride=2), :] = value[a, b]
    out[0] = spread[...].astype(BF16)


def volume_grads(here, cells, plane, row, filters, orders):
    vols, side_a, side_b, depth, count = cells.shape
    inputs = filters.shape[4]
    out = jax.ShapeDtypeStruct((vols, 2 * side_a, 2 * side_b, 2 * depth, inputs), BF16)

    def block(shape):
        return pl.BlockSpec((1,) + shape[1:], lambda n: (n, 0, 0, 0, 0))

    return call(
        functools.partial(volume_kernel, orders),
        [out],
        (here, cells, plane, row, filters),
        [
            pltpu.VMEM((count // LANES, 8 * (PAD + depth), LANES), F32),
            pltpu.VMEM((side_a + 1, side_b + 1, depth, count), BF16),
            pltpu.VMEM((side_a + 1, side_b + 1, depth, count), BF16),
            pltpu.VMEM((2 * side_a, 2 * side_b, 2 * depth, inputs), F32),
        ],
        (vols,),
        [
            pl.BlockSpec(memory_space=pltpu.SMEM),
            block(cells.shape),
            block(plane.shape),
            block(row.shape),
            pl.BlockSpec(memory_space=pltpu.VMEM),
        ],
        [block(out.shape)],
        flops=2 * vols * side_a * side_b * depth * 27 * inputs * count,
    )[0]


class CellExchange:
    def __init__(self, cotangent):
        vols, side_a, side_b, side_c, mine = cotangent.shape
        self.count = bits("chan")
        assert side_b == 2**self.count
        flat = jnp.transpose(cotangent, (2, 4, 0, 1, 3))
        self.value = flat.reshape((2,) * self.count + (mine, vols * side_a * side_c))
        self.open = list(reversed(range(self.count)))

    def stage(self, bit):
        dim = self.open.index(bit)
        mine = (lax.axis_index("chan") >> bit) & 1
        keep = lax.dynamic_index_in_dim(self.value, mine, dim, keepdims=False)
        send = lax.dynamic_index_in_dim(self.value, 1 - mine, dim, keepdims=False)
        other = swapped(send, "chan", bit)
        self.value = jnp.stack([keep, other], axis=self.count - 1)
        self.open.remove(bit)

    def finish(self):
        own = self.value.reshape((2**self.count,) + self.value.shape[self.count :])
        near = jnp.stack([own, shifted(own, (0, -1))])
        return own, near, shifted(near, (-1, 0))


def local(volume, w_first, w_second, cotangent):
    here = position()
    orders = (list(range(bits("space"))), [0] + far_bits())
    side_b = volume.shape[2] // 2

    plane = shifted(volume[:, -1:], (1, 0))
    part = far_gather(own_part(w_first))
    first_full = near_gather(doubled(part, "chan", 0))
    row = jnp.concatenate([plane, volume], axis=1)[:, :, -1:]
    row = shifted(row, (0, 1))
    part = far_gather(own_part(w_second))
    second_full = near_gather(doubled(part, "chan", 0))
    cells = CellExchange(cotangent)
    for bit in far_bits() + [0]:
        cells.stage(bit)
    own_cells, near_cells, beyond_cells = cells.finish()

    vol_main = parted_volume(volume, plane)
    high, corner = forward(here, (vol_main,), first_full, orders, range(1, side_b), "high")
    low, hid_plane, vol_row = forward(here, (vol_main, row, high), first_full, orders, range(1), "low")
    hid_row = shifted(high[:, :, -1:], (0, 1))
    hid_corner = shifted(corner, (1, 1))
    hid_plane = shifted(hid_plane, (1, 0))
    blocks = (low, high, hid_plane, hid_row, hid_corner)
    keep, send, act_parts = second_grads(here, blocks, own_cells, orders)
    second_sum = far_sum(mixed_sum(core_sum(keep, send)))

    pre_back, pre_plane, pre_row, corner = hidden_back(here, near_cells, beyond_cells, second_full, low, high, orders)
    keep, send = first_grads(here, (vol_main, vol_row), pre_back, orders)
    first_sum = far_sum(plain_sum(core_sum(keep, send)))
    first_grad, second_grad = finish_sum([first_sum, second_sum])
    plane = shifted(pre_plane, (-1, 0))
    row = shifted(pre_row, (0, -1))
    corner = shifted(corner, (-1, -1))
    row = jnp.concatenate([row, corner], axis=1)
    out_b = range(act_parts.shape[3] // 2)
    (local_out,) = forward(here, (act_parts,), second_full, orders, out_b, "out")
    second_out = lax.all_to_all(local_out, "chan", split_axis=4, concat_axis=2, tiled=True)
    volume_grad = volume_grads(here, pre_back, plane, row, first_full, orders)
    return (second_out, volume_grad, first_grad, second_grad)


def solution(mesh):
    return jax.shard_map(
        local,
        mesh=mesh,
        in_specs=(
            P(None, "space", "chan", None, None),
            P(None, None, None, None, "chan"),
            P(None, None, None, None, "chan"),
            P(None, "space", None, None, "chan"),
        ),
        out_specs=(
            P(None, "space", None, None, "chan"),
            P(None, "space", "chan", None, None),
            P(None, None, None, None, "chan"),
            P(None, None, None, None, "chan"),
        ),
        check_vma=False,
    )
```

```python
import functools

import jax
import jax.numpy as jnp
from jax import lax
from jax.experimental import pallas as pl
from jax.experimental.pallas import tpu as pltpu
from jax.sharding import PartitionSpec as P


SPACE, CHAN = ("space", "chan")
BF16 = jnp.bfloat16
F32 = jnp.float32
LANES = 128
PAD = 8
NT = (((1,), (1,)), ((), ()))
NN = (((1,), (0,)), ((), ()))
REACH = (((1, 0),), ((0, 1), (2, 0)))


def dot(left, right, dims):
    return lax.dot_general(left, right, dims, preferred_element_type=F32)


def bits(axis):
    return lax.axis_size(axis).bit_length() - 1


def shifted(value, steps):
    pairs = []
    sizes = (lax.axis_size(SPACE), lax.axis_size(CHAN))
    for a in range(sizes[0]):
        for b in range(sizes[1]):
            to = (a + steps[0], b + steps[1])
            if 0 <= to[0] < sizes[0] and 0 <= to[1] < sizes[1]:
                pairs.append((a * sizes[1] + b, to[0] * sizes[1] + to[1]))
    return lax.ppermute(value, (SPACE, CHAN), pairs)


def swapped(value, axis, bit):
    count = lax.axis_size(axis)
    return lax.ppermute(value, axis, [(i, i ^ (1 << bit)) for i in range(count)])


def doubled(value, axis, bit):
    other = swapped(value, axis, bit)
    return jnp.stack([value, other])


def position():
    return jnp.stack([lax.axis_index(SPACE), lax.axis_index(CHAN)]).astype(jnp.int32)


def own_part(shard):
    space = lax.axis_size(SPACE)
    edge, inputs, mine = shard.shape[0], shard.shape[3], shard.shape[4]
    taps = edge**3
    each = -(-taps // space)
    flat = jnp.transpose(shard.reshape(taps, inputs, mine), (0, 2, 1))
    flat = jnp.pad(flat, ((0, each * space - taps), (0, 0), (0, 0)))
    return lax.dynamic_slice_in_dim(flat, lax.axis_index(SPACE) * each, each, 0)


def far_bits():
    return list(reversed(range(1, bits(CHAN))))


def high_bits():
    return list(reversed(range(1, bits(SPACE))))


def far_swapped(value, mask):
    count = lax.axis_size(CHAN)
    return lax.ppermute(value, CHAN, [(i, i ^ (mask << 1)) for i in range(count)])


def far_gather(part):
    others = [far_swapped(part, m) for m in range(1, lax.axis_size(CHAN) // 2)]
    return jnp.stack([part, *others])


def near_gather(part):
    each, mine, inputs = part.shape[-3:]
    for bit in high_bits():
        part = doubled(part, SPACE, bit)
    part = doubled(part, SPACE, 0)
    return part.reshape(lax.axis_size(SPACE), lax.axis_size(CHAN), each, mine, inputs)


def mixed_gather(part):
    each, mine, inputs = part.shape[-3:]
    highs = len(high_bits())
    cut = (each + 1) // 2
    one, two = part[..., :cut, :, :], part[..., cut:, :, :]
    one = doubled(one, CHAN, 0)
    for bit in high_bits():
        two = doubled(two, SPACE, bit)
    for bit in high_bits():
        one = doubled(one, SPACE, bit)
    two = doubled(two, CHAN, 0)
    whole = jnp.concatenate([one, jnp.moveaxis(two, 0, highs)], axis=-3)
    whole = doubled(whole, SPACE, 0)
    return whole.reshape(lax.axis_size(SPACE), lax.axis_size(CHAN), each, mine, inputs)


def relative(index, mine, order):
    apart = index ^ mine
    place = 0
    for bit in order:
        place = place * 2 + ((apart >> bit) & 1)
    return place


def filter_tap(ref, here, tap, orders):
    each = ref.shape[2]
    owner = relative(tap // each, here[0], orders[0])
    rows = [
        ref[owner, relative(chan, here[1], orders[1]), tap % each]
        for chan in range(ref.shape[1])
    ]
    return jnp.concatenate(rows, axis=0)


def scratch_avals(scratch):
    return [jax.ShapeDtypeStruct(ref.inner_aval.shape, ref.inner_aval.dtype) for ref in scratch]


def call(kernel, outs, args, scratch=(), grid=None, in_specs=None, out_specs=None, flops=0):
    moved = sum(a.size * a.dtype.itemsize for a in args)
    moved += sum(o.size * o.dtype.itemsize for o in outs)
    used = sum(v.size * v.dtype.itemsize for v in scratch_avals(scratch))
    grant = min(56 * 2**20, moved + used + 6 * 2**20)
    whole = pl.BlockSpec(memory_space=pltpu.VMEM)
    smem = pl.BlockSpec(memory_space=pltpu.SMEM)
    specs = in_specs or [smem if a.dtype == jnp.int32 else whole for a in args]
    return pl.pallas_call(
        kernel,
        out_shape=outs,
        grid=grid or (),
        in_specs=specs,
        out_specs=out_specs or [whole] * len(outs),
        scratch_shapes=scratch,
        cost_estimate=pl.CostEstimate(flops=flops, bytes_accessed=moved, transcendentals=0),
        compiler_params=pltpu.CompilerParams(vmem_limit_bytes=grant),
    )(*args)


def parted_tile(tile, wide, base, store):
    depth, lanes = tile.shape
    for part in range(lanes // LANES):
        rows = wide.at[part]
        rows[pl.ds(base, PAD), :] = jnp.zeros((PAD, LANES), F32)
        rows[pl.ds(base + PAD, depth), :] = tile[:, part * LANES : (part + 1) * LANES].astype(F32)
        for k in range(3):
            piece = rows[pl.ds(base + PAD - 1 + k, depth // 2, stride=2), :]
            store(k, part, piece.astype(BF16))


def part_block(pick, out, n, shape, wide):
    wide_a, wide_b, depth = shape
    for a in range(wide_a):
        for b in range(wide_b):
            slot = ((a * wide_b + b) % 8) * (PAD + depth)

            def store(k, part, piece):
                out[k, n, a, b, :, part * LANES : (part + 1) * LANES] = piece

            parted_tile(pick(a, b), wide, slot, store)


def part_scratch(depth, lanes):
    return pltpu.VMEM((lanes // LANES, 8 * (PAD + depth), LANES), F32)


def parted_volume(own, plane):
    vols, side_a, side_b, depth, lanes = own.shape
    out = jax.ShapeDtypeStruct((3, vols, side_a + 1, side_b, depth // 2, lanes), BF16)

    def kernel(own, plane, out, wide):
        def pick(a, b):
            return plane[0, 0, b] if a == 0 else own[0, a - 1, b]

        part_block(pick, out, 0, (side_a + 1, side_b, depth), wide)

    def block(shape):
        return pl.BlockSpec((1,) + shape[1:], lambda n: (n, 0, 0, 0, 0))

    return call(
        kernel,
        [out],
        (own, plane),
        [part_scratch(depth, lanes)],
        (vols,),
        [block(own.shape), block(plane.shape)],
        [pl.BlockSpec((3, 1) + out.shape[2:], lambda n: (0, n, 0, 0, 0, 0))],
    )[0]


def window(refs, i, j, sides):
    vols, side_a, cells_b = sides
    rows = []
    for n in range(vols):
        for a in range(side_a):
            for b in cells_b:
                y = 2 * b + j
                ref = refs[0]
                if len(refs) == 2:
                    ref, y = (refs[1], 0) if y == 0 else (refs[0], y - 1)
                assert 0 <= y < ref.shape[3]
                rows.append(jnp.concatenate([ref[k, n, 2 * a + i, y] for k in range(3)], axis=1))
    return jnp.concatenate(rows, axis=0)


def forward_total(orders, sides, refs, here, filters, acc):
    acc[...] = jnp.zeros_like(acc)

    def step(i, carry):
        for j in range(3):
            right = jnp.concatenate(
                [filter_tap(filters, here, i * 9 + j * 3 + k, orders) for k in range(3)], axis=1
            )
            acc[...] += dot(window(refs, i, j, sides), right, NT)
        return carry

    lax.fori_loop(0, 3, step, 0)
    return acc[...]


def leaky(total):
    return jnp.where(total > 0, total, 0.3 * total)


def forward(here, parts, filters, orders, cells_b, kind):
    main = parts[0]
    _, vols, wide_a, _, depth, inputs = main.shape
    sides = (vols, (wide_a - 1) // 2, cells_b)
    count = filters.shape[1] * filters.shape[3]
    cells = vols * sides[1] * len(cells_b) * depth
    outs = [jax.ShapeDtypeStruct((vols, sides[1], len(cells_b), depth, count), BF16)]
    scratch = [pltpu.VMEM((cells, count), F32)]
    if kind == "h":
        outs.append(jax.ShapeDtypeStruct((vols, 1, 1, depth, count), BF16))
    if kind == "l":
        high_b = parts[2].shape[2]
        outs.append(jax.ShapeDtypeStruct((vols, 1, 1 + high_b, depth, count), BF16))
        outs.append(jax.ShapeDtypeStruct(main.shape[:3] + (1,) + main.shape[4:], BF16))
        scratch.append(part_scratch(2 * depth, inputs))

    def kernel(here, filters, main, *rest):
        if kind == "l":
            row, above, out, plane, row_parts, acc, wide = rest

            def split(n, carry):
                part_block(lambda a, b: row[n, a, 0], row_parts, n, (wide_a, 1, 2 * depth), wide)
                return carry

            lax.fori_loop(0, vols, split, 0)
            refs = (main, row_parts)
        else:
            out, acc = rest[0], rest[-1]
            refs = (main, None) if kind == "h" else (main,)
        total = forward_total(orders, sides, refs, here, filters, acc)
        if kind != "u":
            total = leaky(total)
        value = total.astype(BF16).reshape(out.shape)
        out[...] = value
        if kind == "h":
            rest[1][...] = value[:, -1:, -1:]
        if kind == "l":
            plane[:, :, :1] = value[:, -1:]
            plane[:, :, 1:] = above[:, above.shape[1] - 1 :]

    return call(
        kernel,
        outs,
        (here, filters, *parts),
        scratch,
        flops=2 * cells * 27 * inputs * count,
    )


def grads_body(orders, sides, here, refs, keep, send, turned):
    count = turned.shape[0]
    inputs = refs[0].shape[5]
    pieces = inputs // LANES
    chans = 2 ** len(orders[1])
    mine = count // chans
    each = keep.shape[2] // pieces
    half = keep.shape[0]

    def put(ref, place, tap, part):
        for chan in range(chans):
            to = relative(chan, here[1], orders[1])
            for piece in range(pieces):
                lanes = slice(piece * LANES, (piece + 1) * LANES)
                ref[place, to, (tap % each) * pieces + piece] = part[chan * mine : (chan + 1) * mine, lanes]

    def step(i, carry):
        for j in range(3):
            part = dot(turned[...], window(refs, i, j, sides), NN).astype(BF16)
            for k in range(3):
                tap = i * 9 + j * 3 + k
                place = relative(tap // each, here[0], orders[0])
                piece = part[:, k * inputs : (k + 1) * inputs]

                @pl.when(place < half)
                def _():
                    put(keep, place, tap, piece)

                @pl.when(place >= half)
                def _():
                    put(send, place - half, tap, piece)

        return carry

    lax.fori_loop(0, 3, step, 0)
    blank = jnp.zeros((count, inputs), BF16)
    for tap in range(27, each * 2 * half):
        place = relative(tap // each, here[0], orders[0])

        @pl.when(place < half)
        def _():
            put(keep, place, tap, blank)

        @pl.when(place >= half)
        def _():
            put(send, place - half, tap, blank)


def grads_out(count, inputs, orders):
    space, chans = 2 ** len(orders[0]), 2 ** len(orders[1])
    each = -(-27 // space) * (inputs // LANES)
    return jax.ShapeDtypeStruct((space // 2, chans, each, count // chans, LANES), BF16)


def first_grads(here, refs, grads, orders):
    inputs = refs[0].shape[5]
    vols, side_a, side_b, depth, count = grads.shape
    sides = (vols, side_a, range(side_b))
    cells = vols * side_a * side_b * depth
    out = grads_out(count, inputs, orders)

    def kernel(here, grads, main, row, keep, send, turned):
        flat = grads[...].reshape(cells, count).astype(F32)
        turned[...] = jnp.transpose(flat, (1, 0)).astype(BF16)
        grads_body(orders, sides, here, (main, row), keep, send, turned)

    return call(
        kernel,
        [out, out],
        (here, grads, *refs),
        [pltpu.VMEM((count, cells), BF16)],
        flops=2 * cells * 27 * inputs * count,
    )


def second_grads(here, blocks, grads, orders):
    low, high = blocks[:2]
    side_x, deep, inputs = low.shape[1], low.shape[3], low.shape[4]
    wide_b = low.shape[2] + high.shape[2] + 1
    vols, side_a, side_b, depth = low.shape[0], side_x // 2, wide_b // 2, deep // 2
    chans, mine, cells = grads.shape
    count = chans * mine
    sides = (vols, side_a, range(side_b))
    out = grads_out(count, inputs, orders)
    parts = jax.ShapeDtypeStruct((3, vols, side_x + 1, wide_b, depth, inputs), BF16)

    def kernel(here, grads, low, high, plane, row, corner, keep, send, parts, turned, wide):
        def split(n, carry):
            def pick(a, b):
                if b == 0:
                    return corner[n, 0, 0] if a == 0 else row[n, a - 1, 0]
                if a == 0:
                    return plane[n, 0, b - 1]
                return low[n, a - 1, 0] if b == 1 else high[n, a - 1, b - 2]

            part_block(pick, parts, n, (side_x + 1, wide_b, deep), wide)
            return carry

        lax.fori_loop(0, vols, split, 0)
        for chan in range(chans):
            turned[chan * mine : (chan + 1) * mine] = grads[chan ^ here[1]]
        grads_body(orders, sides, here, (parts,), keep, send, turned)

    return call(
        kernel,
        [out, out, parts],
        (here, grads, *blocks),
        [pltpu.VMEM((count, cells), BF16), part_scratch(deep, inputs)],
        flops=2 * cells * 27 * inputs * count,
    )


def core_sum(keep, send):
    tail = keep.shape[2:]
    other = swapped(send, SPACE, 0)
    total = keep.astype(F32) + other.astype(F32)
    highs = bits(SPACE) - 1
    return total.reshape((2,) * highs + (2, -1) + tail)


def half_sum(value, axis, bit, dim):
    keep = lax.index_in_dim(value, 0, dim, keepdims=False)
    send = lax.index_in_dim(value, 1, dim, keepdims=False)
    other = swapped(send.astype(BF16), axis, bit)
    return keep.astype(F32) + other.astype(F32)


def plain_sum(total):
    total = half_sum(total, CHAN, 0, bits(SPACE) - 1)
    for bit in range(1, bits(SPACE)):
        total = half_sum(total, SPACE, bit, 0)
    return total


def far_sum(total):
    part = total[0].astype(F32)
    for m in range(1, lax.axis_size(CHAN) // 2):
        part = part + far_swapped(total[m].astype(BF16), m).astype(F32)
    return part.astype(BF16)


def mixed_sum(total):
    highs = list(range(1, bits(SPACE)))
    cut = (total.shape[-3] + 1) // 2
    one, two = total[..., :cut, :, :], total[..., cut:, :, :]
    two = half_sum(two, CHAN, 0, len(highs))
    for bit in highs:
        one = half_sum(one, SPACE, bit, 0)
    one = half_sum(one, CHAN, 0, 0)
    for bit in highs:
        two = half_sum(two, SPACE, bit, 0)
    return jnp.concatenate([one, two], axis=-3)


def finish_sum(totals):
    space = lax.axis_size(SPACE)
    part = merged = jnp.concatenate(totals, axis=0)
    for bit in high_bits():
        part = doubled(part, SPACE, bit)
    part = doubled(part, SPACE, 0)
    part = part.reshape((space,) + merged.shape)
    apart = [jnp.int32(s) ^ lax.axis_index(SPACE) for s in range(space)]
    ordered = [lax.dynamic_index_in_dim(part, space_order(a), 0, keepdims=False) for a in apart]
    outs, begin = [], 0
    taps = -(-27 // space)
    for total in totals:
        rows, mine = total.shape[0], total.shape[1]
        pieces = rows // taps
        full = jnp.concatenate([o[begin : begin + rows] for o in ordered], axis=0)
        full = full.reshape(space * taps, pieces, mine, LANES)[:27].astype(F32)
        full = jnp.transpose(full, (0, 1, 3, 2)).reshape(3, 3, 3, pieces * LANES, mine)
        outs.append(full)
        begin += rows
    return outs


def space_order(apart):
    place = 0
    for bit in range(bits(SPACE)):
        place = place * 2 + ((apart >> bit) & 1)
    return place


def stepped_tile(tile, wide, base, store):
    depth, lanes = tile.shape
    for part in range(lanes // LANES):
        rows = wide.at[part]
        rows[pl.ds(base + depth, PAD), :] = jnp.zeros((PAD, LANES), F32)
        rows[pl.ds(base, depth), :] = tile[:, part * LANES : (part + 1) * LANES].astype(F32)
        store(part, rows[pl.ds(base + 1, depth), :].astype(BF16))


def back_kernel(
    orders, here, near, beyond, filters, low, high, out, plane, row, corner, wide, cells, moved, spread
):
    vols, wide_a, wide_b, depth, count = cells.shape
    side_a, side_b = wide_a - 1, wide_b - 1
    inputs = filters.shape[4]
    chans = near.shape[1]
    for b in range(2):
        owner = (here[1] + b) & (chans - 1)
        for ref in (near, beyond):
            rows = jnp.concatenate([ref[b, chan ^ owner] for chan in range(chans)], axis=0)
            flat = jnp.transpose(rows.astype(F32), (1, 0)).astype(BF16)
            for n in range(vols):
                for a in range(side_a if ref is near else 1):
                    begin = (n * side_a + a) * depth
                    cells[n, a if ref is near else side_a, b] = flat[begin : begin + depth]
    for n in range(vols):
        for a in range(wide_a):
            for b in range(wide_b):
                slot = ((n * wide_a + a) * wide_b + b) % 8 * (PAD + depth)

                def store(part, piece):
                    moved[n, a, b, :, part * LANES : (part + 1) * LANES] = piece

                stepped_tile(cells[n, a, b], wide, slot, store)

    def lefts(ref, da, db):
        return ref[:, da : da + side_a, db : db + side_b].reshape(-1, count)

    for sa in range(2):
        for sb in range(2):
            even = odd = None
            for i, da in REACH[sa]:
                for j, db in REACH[sb]:
                    tap = (i * 3 + j) * 3
                    here_cells = lefts(cells, da, db)
                    first = dot(here_cells, filter_tap(filters, here, tap + 1, orders), NN)
                    second = dot(here_cells, filter_tap(filters, here, tap + 2, orders), NN)
                    second += dot(lefts(moved, da, db), filter_tap(filters, here, tap, orders), NN)
                    even = first if even is None else even + first
                    odd = second if odd is None else odd + second
            for parity, value in enumerate((even, odd)):
                value = value.reshape(vols, side_a, side_b, depth, inputs)
                for n in range(vols):
                    for a in range(side_a):
                        for b in range(side_b):
                            for part in range(inputs // LANES):
                                spread[
                                    part, n, 2 * a + sa, 2 * b + sb, pl.ds(parity, depth, stride=2), :
                                ] = value[n, a, b, :, part * LANES : (part + 1) * LANES]
    for part in range(inputs // LANES):
        lanes = slice(part * LANES, (part + 1) * LANES)
        act = jnp.concatenate([low[:, :, :, :, lanes], high[:, :, :, :, lanes]], axis=2)
        act = act.astype(F32)
        value = (spread[part] * jnp.where(act > 0, 1.0, 0.3)).astype(BF16)
        out[:, :, :, :, lanes] = value
        plane[:, :, :, :, lanes] = value[:, :1]
        row[:, :, :, :, lanes] = value[:, :, :1]
        corner[:, :, :, :, lanes] = value[:, :1, :1]


def hidden_back(here, near, beyond, filters, low, high, orders):
    inputs = low.shape[-1]
    shape = low.shape[:2] + (low.shape[2] + high.shape[2],) + low.shape[3:]
    vols, depth = shape[0], shape[3] // 2
    count = near.shape[1] * near.shape[2]
    ext = (vols, shape[1] // 2 + 1, shape[2] // 2 + 1, depth, count)
    outs = [
        jax.ShapeDtypeStruct(shape, BF16),
        jax.ShapeDtypeStruct((vols, 1) + shape[2:], BF16),
        jax.ShapeDtypeStruct(shape[:2] + (1,) + shape[3:], BF16),
        jax.ShapeDtypeStruct((vols, 1, 1) + shape[3:], BF16),
    ]
    return call(
        functools.partial(back_kernel, orders),
        outs,
        (here, near, beyond, filters, low, high),
        [
            pltpu.VMEM((count // LANES, 8 * (PAD + depth), LANES), F32),
            pltpu.VMEM(ext, BF16),
            pltpu.VMEM(ext, BF16),
            pltpu.VMEM((inputs // LANES,) + shape[:4] + (LANES,), F32),
        ],
        flops=2 * vols * (ext[1] - 1) * (ext[2] - 1) * depth * 27 * inputs * count,
    )


def volume_kernel(orders, here, cells, plane, row, filters, out, wide, ext, moved, spread):
    _, side_a, side_b, depth, count = cells.shape
    inputs = filters.shape[4]
    for a in range(side_a + 1):
        for b in range(side_b + 1):
            if b == side_b:
                tile = row[0, a, 0]
            elif a == side_a:
                tile = plane[0, 0, b]
            else:
                tile = cells[0, a, b]
            ext[a, b] = tile
            slot = ((a * (side_b + 1) + b) % 8) * (PAD + depth)

            def store(part, piece):
                moved[a, b, :, part * LANES : (part + 1) * LANES] = piece

            stepped_tile(tile, wide, slot, store)

    def lefts(ref, da, db):
        return ref[da : da + side_a, db : db + side_b].reshape(-1, count)

    for sa in range(2):
        for sb in range(2):
            both = late = None
            for i, da in REACH[sa]:
                for j, db in REACH[sb]:
                    tap = (i * 3 + j) * 3
                    pair = jnp.concatenate(
                        [filter_tap(filters, here, tap + k, orders) for k in (1, 2)], axis=1
                    )
                    first = dot(lefts(ext, da, db), pair, NN)
                    second = dot(lefts(moved, da, db), filter_tap(filters, here, tap, orders), NN)
                    both = first if both is None else both + first
                    late = second if late is None else late + second
            halves = (both[:, :inputs], both[:, inputs:] + late)
            for parity, value in enumerate(halves):
                value = value.reshape(side_a, side_b, depth, inputs)
                for a in range(side_a):
                    for b in range(side_b):
                        spread[2 * a + sa, 2 * b + sb, pl.ds(parity, depth, stride=2), :] = value[a, b]
    out[0] = spread[...].astype(BF16)


def volume_grads(here, cells, plane, row, filters, orders):
    vols, side_a, side_b, depth, count = cells.shape
    inputs = filters.shape[4]
    out = jax.ShapeDtypeStruct((vols, 2 * side_a, 2 * side_b, 2 * depth, inputs), BF16)

    def block(shape):
        return pl.BlockSpec((1,) + shape[1:], lambda n: (n, 0, 0, 0, 0))

    return call(
        functools.partial(volume_kernel, orders),
        [out],
        (here, cells, plane, row, filters),
        [
            pltpu.VMEM((count // LANES, 8 * (PAD + depth), LANES), F32),
            pltpu.VMEM((side_a + 1, side_b + 1, depth, count), BF16),
            pltpu.VMEM((side_a + 1, side_b + 1, depth, count), BF16),
            pltpu.VMEM((2 * side_a, 2 * side_b, 2 * depth, inputs), F32),
        ],
        (vols,),
        [
            pl.BlockSpec(memory_space=pltpu.SMEM),
            block(cells.shape),
            block(plane.shape),
            block(row.shape),
            pl.BlockSpec(memory_space=pltpu.VMEM),
        ],
        [block(out.shape)],
        flops=2 * vols * side_a * side_b * depth * 27 * inputs * count,
    )[0]


class CellExchange:
    def __init__(self, cotangent):
        vols, side_a, side_b, side_c, mine = cotangent.shape
        self.count = bits(CHAN)
        assert side_b == 2**self.count
        flat = jnp.transpose(cotangent, (2, 4, 0, 1, 3))
        self.value = flat.reshape((2,) * self.count + (mine, vols * side_a * side_c))
        self.open = list(reversed(range(self.count)))

    def stage(self, bit):
        dim = self.open.index(bit)
        mine = (lax.axis_index(CHAN) >> bit) & 1
        keep = lax.dynamic_index_in_dim(self.value, mine, dim, keepdims=False)
        send = lax.dynamic_index_in_dim(self.value, 1 - mine, dim, keepdims=False)
        other = swapped(send, CHAN, bit)
        self.value = jnp.stack([keep, other], axis=self.count - 1)
        self.open.remove(bit)

    def finish(self):
        own = self.value.reshape((2**self.count,) + self.value.shape[self.count :])
        near = jnp.stack([own, shifted(own, (0, -1))])
        return own, near, shifted(near, (-1, 0))


def local(volume, w_first, w_second, cotangent):
    here = position()
    orders = (list(range(bits(SPACE))), [0] + far_bits())
    side_b = volume.shape[2] // 2

    plane = shifted(volume[:, -1:], (1, 0))
    part = far_gather(own_part(w_first))
    first_full = near_gather(doubled(part, CHAN, 0))
    row = jnp.concatenate([plane, volume], axis=1)[:, :, -1:]
    row = shifted(row, (0, 1))
    part = far_gather(own_part(w_second))
    second_full = mixed_gather(part)
    cells = CellExchange(cotangent)
    for bit in far_bits() + [0]:
        cells.stage(bit)
    own_cells, near_cells, beyond_cells = cells.finish()

    vol_main = parted_volume(volume, plane)
    high, corner = forward(here, (vol_main,), first_full, orders, range(1, side_b), "h")
    low, hid_plane, vol_row = forward(here, (vol_main, row, high), first_full, orders, range(1), "l")
    hid_row = shifted(high[:, :, -1:], (0, 1))
    hid_corner = shifted(corner, (1, 1))
    hid_plane = shifted(hid_plane, (1, 0))
    blocks = (low, high, hid_plane, hid_row, hid_corner)
    keep, send, act_parts = second_grads(here, blocks, own_cells, orders)
    second_sum = far_sum(mixed_sum(core_sum(keep, send)))

    pre_back, pre_plane, pre_row, corner = hidden_back(
        here, near_cells, beyond_cells, second_full, low, high, orders
    )
    keep, send = first_grads(here, (vol_main, vol_row), pre_back, orders)
    first_sum = far_sum(plain_sum(core_sum(keep, send)))
    first_grad, second_grad = finish_sum([first_sum, second_sum])
    plane = shifted(pre_plane, (-1, 0))
    row = shifted(pre_row, (0, -1))
    corner = shifted(corner, (-1, -1))
    row = jnp.concatenate([row, corner], axis=1)
    out_b = range(act_parts.shape[3] // 2)
    (local_out,) = forward(here, (act_parts,), second_full, orders, out_b, "u")
    second_out = lax.all_to_all(local_out, CHAN, split_axis=4, concat_axis=2, tiled=True)
    volume_grad = volume_grads(here, pre_back, plane, row, first_full, orders)
    return (second_out, volume_grad, first_grad, second_grad)


def solution(mesh):
    return jax.shard_map(
        local,
        mesh=mesh,
        in_specs=(
            P(None, SPACE, CHAN, None, None),
            P(None, None, None, None, CHAN),
            P(None, None, None, None, CHAN),
            P(None, SPACE, None, None, CHAN),
        ),
        out_specs=(
            P(None, SPACE, None, None, CHAN),
            P(None, SPACE, CHAN, None, None),
            P(None, None, None, None, CHAN),
            P(None, None, None, None, CHAN),
        ),
        check_vma=False,
    )
```

```python
import functools

import jax
import jax.numpy as jnp
from jax import lax
from jax.experimental import pallas as pl
from jax.experimental.pallas import tpu as pltpu
from jax.sharding import PartitionSpec as P


SPACE, CHAN = ("space", "chan")
BF16 = jnp.bfloat16
F32 = jnp.float32
LANES = 128
PAD = 8
NT = (((1,), (1,)), ((), ()))
NN = (((1,), (0,)), ((), ()))
REACH = (((1, 0),), ((0, 1), (2, 0)))


def dot(left, right, dims):
    return lax.dot_general(left, right, dims, preferred_element_type=F32)


def bits(axis):
    return lax.axis_size(axis).bit_length() - 1


def shifted(value, steps):
    pairs = []
    sizes = (lax.axis_size(SPACE), lax.axis_size(CHAN))
    for a in range(sizes[0]):
        for b in range(sizes[1]):
            to = (a + steps[0], b + steps[1])
            if 0 <= to[0] < sizes[0] and 0 <= to[1] < sizes[1]:
                pairs.append((a * sizes[1] + b, to[0] * sizes[1] + to[1]))
    return lax.ppermute(value, (SPACE, CHAN), pairs)


def swapped(value, axis, bit):
    count = lax.axis_size(axis)
    return lax.ppermute(value, axis, [(i, i ^ (1 << bit)) for i in range(count)])


def doubled(value, axis, bit):
    other = swapped(value, axis, bit)
    return jnp.stack([value, other])


def position():
    return jnp.stack([lax.axis_index(SPACE), lax.axis_index(CHAN)]).astype(jnp.int32)


def own_part(shard):
    space = lax.axis_size(SPACE)
    edge, inputs, mine = shard.shape[0], shard.shape[3], shard.shape[4]
    taps = edge**3
    each = -(-taps // space)
    flat = jnp.transpose(shard.reshape(taps, inputs, mine), (0, 2, 1))
    flat = jnp.pad(flat, ((0, each * space - taps), (0, 0), (0, 0)))
    return lax.dynamic_slice_in_dim(flat, lax.axis_index(SPACE) * each, each, 0)


def far_bits():
    return list(reversed(range(1, bits(CHAN))))


def high_bits():
    return list(reversed(range(1, bits(SPACE))))


def far_swapped(value, mask):
    count = lax.axis_size(CHAN)
    return lax.ppermute(value, CHAN, [(i, i ^ (mask << 1)) for i in range(count)])


def far_gather(part):
    others = [far_swapped(part, m) for m in range(1, lax.axis_size(CHAN) // 2)]
    return jnp.stack([part, *others])


def near_gather(part):
    each, mine, inputs = part.shape[-3:]
    for bit in high_bits():
        part = doubled(part, SPACE, bit)
    part = doubled(part, SPACE, 0)
    return part.reshape(lax.axis_size(SPACE), lax.axis_size(CHAN), each, mine, inputs)


def mixed_gather(part):
    each, mine, inputs = part.shape[-3:]
    highs = len(high_bits())
    cut = (each + 1) // 2
    one, two = part[..., :cut, :, :], part[..., cut:, :, :]
    one = doubled(one, CHAN, 0)
    for bit in high_bits():
        two = doubled(two, SPACE, bit)
    for bit in high_bits():
        one = doubled(one, SPACE, bit)
    two = doubled(two, CHAN, 0)
    whole = jnp.concatenate([one, jnp.moveaxis(two, 0, highs)], axis=-3)
    whole = doubled(whole, SPACE, 0)
    return whole.reshape(lax.axis_size(SPACE), lax.axis_size(CHAN), each, mine, inputs)


def relative(index, mine, order):
    apart = index ^ mine
    place = 0
    for bit in order:
        place = place * 2 + ((apart >> bit) & 1)
    return place


def filter_tap(ref, here, tap, orders):
    each = ref.shape[2]
    owner = relative(tap // each, here[0], orders[0])
    rows = [
        ref[owner, relative(chan, here[1], orders[1]), tap % each]
        for chan in range(ref.shape[1])
    ]
    return jnp.concatenate(rows, axis=0)


def scratch_avals(scratch):
    return [jax.ShapeDtypeStruct(ref.inner_aval.shape, ref.inner_aval.dtype) for ref in scratch]


def call(kernel, outs, args, scratch=(), grid=None, in_specs=None, out_specs=None, flops=0):
    moved = sum(a.size * a.dtype.itemsize for a in args)
    moved += sum(o.size * o.dtype.itemsize for o in outs)
    used = sum(v.size * v.dtype.itemsize for v in scratch_avals(scratch))
    grant = min(56 * 2**20, moved + used + 6 * 2**20)
    whole = pl.BlockSpec(memory_space=pltpu.VMEM)
    smem = pl.BlockSpec(memory_space=pltpu.SMEM)
    specs = in_specs or [smem if a.dtype == jnp.int32 else whole for a in args]
    return pl.pallas_call(
        kernel,
        out_shape=outs,
        grid=grid or (),
        in_specs=specs,
        out_specs=out_specs or [whole] * len(outs),
        scratch_shapes=scratch,
        cost_estimate=pl.CostEstimate(flops=flops, bytes_accessed=moved, transcendentals=0),
        compiler_params=pltpu.CompilerParams(vmem_limit_bytes=grant),
    )(*args)


def parted_tile(tile, wide, base, store):
    depth, lanes = tile.shape
    for part in range(lanes // LANES):
        rows = wide.at[part]
        rows[pl.ds(base, PAD), :] = jnp.zeros((PAD, LANES), F32)
        rows[pl.ds(base + PAD, depth), :] = tile[:, part * LANES : (part + 1) * LANES].astype(F32)
        for k in range(3):
            piece = rows[pl.ds(base + PAD - 1 + k, depth // 2, stride=2), :]
            store(k, part, piece.astype(BF16))


def part_block(pick, out, n, shape, wide):
    wide_a, wide_b, depth = shape
    for a in range(wide_a):
        for b in range(wide_b):
            slot = ((a * wide_b + b) % 8) * (PAD + depth)

            def store(k, part, piece):
                out[k, n, a, b, :, part * LANES : (part + 1) * LANES] = piece

            parted_tile(pick(a, b), wide, slot, store)


def part_scratch(depth, lanes):
    return pltpu.VMEM((lanes // LANES, 8 * (PAD + depth), LANES), F32)


def parted_volume(own, plane):
    vols, side_a, side_b, depth, lanes = own.shape
    out = jax.ShapeDtypeStruct((3, vols, side_a + 1, side_b, depth // 2, lanes), BF16)

    def kernel(own, plane, out, wide):
        def pick(a, b):
            return plane[0, 0, b] if a == 0 else own[0, a - 1, b]

        part_block(pick, out, 0, (side_a + 1, side_b, depth), wide)

    def block(shape):
        return pl.BlockSpec((1,) + shape[1:], lambda n: (n, 0, 0, 0, 0))

    return call(
        kernel,
        [out],
        (own, plane),
        [part_scratch(depth, lanes)],
        (vols,),
        [block(own.shape), block(plane.shape)],
        [pl.BlockSpec((3, 1) + out.shape[2:], lambda n: (0, n, 0, 0, 0, 0))],
    )[0]


def window(refs, i, j, sides):
    vols, side_a, cells_b = sides
    rows = []
    for n in range(vols):
        for a in range(side_a):
            for b in cells_b:
                y = 2 * b + j
                ref = refs[0]
                if len(refs) == 2:
                    ref, y = (refs[1], 0) if y == 0 else (refs[0], y - 1)
                assert 0 <= y < ref.shape[3]
                rows.append(jnp.concatenate([ref[k, n, 2 * a + i, y] for k in range(3)], axis=1))
    return jnp.concatenate(rows, axis=0)


def forward_total(orders, sides, refs, here, filters, acc):
    acc[...] = jnp.zeros_like(acc)

    def step(i, carry):
        for j in range(3):
            right = jnp.concatenate(
                [filter_tap(filters, here, i * 9 + j * 3 + k, orders) for k in range(3)], axis=1
            )
            acc[...] += dot(window(refs, i, j, sides), right, NT)
        return carry

    lax.fori_loop(0, 3, step, 0)
    return acc[...]


def leaky(total):
    return jnp.where(total > 0, total, 0.3 * total)


def forward(here, parts, filters, orders, cells_b, kind):
    main = parts[0]
    _, vols, wide_a, _, depth, inputs = main.shape
    sides = (vols, (wide_a - 1) // 2, cells_b)
    count = filters.shape[1] * filters.shape[3]
    cells = vols * sides[1] * len(cells_b) * depth
    outs = [jax.ShapeDtypeStruct((vols, sides[1], len(cells_b), depth, count), BF16)]
    scratch = [pltpu.VMEM((cells, count), F32)]
    if kind == "u":
        outs = [jax.ShapeDtypeStruct((count, cells), BF16)]
    if kind == "h":
        outs.append(jax.ShapeDtypeStruct((vols, 1, 1, depth, count), BF16))
    if kind == "l":
        high_b = parts[2].shape[2]
        outs.append(jax.ShapeDtypeStruct((vols, 1, 1 + high_b, depth, count), BF16))
        outs.append(jax.ShapeDtypeStruct(main.shape[:3] + (1,) + main.shape[4:], BF16))
        scratch.append(part_scratch(2 * depth, inputs))

    def kernel(here, filters, main, *rest):
        if kind == "l":
            row, above, out, plane, row_parts, acc, wide = rest

            def split(n, carry):
                part_block(lambda a, b: row[n, a, 0], row_parts, n, (wide_a, 1, 2 * depth), wide)
                return carry

            lax.fori_loop(0, vols, split, 0)
            refs = (main, row_parts)
        else:
            out, acc = rest[0], rest[-1]
            refs = (main, None) if kind == "h" else (main,)
        total = forward_total(orders, sides, refs, here, filters, acc)
        if kind != "u":
            total = leaky(total)
        if kind == "u":
            out[...] = jnp.transpose(total, (1, 0)).astype(BF16)
            return
        value = total.astype(BF16).reshape(out.shape)
        out[...] = value
        if kind == "h":
            rest[1][...] = value[:, -1:, -1:]
        if kind == "l":
            plane[:, :, :1] = value[:, -1:]
            plane[:, :, 1:] = above[:, above.shape[1] - 1 :]

    return call(
        kernel,
        outs,
        (here, filters, *parts),
        scratch,
        flops=2 * cells * 27 * inputs * count,
    )


def grads_body(orders, sides, here, refs, keep, send, turned):
    count = turned.shape[0]
    inputs = refs[0].shape[5]
    pieces = inputs // LANES
    chans = 2 ** len(orders[1])
    mine = count // chans
    each = keep.shape[2] // pieces
    half = keep.shape[0]

    def put(ref, place, tap, part):
        for chan in range(chans):
            to = relative(chan, here[1], orders[1])
            for piece in range(pieces):
                lanes = slice(piece * LANES, (piece + 1) * LANES)
                ref[place, to, (tap % each) * pieces + piece] = part[chan * mine : (chan + 1) * mine, lanes]

    def step(i, carry):
        for j in range(3):
            part = dot(turned[...], window(refs, i, j, sides), NN).astype(BF16)
            for k in range(3):
                tap = i * 9 + j * 3 + k
                place = relative(tap // each, here[0], orders[0])
                piece = part[:, k * inputs : (k + 1) * inputs]

                @pl.when(place < half)
                def _():
                    put(keep, place, tap, piece)

                @pl.when(place >= half)
                def _():
                    put(send, place - half, tap, piece)

        return carry

    lax.fori_loop(0, 3, step, 0)
    blank = jnp.zeros((count, inputs), BF16)
    for tap in range(27, each * 2 * half):
        place = relative(tap // each, here[0], orders[0])

        @pl.when(place < half)
        def _():
            put(keep, place, tap, blank)

        @pl.when(place >= half)
        def _():
            put(send, place - half, tap, blank)


def grads_out(count, inputs, orders):
    space, chans = 2 ** len(orders[0]), 2 ** len(orders[1])
    each = -(-27 // space) * (inputs // LANES)
    return jax.ShapeDtypeStruct((space // 2, chans, each, count // chans, LANES), BF16)


def first_grads(here, refs, grads, orders):
    inputs = refs[0].shape[5]
    vols, side_a, side_b, depth, count = grads.shape
    sides = (vols, side_a, range(side_b))
    cells = vols * side_a * side_b * depth
    out = grads_out(count, inputs, orders)

    def kernel(here, grads, main, row, keep, send, turned):
        flat = grads[...].reshape(cells, count).astype(F32)
        turned[...] = jnp.transpose(flat, (1, 0)).astype(BF16)
        grads_body(orders, sides, here, (main, row), keep, send, turned)

    return call(
        kernel,
        [out, out],
        (here, grads, *refs),
        [pltpu.VMEM((count, cells), BF16)],
        flops=2 * cells * 27 * inputs * count,
    )


def second_grads(here, blocks, grads, orders):
    low, high = blocks[:2]
    side_x, deep, inputs = low.shape[1], low.shape[3], low.shape[4]
    wide_b = low.shape[2] + high.shape[2] + 1
    vols, side_a, side_b, depth = low.shape[0], side_x // 2, wide_b // 2, deep // 2
    chans, mine, cells = grads.shape
    count = chans * mine
    sides = (vols, side_a, range(side_b))
    out = grads_out(count, inputs, orders)
    parts = jax.ShapeDtypeStruct((3, vols, side_x + 1, wide_b, depth, inputs), BF16)

    def kernel(here, grads, low, high, plane, row, corner, keep, send, parts, turned, wide):
        def split(n, carry):
            def pick(a, b):
                if b == 0:
                    return corner[n, 0, 0] if a == 0 else row[n, a - 1, 0]
                if a == 0:
                    return plane[n, 0, b - 1]
                return low[n, a - 1, 0] if b == 1 else high[n, a - 1, b - 2]

            part_block(pick, parts, n, (side_x + 1, wide_b, deep), wide)
            return carry

        lax.fori_loop(0, vols, split, 0)
        for chan in range(chans):
            turned[chan * mine : (chan + 1) * mine] = grads[chan ^ here[1]]
        grads_body(orders, sides, here, (parts,), keep, send, turned)

    return call(
        kernel,
        [out, out, parts],
        (here, grads, *blocks),
        [pltpu.VMEM((count, cells), BF16), part_scratch(deep, inputs)],
        flops=2 * cells * 27 * inputs * count,
    )


def core_sum(keep, send):
    tail = keep.shape[2:]
    other = swapped(send, SPACE, 0)
    total = keep.astype(F32) + other.astype(F32)
    highs = bits(SPACE) - 1
    return total.reshape((2,) * highs + (2, -1) + tail)


def half_sum(value, axis, bit, dim):
    keep = lax.index_in_dim(value, 0, dim, keepdims=False)
    send = lax.index_in_dim(value, 1, dim, keepdims=False)
    other = swapped(send.astype(BF16), axis, bit)
    return keep.astype(F32) + other.astype(F32)


def plain_sum(total):
    total = half_sum(total, CHAN, 0, bits(SPACE) - 1)
    for bit in range(1, bits(SPACE)):
        total = half_sum(total, SPACE, bit, 0)
    return total


def far_sum(total):
    part = total[0].astype(F32)
    for m in range(1, lax.axis_size(CHAN) // 2):
        part = part + far_swapped(total[m].astype(BF16), m).astype(F32)
    return part.astype(BF16)


def mixed_sum(total):
    highs = list(range(1, bits(SPACE)))
    cut = (total.shape[-3] + 1) // 2
    one, two = total[..., :cut, :, :], total[..., cut:, :, :]
    two = half_sum(two, CHAN, 0, len(highs))
    for bit in highs:
        one = half_sum(one, SPACE, bit, 0)
    one = half_sum(one, CHAN, 0, 0)
    for bit in highs:
        two = half_sum(two, SPACE, bit, 0)
    return jnp.concatenate([one, two], axis=-3)


def finish_sum(part):
    space = lax.axis_size(SPACE)
    rows, mine = part.shape[:2]
    taps = -(-27 // space)
    pieces = rows // taps
    shape = part.shape
    for bit in high_bits():
        part = doubled(part, SPACE, bit)
    part = doubled(part, SPACE, 0).reshape((space,) + shape)
    apart = [jnp.int32(s) ^ lax.axis_index(SPACE) for s in range(space)]
    ordered = [lax.dynamic_index_in_dim(part, space_order(a), 0, keepdims=False) for a in apart]
    full = jnp.concatenate(ordered, axis=0)
    full = full.reshape(space * taps, pieces, mine, LANES)[:27].astype(F32)
    return jnp.transpose(full, (0, 1, 3, 2)).reshape(3, 3, 3, pieces * LANES, mine)


def space_order(apart):
    place = 0
    for bit in range(bits(SPACE)):
        place = place * 2 + ((apart >> bit) & 1)
    return place


def stepped_tile(tile, wide, base, store):
    depth, lanes = tile.shape
    for part in range(lanes // LANES):
        rows = wide.at[part]
        rows[pl.ds(base + depth, PAD), :] = jnp.zeros((PAD, LANES), F32)
        rows[pl.ds(base, depth), :] = tile[:, part * LANES : (part + 1) * LANES].astype(F32)
        store(part, rows[pl.ds(base + 1, depth), :].astype(BF16))


def back_kernel(
    orders, here, near, beyond, filters, low, high, out, plane, row, corner, wide, cells, moved, spread
):
    vols, wide_a, wide_b, depth, count = cells.shape
    side_a, side_b = wide_a - 1, wide_b - 1
    inputs = filters.shape[4]
    chans = near.shape[1]
    for b in range(2):
        owner = (here[1] + b) & (chans - 1)
        for ref in (near, beyond):
            rows = jnp.concatenate([ref[b, chan ^ owner] for chan in range(chans)], axis=0)
            flat = jnp.transpose(rows.astype(F32), (1, 0)).astype(BF16)
            for n in range(vols):
                for a in range(side_a if ref is near else 1):
                    begin = (n * side_a + a) * depth
                    cells[n, a if ref is near else side_a, b] = flat[begin : begin + depth]
    for n in range(vols):
        for a in range(wide_a):
            for b in range(wide_b):
                slot = ((n * wide_a + a) * wide_b + b) % 8 * (PAD + depth)

                def store(part, piece):
                    moved[n, a, b, :, part * LANES : (part + 1) * LANES] = piece

                stepped_tile(cells[n, a, b], wide, slot, store)

    def lefts(ref, da, db):
        return ref[:, da : da + side_a, db : db + side_b].reshape(-1, count)

    for sa in range(2):
        for sb in range(2):
            even = odd = None
            for i, da in REACH[sa]:
                for j, db in REACH[sb]:
                    tap = (i * 3 + j) * 3
                    here_cells = lefts(cells, da, db)
                    first = dot(here_cells, filter_tap(filters, here, tap + 1, orders), NN)
                    second = dot(here_cells, filter_tap(filters, here, tap + 2, orders), NN)
                    second += dot(lefts(moved, da, db), filter_tap(filters, here, tap, orders), NN)
                    even = first if even is None else even + first
                    odd = second if odd is None else odd + second
            for parity, value in enumerate((even, odd)):
                value = value.reshape(vols, side_a, side_b, depth, inputs)
                for n in range(vols):
                    for a in range(side_a):
                        for b in range(side_b):
                            for part in range(inputs // LANES):
                                spread[
                                    part, n, 2 * a + sa, 2 * b + sb, pl.ds(parity, depth, stride=2), :
                                ] = value[n, a, b, :, part * LANES : (part + 1) * LANES]
    for part in range(inputs // LANES):
        lanes = slice(part * LANES, (part + 1) * LANES)
        act = jnp.concatenate([low[:, :, :, :, lanes], high[:, :, :, :, lanes]], axis=2)
        act = act.astype(F32)
        value = (spread[part] * jnp.where(act > 0, 1.0, 0.3)).astype(BF16)
        out[:, :, :, :, lanes] = value
        plane[:, :, :, :, lanes] = value[:, :1]
        row[:, :, :, :, lanes] = value[:, :, :1]
        corner[:, :, :, :, lanes] = value[:, :1, :1]


def hidden_back(here, near, beyond, filters, low, high, orders):
    inputs = low.shape[-1]
    shape = low.shape[:2] + (low.shape[2] + high.shape[2],) + low.shape[3:]
    vols, depth = shape[0], shape[3] // 2
    count = near.shape[1] * near.shape[2]
    ext = (vols, shape[1] // 2 + 1, shape[2] // 2 + 1, depth, count)
    outs = [
        jax.ShapeDtypeStruct(shape, BF16),
        jax.ShapeDtypeStruct((vols, 1) + shape[2:], BF16),
        jax.ShapeDtypeStruct(shape[:2] + (1,) + shape[3:], BF16),
        jax.ShapeDtypeStruct((vols, 1, 1) + shape[3:], BF16),
    ]
    return call(
        functools.partial(back_kernel, orders),
        outs,
        (here, near, beyond, filters, low, high),
        [
            pltpu.VMEM((count // LANES, 8 * (PAD + depth), LANES), F32),
            pltpu.VMEM(ext, BF16),
            pltpu.VMEM(ext, BF16),
            pltpu.VMEM((inputs // LANES,) + shape[:4] + (LANES,), F32),
        ],
        flops=2 * vols * (ext[1] - 1) * (ext[2] - 1) * depth * 27 * inputs * count,
    )


def volume_kernel(orders, here, cells, plane, row, filters, out, wide, ext, moved, spread):
    _, side_a, side_b, depth, count = cells.shape
    inputs = filters.shape[4]
    for a in range(side_a + 1):
        for b in range(side_b + 1):
            if b == side_b:
                tile = row[0, a, 0]
            elif a == side_a:
                tile = plane[0, 0, b]
            else:
                tile = cells[0, a, b]
            ext[a, b] = tile
            slot = ((a * (side_b + 1) + b) % 8) * (PAD + depth)

            def store(part, piece):
                moved[a, b, :, part * LANES : (part + 1) * LANES] = piece

            stepped_tile(tile, wide, slot, store)

    def lefts(ref, da, db):
        return ref[da : da + side_a, db : db + side_b].reshape(-1, count)

    for sa in range(2):
        for sb in range(2):
            both = late = None
            for i, da in REACH[sa]:
                for j, db in REACH[sb]:
                    tap = (i * 3 + j) * 3
                    pair = jnp.concatenate(
                        [filter_tap(filters, here, tap + k, orders) for k in (1, 2)], axis=1
                    )
                    first = dot(lefts(ext, da, db), pair, NN)
                    second = dot(lefts(moved, da, db), filter_tap(filters, here, tap, orders), NN)
                    both = first if both is None else both + first
                    late = second if late is None else late + second
            halves = (both[:, :inputs], both[:, inputs:] + late)
            for parity, value in enumerate(halves):
                value = value.reshape(side_a, side_b, depth, inputs)
                for a in range(side_a):
                    for b in range(side_b):
                        spread[2 * a + sa, 2 * b + sb, pl.ds(parity, depth, stride=2), :] = value[a, b]
    out[0] = spread[...].astype(BF16)


def volume_grads(here, cells, plane, row, filters, orders):
    vols, side_a, side_b, depth, count = cells.shape
    inputs = filters.shape[4]
    out = jax.ShapeDtypeStruct((vols, 2 * side_a, 2 * side_b, 2 * depth, inputs), BF16)

    def block(shape):
        return pl.BlockSpec((1,) + shape[1:], lambda n: (n, 0, 0, 0, 0))

    return call(
        functools.partial(volume_kernel, orders),
        [out],
        (here, cells, plane, row, filters),
        [
            pltpu.VMEM((count // LANES, 8 * (PAD + depth), LANES), F32),
            pltpu.VMEM((side_a + 1, side_b + 1, depth, count), BF16),
            pltpu.VMEM((side_a + 1, side_b + 1, depth, count), BF16),
            pltpu.VMEM((2 * side_a, 2 * side_b, 2 * depth, inputs), F32),
        ],
        (vols,),
        [
            pl.BlockSpec(memory_space=pltpu.SMEM),
            block(cells.shape),
            block(plane.shape),
            block(row.shape),
            pl.BlockSpec(memory_space=pltpu.VMEM),
        ],
        [block(out.shape)],
        flops=2 * vols * side_a * side_b * depth * 27 * inputs * count,
    )[0]


class CellExchange:
    def __init__(self, cotangent):
        vols, side_a, side_b, side_c, mine = cotangent.shape
        self.count = bits(CHAN)
        assert side_b == 2**self.count
        flat = jnp.transpose(cotangent, (2, 4, 0, 1, 3))
        self.value = flat.reshape((2,) * self.count + (mine, vols * side_a * side_c))
        self.open = list(reversed(range(self.count)))

    def stage(self, bit):
        dim = self.open.index(bit)
        mine = (lax.axis_index(CHAN) >> bit) & 1
        keep = lax.dynamic_index_in_dim(self.value, mine, dim, keepdims=False)
        send = lax.dynamic_index_in_dim(self.value, 1 - mine, dim, keepdims=False)
        other = swapped(send, CHAN, bit)
        self.value = jnp.stack([keep, other], axis=self.count - 1)
        self.open.remove(bit)

    def finish(self):
        own = self.value.reshape((2**self.count,) + self.value.shape[self.count :])
        near = jnp.stack([own, shifted(own, (0, -1))])
        return own, near, shifted(near, (-1, 0))


def local(volume, w_first, w_second, cotangent):
    here = position()
    orders = (list(range(bits(SPACE))), [0] + far_bits())
    side_b = volume.shape[2] // 2

    plane = shifted(volume[:, -1:], (1, 0))
    part = far_gather(own_part(w_first))
    first_full = near_gather(doubled(part, CHAN, 0))
    row = jnp.concatenate([plane, volume], axis=1)[:, :, -1:]
    row = shifted(row, (0, 1))
    part = far_gather(own_part(w_second))
    second_full = mixed_gather(part)
    cells = CellExchange(cotangent)
    for bit in far_bits() + [0]:
        cells.stage(bit)
    own_cells, near_cells, beyond_cells = cells.finish()

    vol_main = parted_volume(volume, plane)
    high, corner = forward(here, (vol_main,), first_full, orders, range(1, side_b), "h")
    low, hid_plane, vol_row = forward(here, (vol_main, row, high), first_full, orders, range(1), "l")
    hid_row = shifted(high[:, :, -1:], (0, 1))
    hid_corner = shifted(corner, (1, 1))
    hid_plane = shifted(hid_plane, (1, 0))
    blocks = (low, high, hid_plane, hid_row, hid_corner)
    keep, send, act_parts = second_grads(here, blocks, own_cells, orders)
    second_sum = far_sum(mixed_sum(core_sum(keep, send)))

    pre_back, pre_plane, pre_row, corner = hidden_back(
        here, near_cells, beyond_cells, second_full, low, high, orders
    )
    keep, send = first_grads(here, (vol_main, vol_row), pre_back, orders)
    first_sum = far_sum(plain_sum(core_sum(keep, send)))
    first_grad = finish_sum(first_sum)
    second_grad = finish_sum(second_sum)
    plane = shifted(pre_plane, (-1, 0))
    row = shifted(pre_row, (0, -1))
    corner = shifted(corner, (-1, -1))
    row = jnp.concatenate([row, corner], axis=1)
    out_b = range(act_parts.shape[3] // 2)
    (local_out,) = forward(here, (act_parts,), second_full, orders, out_b, "u")
    second_out = lax.all_to_all(local_out, CHAN, split_axis=0, concat_axis=0, tiled=True)
    vols, side_a, rows, deep, mine = cotangent.shape
    second_out = second_out.reshape(rows, mine, vols, side_a, deep)
    second_out = jnp.transpose(second_out, (2, 3, 0, 4, 1))
    volume_grad = volume_grads(here, pre_back, plane, row, first_full, orders)
    return (second_out, volume_grad, first_grad, second_grad)


def solution(mesh):
    return jax.shard_map(
        local,
        mesh=mesh,
        in_specs=(
            P(None, SPACE, CHAN, None, None),
            P(None, None, None, None, CHAN),
            P(None, None, None, None, CHAN),
            P(None, SPACE, None, None, CHAN),
        ),
        out_specs=(
            P(None, SPACE, None, None, CHAN),
            P(None, SPACE, CHAN, None, None),
            P(None, None, None, None, CHAN),
            P(None, None, None, None, CHAN),
        ),
        check_vma=False,
    )
```

```python
import functools

import jax
import jax.numpy as jnp
from jax import lax
from jax.experimental import pallas as pl
from jax.experimental.pallas import tpu as pltpu
from jax.sharding import PartitionSpec as P


SPACE, CHAN = ("space", "chan")
BF16 = jnp.bfloat16
F32 = jnp.float32
LANES = 128
PAD = 8
NT = (((1,), (1,)), ((), ()))
NN = (((1,), (0,)), ((), ()))
REACH = (((1, 0),), ((0, 1), (2, 0)))


def dot(left, right, dims):
    return lax.dot_general(left, right, dims, preferred_element_type=F32)


def bits(axis):
    return lax.axis_size(axis).bit_length() - 1


def shifted(value, steps):
    pairs = []
    sizes = (lax.axis_size(SPACE), lax.axis_size(CHAN))
    for a in range(sizes[0]):
        for b in range(sizes[1]):
            to = (a + steps[0], b + steps[1])
            if 0 <= to[0] < sizes[0] and 0 <= to[1] < sizes[1]:
                pairs.append((a * sizes[1] + b, to[0] * sizes[1] + to[1]))
    return lax.ppermute(value, (SPACE, CHAN), pairs)


def swapped(value, axis, bit):
    count = lax.axis_size(axis)
    return lax.ppermute(value, axis, [(i, i ^ (1 << bit)) for i in range(count)])


def doubled(value, axis, bit):
    other = swapped(value, axis, bit)
    return jnp.stack([value, other])


def position():
    return jnp.stack([lax.axis_index(SPACE), lax.axis_index(CHAN)]).astype(jnp.int32)


def own_part(shard):
    space = lax.axis_size(SPACE)
    edge, inputs, mine = shard.shape[0], shard.shape[3], shard.shape[4]
    taps = edge**3
    each = -(-taps // space)
    flat = jnp.transpose(shard.reshape(taps, inputs, mine), (0, 2, 1))
    flat = jnp.pad(flat, ((0, each * space - taps), (0, 0), (0, 0)))
    return lax.dynamic_slice_in_dim(flat, lax.axis_index(SPACE) * each, each, 0)


def far_bits():
    return list(reversed(range(1, bits(CHAN))))


def high_bits():
    return list(reversed(range(1, bits(SPACE))))


def far_swapped(value, mask):
    count = lax.axis_size(CHAN)
    return lax.ppermute(value, CHAN, [(i, i ^ (mask << 1)) for i in range(count)])


def far_gather(part):
    others = [far_swapped(part, m) for m in range(1, lax.axis_size(CHAN) // 2)]
    return jnp.stack([part, *others])


def near_gather(part):
    each, mine, inputs = part.shape[-3:]
    for bit in high_bits():
        part = doubled(part, SPACE, bit)
    part = doubled(part, SPACE, 0)
    return part.reshape(lax.axis_size(SPACE), lax.axis_size(CHAN), each, mine, inputs)


def mixed_gather(part):
    each, mine, inputs = part.shape[-3:]
    highs = len(high_bits())
    cut = (each + 1) // 2
    one, two = part[..., :cut, :, :], part[..., cut:, :, :]
    one = doubled(one, CHAN, 0)
    for bit in high_bits():
        two = doubled(two, SPACE, bit)
    for bit in high_bits():
        one = doubled(one, SPACE, bit)
    two = doubled(two, CHAN, 0)
    whole = jnp.concatenate([one, jnp.moveaxis(two, 0, highs)], axis=-3)
    whole = doubled(whole, SPACE, 0)
    return whole.reshape(lax.axis_size(SPACE), lax.axis_size(CHAN), each, mine, inputs)


def relative(index, mine, order):
    apart = index ^ mine
    place = 0
    for bit in order:
        place = place * 2 + ((apart >> bit) & 1)
    return place


def filter_tap(ref, here, tap, orders):
    each = ref.shape[2]
    owner = relative(tap // each, here[0], orders[0])
    rows = [
        ref[owner, relative(chan, here[1], orders[1]), tap % each]
        for chan in range(ref.shape[1])
    ]
    return jnp.concatenate(rows, axis=0)


def scratch_avals(scratch):
    return [jax.ShapeDtypeStruct(ref.inner_aval.shape, ref.inner_aval.dtype) for ref in scratch]


def call(kernel, outs, args, scratch=(), grid=None, in_specs=None, out_specs=None, flops=0):
    moved = sum(a.size * a.dtype.itemsize for a in args)
    moved += sum(o.size * o.dtype.itemsize for o in outs)
    used = sum(v.size * v.dtype.itemsize for v in scratch_avals(scratch))
    grant = min(56 * 2**20, moved + used + 6 * 2**20)
    whole = pl.BlockSpec(memory_space=pltpu.VMEM)
    smem = pl.BlockSpec(memory_space=pltpu.SMEM)
    specs = in_specs or [smem if a.dtype == jnp.int32 else whole for a in args]
    return pl.pallas_call(
        kernel,
        out_shape=outs,
        grid=grid or (),
        in_specs=specs,
        out_specs=out_specs or [whole] * len(outs),
        scratch_shapes=scratch,
        cost_estimate=pl.CostEstimate(flops=flops, bytes_accessed=moved, transcendentals=0),
        compiler_params=pltpu.CompilerParams(vmem_limit_bytes=grant),
    )(*args)


def parted_tile(tile, wide, base, store):
    depth, lanes = tile.shape
    for part in range(lanes // LANES):
        rows = wide.at[part]
        rows[pl.ds(base, PAD), :] = jnp.zeros((PAD, LANES), F32)
        rows[pl.ds(base + PAD, depth), :] = tile[:, part * LANES : (part + 1) * LANES].astype(F32)
        for k in range(3):
            piece = rows[pl.ds(base + PAD - 1 + k, depth // 2, stride=2), :]
            store(k, part, piece.astype(BF16))


def part_block(pick, out, n, shape, wide):
    wide_a, wide_b, depth = shape
    for a in range(wide_a):
        for b in range(wide_b):
            slot = ((a * wide_b + b) % 8) * (PAD + depth)

            def store(k, part, piece):
                out[k, n, a, b, :, part * LANES : (part + 1) * LANES] = piece

            parted_tile(pick(a, b), wide, slot, store)


def part_scratch(depth, lanes):
    return pltpu.VMEM((lanes // LANES, 8 * (PAD + depth), LANES), F32)


def parted_volume(own, plane):
    vols, side_a, side_b, depth, lanes = own.shape
    out = jax.ShapeDtypeStruct((3, vols, side_a + 1, side_b, depth // 2, lanes), BF16)

    def kernel(own, plane, out, wide):
        def pick(a, b):
            return plane[0, 0, b] if a == 0 else own[0, a - 1, b]

        part_block(pick, out, 0, (side_a + 1, side_b, depth), wide)

    def block(shape):
        return pl.BlockSpec((1,) + shape[1:], lambda n: (n, 0, 0, 0, 0))

    return call(
        kernel,
        [out],
        (own, plane),
        [part_scratch(depth, lanes)],
        (vols,),
        [block(own.shape), block(plane.shape)],
        [pl.BlockSpec((3, 1) + out.shape[2:], lambda n: (0, n, 0, 0, 0, 0))],
    )[0]


def window(refs, i, j, sides):
    vols, side_a, cells_b = sides
    rows = []
    for n in range(vols):
        for a in range(side_a):
            for b in cells_b:
                y = 2 * b + j
                ref = refs[0]
                if len(refs) == 2:
                    ref, y = (refs[1], 0) if y == 0 else (refs[0], y - 1)
                assert 0 <= y < ref.shape[3]
                rows.append(jnp.concatenate([ref[k, n, 2 * a + i, y] for k in range(3)], axis=1))
    return jnp.concatenate(rows, axis=0)


def forward_total(orders, sides, refs, here, filters, acc):
    acc[...] = jnp.zeros_like(acc)

    def step(i, carry):
        for j in range(3):
            right = jnp.concatenate(
                [filter_tap(filters, here, i * 9 + j * 3 + k, orders) for k in range(3)], axis=1
            )
            acc[...] += dot(window(refs, i, j, sides), right, NT)
        return carry

    lax.fori_loop(0, 3, step, 0)
    return acc[...]


def leaky(total):
    return jnp.where(total > 0, total, 0.3 * total)


def forward(here, parts, filters, orders, cells_b, kind):
    main = parts[0]
    _, vols, wide_a, _, depth, inputs = main.shape
    sides = (vols, (wide_a - 1) // 2, cells_b)
    count = filters.shape[1] * filters.shape[3]
    cells = vols * sides[1] * len(cells_b) * depth
    outs = [jax.ShapeDtypeStruct((vols, sides[1], len(cells_b), depth, count), BF16)]
    scratch = [pltpu.VMEM((cells, count), F32)]
    if kind == "u":
        outs = [jax.ShapeDtypeStruct((count, cells), BF16)]
    if kind == "h":
        outs.append(jax.ShapeDtypeStruct((vols, 1, 1, depth, count), BF16))
    if kind == "l":
        high_b = parts[2].shape[2]
        outs.append(jax.ShapeDtypeStruct((vols, 1, 1 + high_b, depth, count), BF16))
        outs.append(jax.ShapeDtypeStruct(main.shape[:3] + (1,) + main.shape[4:], BF16))
        scratch.append(part_scratch(2 * depth, inputs))

    def kernel(here, filters, main, *rest):
        if kind == "l":
            row, above, out, plane, row_parts, acc, wide = rest

            def split(n, carry):
                part_block(lambda a, b: row[n, a, 0], row_parts, n, (wide_a, 1, 2 * depth), wide)
                return carry

            lax.fori_loop(0, vols, split, 0)
            refs = (main, row_parts)
        else:
            out, acc = rest[0], rest[-1]
            refs = (main, None) if kind == "h" else (main,)
        total = forward_total(orders, sides, refs, here, filters, acc)
        if kind != "u":
            total = leaky(total)
        if kind == "u":
            out[...] = jnp.transpose(total, (1, 0)).astype(BF16)
            return
        value = total.astype(BF16).reshape(out.shape)
        out[...] = value
        if kind == "h":
            rest[1][...] = value[:, -1:, -1:]
        if kind == "l":
            plane[:, :, :1] = value[:, -1:]
            plane[:, :, 1:] = above[:, above.shape[1] - 1 :]

    return call(
        kernel,
        outs,
        (here, filters, *parts),
        scratch,
        flops=2 * cells * 27 * inputs * count,
    )


def grads_body(orders, sides, here, refs, keep, send, turned):
    count = turned.shape[0]
    inputs = refs[0].shape[5]
    pieces = inputs // LANES
    chans = 2 ** len(orders[1])
    mine = count // chans
    each = keep.shape[2] // pieces
    half = keep.shape[0]

    def put(ref, place, tap, part):
        for chan in range(chans):
            to = relative(chan, here[1], orders[1])
            for piece in range(pieces):
                lanes = slice(piece * LANES, (piece + 1) * LANES)
                ref[place, to, (tap % each) * pieces + piece] = part[chan * mine : (chan + 1) * mine, lanes]

    def step(i, carry):
        for j in range(3):
            part = dot(turned[...], window(refs, i, j, sides), NN).astype(BF16)
            for k in range(3):
                tap = i * 9 + j * 3 + k
                place = relative(tap // each, here[0], orders[0])
                piece = part[:, k * inputs : (k + 1) * inputs]

                @pl.when(place < half)
                def _():
                    put(keep, place, tap, piece)

                @pl.when(place >= half)
                def _():
                    put(send, place - half, tap, piece)

        return carry

    lax.fori_loop(0, 3, step, 0)
    blank = jnp.zeros((count, inputs), BF16)
    for tap in range(27, each * 2 * half):
        place = relative(tap // each, here[0], orders[0])

        @pl.when(place < half)
        def _():
            put(keep, place, tap, blank)

        @pl.when(place >= half)
        def _():
            put(send, place - half, tap, blank)


def grads_out(count, inputs, orders):
    space, chans = 2 ** len(orders[0]), 2 ** len(orders[1])
    each = -(-27 // space) * (inputs // LANES)
    return jax.ShapeDtypeStruct((space // 2, chans, each, count // chans, LANES), BF16)


def first_grads(here, refs, grads, orders):
    inputs = refs[0].shape[5]
    vols, side_a, side_b, depth, count = grads.shape
    sides = (vols, side_a, range(side_b))
    cells = vols * side_a * side_b * depth
    out = grads_out(count, inputs, orders)

    def kernel(here, grads, main, row, keep, send, turned):
        flat = grads[...].reshape(cells, count).astype(F32)
        turned[...] = jnp.transpose(flat, (1, 0)).astype(BF16)
        grads_body(orders, sides, here, (main, row), keep, send, turned)

    return call(
        kernel,
        [out, out],
        (here, grads, *refs),
        [pltpu.VMEM((count, cells), BF16)],
        flops=2 * cells * 27 * inputs * count,
    )


def second_grads(here, blocks, grads, orders):
    low, high = blocks[:2]
    side_x, deep, inputs = low.shape[1], low.shape[3], low.shape[4]
    wide_b = low.shape[2] + high.shape[2] + 1
    vols, side_a, side_b, depth = low.shape[0], side_x // 2, wide_b // 2, deep // 2
    chans, mine, cells = grads.shape
    count = chans * mine
    sides = (vols, side_a, range(side_b))
    out = grads_out(count, inputs, orders)
    parts = jax.ShapeDtypeStruct((3, vols, side_x + 1, wide_b, depth, inputs), BF16)

    def kernel(here, grads, low, high, plane, row, corner, keep, send, parts, turned, wide):
        def split(n, carry):
            def pick(a, b):
                if b == 0:
                    return corner[n, 0, 0] if a == 0 else row[n, a - 1, 0]
                if a == 0:
                    return plane[n, 0, b - 1]
                return low[n, a - 1, 0] if b == 1 else high[n, a - 1, b - 2]

            part_block(pick, parts, n, (side_x + 1, wide_b, deep), wide)
            return carry

        lax.fori_loop(0, vols, split, 0)
        for chan in range(chans):
            turned[chan * mine : (chan + 1) * mine] = grads[relative(chan, here[1], orders[1])]
        grads_body(orders, sides, here, (parts,), keep, send, turned)

    return call(
        kernel,
        [out, out, parts],
        (here, grads, *blocks),
        [pltpu.VMEM((count, cells), BF16), part_scratch(deep, inputs)],
        flops=2 * cells * 27 * inputs * count,
    )


def core_sum(keep, send):
    tail = keep.shape[2:]
    other = swapped(send, SPACE, 0)
    total = keep.astype(F32) + other.astype(F32)
    highs = bits(SPACE) - 1
    return total.reshape((2,) * highs + (2, -1) + tail)


def half_sum(value, axis, bit, dim):
    keep = lax.index_in_dim(value, 0, dim, keepdims=False)
    send = lax.index_in_dim(value, 1, dim, keepdims=False)
    other = swapped(send.astype(BF16), axis, bit)
    return keep.astype(F32) + other.astype(F32)


def plain_sum(total):
    total = half_sum(total, CHAN, 0, bits(SPACE) - 1)
    for bit in range(1, bits(SPACE)):
        total = half_sum(total, SPACE, bit, 0)
    return total


def far_sum(total):
    part = total[0].astype(F32)
    for m in range(1, lax.axis_size(CHAN) // 2):
        part = part + far_swapped(total[m].astype(BF16), m).astype(F32)
    return part.astype(BF16)


def mixed_sum(total):
    highs = list(range(1, bits(SPACE)))
    cut = (total.shape[-3] + 1) // 2
    one, two = total[..., :cut, :, :], total[..., cut:, :, :]
    two = half_sum(two, CHAN, 0, len(highs))
    for bit in highs:
        one = half_sum(one, SPACE, bit, 0)
    one = half_sum(one, CHAN, 0, 0)
    for bit in highs:
        two = half_sum(two, SPACE, bit, 0)
    return jnp.concatenate([one, two], axis=-3)


def finish_sum(part):
    space = lax.axis_size(SPACE)
    rows, mine = part.shape[:2]
    taps = -(-27 // space)
    pieces = rows // taps
    shape = part.shape
    for bit in high_bits():
        part = doubled(part, SPACE, bit)
    part = doubled(part, SPACE, 0).reshape((space,) + shape)
    apart = [jnp.int32(s) ^ lax.axis_index(SPACE) for s in range(space)]
    ordered = [lax.dynamic_index_in_dim(part, space_order(a), 0, keepdims=False) for a in apart]
    full = jnp.concatenate(ordered, axis=0)
    full = full.reshape(space * taps, pieces, mine, LANES)[:27].astype(F32)
    return jnp.transpose(full, (0, 1, 3, 2)).reshape(3, 3, 3, pieces * LANES, mine)


def space_order(apart):
    place = 0
    for bit in range(bits(SPACE)):
        place = place * 2 + ((apart >> bit) & 1)
    return place


def stepped_tile(tile, wide, base, store):
    depth, lanes = tile.shape
    for part in range(lanes // LANES):
        rows = wide.at[part]
        rows[pl.ds(base + depth, PAD), :] = jnp.zeros((PAD, LANES), F32)
        rows[pl.ds(base, depth), :] = tile[:, part * LANES : (part + 1) * LANES].astype(F32)
        store(part, rows[pl.ds(base + 1, depth), :].astype(BF16))


def back_kernel(
    orders, here, near, beyond, filters, low, high, out, plane, row, corner, wide, cells, moved, spread
):
    vols, wide_a, wide_b, depth, count = cells.shape
    side_a, side_b = wide_a - 1, wide_b - 1
    inputs = filters.shape[4]
    chans = near.shape[1]
    for b in range(2):
        owner = (here[1] + b) & (chans - 1)
        for ref in (near, beyond):
            rows = jnp.concatenate([ref[b, relative(chan, owner, orders[1])] for chan in range(chans)], axis=0)
            flat = jnp.transpose(rows.astype(F32), (1, 0)).astype(BF16)
            for n in range(vols):
                for a in range(side_a if ref is near else 1):
                    begin = (n * side_a + a) * depth
                    cells[n, a if ref is near else side_a, b] = flat[begin : begin + depth]
    for n in range(vols):
        for a in range(wide_a):
            for b in range(wide_b):
                slot = ((n * wide_a + a) * wide_b + b) % 8 * (PAD + depth)

                def store(part, piece):
                    moved[n, a, b, :, part * LANES : (part + 1) * LANES] = piece

                stepped_tile(cells[n, a, b], wide, slot, store)

    def lefts(ref, da, db):
        return ref[:, da : da + side_a, db : db + side_b].reshape(-1, count)

    for sa in range(2):
        for sb in range(2):
            even = odd = None
            for i, da in REACH[sa]:
                for j, db in REACH[sb]:
                    tap = (i * 3 + j) * 3
                    here_cells = lefts(cells, da, db)
                    first = dot(here_cells, filter_tap(filters, here, tap + 1, orders), NN)
                    second = dot(here_cells, filter_tap(filters, here, tap + 2, orders), NN)
                    second += dot(lefts(moved, da, db), filter_tap(filters, here, tap, orders), NN)
                    even = first if even is None else even + first
                    odd = second if odd is None else odd + second
            for parity, value in enumerate((even, odd)):
                value = value.reshape(vols, side_a, side_b, depth, inputs)
                for n in range(vols):
                    for a in range(side_a):
                        for b in range(side_b):
                            for part in range(inputs // LANES):
                                spread[
                                    part, n, 2 * a + sa, 2 * b + sb, pl.ds(parity, depth, stride=2), :
                                ] = value[n, a, b, :, part * LANES : (part + 1) * LANES]
    for part in range(inputs // LANES):
        lanes = slice(part * LANES, (part + 1) * LANES)
        act = jnp.concatenate([low[:, :, :, :, lanes], high[:, :, :, :, lanes]], axis=2)
        act = act.astype(F32)
        value = (spread[part] * jnp.where(act > 0, 1.0, 0.3)).astype(BF16)
        out[:, :, :, :, lanes] = value
        plane[:, :, :, :, lanes] = value[:, :1]
        row[:, :, :, :, lanes] = value[:, :, :1]
        corner[:, :, :, :, lanes] = value[:, :1, :1]


def hidden_back(here, near, beyond, filters, low, high, orders):
    inputs = low.shape[-1]
    shape = low.shape[:2] + (low.shape[2] + high.shape[2],) + low.shape[3:]
    vols, depth = shape[0], shape[3] // 2
    count = near.shape[1] * near.shape[2]
    ext = (vols, shape[1] // 2 + 1, shape[2] // 2 + 1, depth, count)
    outs = [
        jax.ShapeDtypeStruct(shape, BF16),
        jax.ShapeDtypeStruct((vols, 1) + shape[2:], BF16),
        jax.ShapeDtypeStruct(shape[:2] + (1,) + shape[3:], BF16),
        jax.ShapeDtypeStruct((vols, 1, 1) + shape[3:], BF16),
    ]
    return call(
        functools.partial(back_kernel, orders),
        outs,
        (here, near, beyond, filters, low, high),
        [
            pltpu.VMEM((count // LANES, 8 * (PAD + depth), LANES), F32),
            pltpu.VMEM(ext, BF16),
            pltpu.VMEM(ext, BF16),
            pltpu.VMEM((inputs // LANES,) + shape[:4] + (LANES,), F32),
        ],
        flops=2 * vols * (ext[1] - 1) * (ext[2] - 1) * depth * 27 * inputs * count,
    )


def volume_kernel(orders, here, cells, plane, row, filters, out, wide, ext, moved, spread):
    _, side_a, side_b, depth, count = cells.shape
    inputs = filters.shape[4]
    for a in range(side_a + 1):
        for b in range(side_b + 1):
            if b == side_b:
                tile = row[0, a, 0]
            elif a == side_a:
                tile = plane[0, 0, b]
            else:
                tile = cells[0, a, b]
            ext[a, b] = tile
            slot = ((a * (side_b + 1) + b) % 8) * (PAD + depth)

            def store(part, piece):
                moved[a, b, :, part * LANES : (part + 1) * LANES] = piece

            stepped_tile(tile, wide, slot, store)

    def lefts(ref, da, db):
        return ref[da : da + side_a, db : db + side_b].reshape(-1, count)

    for sa in range(2):
        for sb in range(2):
            both = late = None
            for i, da in REACH[sa]:
                for j, db in REACH[sb]:
                    tap = (i * 3 + j) * 3
                    pair = jnp.concatenate(
                        [filter_tap(filters, here, tap + k, orders) for k in (1, 2)], axis=1
                    )
                    first = dot(lefts(ext, da, db), pair, NN)
                    second = dot(lefts(moved, da, db), filter_tap(filters, here, tap, orders), NN)
                    both = first if both is None else both + first
                    late = second if late is None else late + second
            halves = (both[:, :inputs], both[:, inputs:] + late)
            for parity, value in enumerate(halves):
                value = value.reshape(side_a, side_b, depth, inputs)
                for a in range(side_a):
                    for b in range(side_b):
                        spread[2 * a + sa, 2 * b + sb, pl.ds(parity, depth, stride=2), :] = value[a, b]
    out[0] = spread[...].astype(BF16)


def volume_grads(here, cells, plane, row, filters, orders):
    vols, side_a, side_b, depth, count = cells.shape
    inputs = filters.shape[4]
    out = jax.ShapeDtypeStruct((vols, 2 * side_a, 2 * side_b, 2 * depth, inputs), BF16)

    def block(shape):
        return pl.BlockSpec((1,) + shape[1:], lambda n: (n, 0, 0, 0, 0))

    return call(
        functools.partial(volume_kernel, orders),
        [out],
        (here, cells, plane, row, filters),
        [
            pltpu.VMEM((count // LANES, 8 * (PAD + depth), LANES), F32),
            pltpu.VMEM((side_a + 1, side_b + 1, depth, count), BF16),
            pltpu.VMEM((side_a + 1, side_b + 1, depth, count), BF16),
            pltpu.VMEM((2 * side_a, 2 * side_b, 2 * depth, inputs), F32),
        ],
        (vols,),
        [
            pl.BlockSpec(memory_space=pltpu.SMEM),
            block(cells.shape),
            block(plane.shape),
            block(row.shape),
            pl.BlockSpec(memory_space=pltpu.VMEM),
        ],
        [block(out.shape)],
        flops=2 * vols * side_a * side_b * depth * 27 * inputs * count,
    )[0]


class CellExchange:
    def __init__(self, cotangent):
        vols, side_a, side_b, side_c, mine = cotangent.shape
        self.count = bits(CHAN)
        assert side_b == 2**self.count
        flat = jnp.transpose(cotangent, (2, 4, 0, 1, 3))
        self.value = flat.reshape((2,) * self.count + (mine, vols * side_a * side_c))
        self.open = list(reversed(range(self.count)))

    def stage(self, bit):
        dim = self.open.index(bit)
        mine = (lax.axis_index(CHAN) >> bit) & 1
        keep = lax.dynamic_index_in_dim(self.value, mine, dim, keepdims=False)
        send = lax.dynamic_index_in_dim(self.value, 1 - mine, dim, keepdims=False)
        other = swapped(send, CHAN, bit)
        self.value = jnp.stack([keep, other], axis=self.count - 1)
        self.open.remove(bit)

    def finish(self):
        own = self.value.reshape((2**self.count,) + self.value.shape[self.count :])
        near = jnp.stack([own, shifted(own, (0, -1))])
        return own, near, shifted(near, (-1, 0))


def local(volume, w_first, w_second, cotangent):
    here = position()
    orders = (list(range(bits(SPACE))), [0] + far_bits())
    side_b = volume.shape[2] // 2

    plane = shifted(volume[:, -1:], (1, 0))
    part = far_gather(own_part(w_first))
    first_full = near_gather(doubled(part, CHAN, 0))
    row = jnp.concatenate([plane, volume], axis=1)[:, :, -1:]
    row = shifted(row, (0, 1))
    part = far_gather(own_part(w_second))
    second_full = mixed_gather(part)
    cells = CellExchange(cotangent)
    for bit in [0] + far_bits():
        cells.stage(bit)
    own_cells, near_cells, beyond_cells = cells.finish()

    vol_main = parted_volume(volume, plane)
    high, corner = forward(here, (vol_main,), first_full, orders, range(1, side_b), "h")
    low, hid_plane, vol_row = forward(here, (vol_main, row, high), first_full, orders, range(1), "l")
    hid_row = shifted(high[:, :, -1:], (0, 1))
    hid_corner = shifted(corner, (1, 1))
    hid_plane = shifted(hid_plane, (1, 0))
    blocks = (low, high, hid_plane, hid_row, hid_corner)
    keep, send, act_parts = second_grads(here, blocks, own_cells, orders)
    second_sum = far_sum(mixed_sum(core_sum(keep, send)))

    pre_back, pre_plane, pre_row, corner = hidden_back(here, near_cells, beyond_cells, second_full, low, high, orders)
    keep, send = first_grads(here, (vol_main, vol_row), pre_back, orders)
    first_sum = far_sum(plain_sum(core_sum(keep, send)))
    first_grad = finish_sum(first_sum)
    second_grad = finish_sum(second_sum)
    plane = shifted(pre_plane, (-1, 0))
    row = shifted(pre_row, (0, -1))
    corner = shifted(corner, (-1, -1))
    row = jnp.concatenate([row, corner], axis=1)
    out_b = range(act_parts.shape[3] // 2)
    (local_out,) = forward(here, (act_parts,), second_full, orders, out_b, "u")
    second_out = lax.all_to_all(local_out, CHAN, split_axis=0, concat_axis=0, tiled=True)
    vols, side_a, rows, deep, mine = cotangent.shape
    second_out = second_out.reshape(rows, mine, vols, side_a, deep)
    second_out = jnp.transpose(second_out, (2, 3, 0, 4, 1))
    volume_grad = volume_grads(here, pre_back, plane, row, first_full, orders)
    return (second_out, volume_grad, first_grad, second_grad)


def solution(mesh):
    return jax.shard_map(
        local,
        mesh=mesh,
        in_specs=(
            P(None, SPACE, CHAN, None, None),
            P(None, None, None, None, CHAN),
            P(None, None, None, None, CHAN),
            P(None, SPACE, None, None, CHAN),
        ),
        out_specs=(
            P(None, SPACE, None, None, CHAN),
            P(None, SPACE, CHAN, None, None),
            P(None, None, None, None, CHAN),
            P(None, None, None, None, CHAN),
        ),
        check_vma=False,
    )
```
